32 devices in a mesh: dp: 4 (over z), row: 4 (over x, core), col: 2 (over y).
Axes of the slice: x: 2, y: 2, z: 4, core: 2. Of those that a mesh axis runs over, the one named last changes fastest.
Arguments:
- hidden: float32 [4096, 1024], P(('dp', 'row')), may hold values from -6 to 6
- cotangent: float32 [4096, 1024], P(('dp', 'row'), 'col'), may hold values from -6 to 6
- norm_gain: float32 [1024], replicated, may hold values from 0.5 to 1.5
- weight_z: bfloat16 [1024, 2048], P('col', 'row'), may hold values from -0.1875 to 0.1875
- weight_x: bfloat16 [1024, 2048], P('col', 'row'), may hold values from -0.1875 to 0.1875
- weight_dt: bfloat16 [1024, 32], P('col', 'row'), may hold values from -0.1875 to 0.1875
- weight_bc: bfloat16 [1024, 256], P('col'), may hold values from -0.1875 to 0.1875
- conv_weight: float32 [4, 2048], P(None, ('row', 'col')), may hold values from -3 to 3
- conv_bias: float32 [2048], P(('row', 'col')), may hold values from -3 to 3
- bc_conv_weight: float32 [4, 256], replicated, may hold values from -3 to 3
- bc_conv_bias: float32 [256], replicated, may hold values from -3 to 3
- dt_bias: float32 [32], P(('row', 'col')), may hold values from -5 to -1
- decay_log: float32 [32], P(('row', 'col')), may hold values from 0 to 2.77
- skip_gain: float32 [32], P(('row', 'col')), may hold values from 0.5 to 1.5
- gate_gain: float32 [2048], P(('row', 'col')), may hold values from 0.25 to 1.75
- out_weight: bfloat16 [2048, 1024], P('row', 'col'), may hold values from -0.125 to 0.125
Outputs:
- output: float32 [4096, 1024], P(('dp', 'row'), 'col')
- grad_hidden: float32 [4096, 1024], P(('dp', 'row'), 'col')
- grad_norm_gain: float32 [1024], P('col')
- grad_weight_z: float32 [1024, 2048], P('col', 'row')
- grad_weight_x: float32 [1024, 2048], P('col', 'row')
- grad_weight_dt: float32 [1024, 32], P('col', 'row')
- grad_weight_bc: float32 [1024, 256], P('col')
- grad_conv_weight: float32 [4, 2048], P(None, ('row', 'col'))
- grad_conv_bias: float32 [2048], P(('row', 'col'))
- grad_bc_conv_weight: float32 [4, 256], replicated
- grad_bc_conv_bias: float32 [256], replicated
- grad_dt_bias: float32 [32], P(('row', 'col'))
- grad_decay_log: float32 [32], P(('row', 'col'))
- grad_skip_gain: float32 [32], P(('row', 'col'))
- grad_gate_gain: float32 [2048], P(('row', 'col'))
- grad_out_weight: float32 [2048, 1024], P('row', 'col')
The draws below stay inside these ranges and needn't reach their ends.
All inputs are finite; a program needn't handle non-finite values.
Results may differ from the reference program's by a relative error of at most 0.012.
Values may be sent and summed in bfloat16 or wider, within the bound.
A program may use at most 128 MiB of HBM per device.

```python
import jax
import jax.numpy as jnp
from jax import lax

D = 1024
HEADS = 32
STATE = 128
KERNEL = 4
BLOCK = 256
SEQ_LEN = 1024
INNER = 2048
TOKENS = 4096


def block_scale(key, extent, cuts, smallest, high):
    factor_of, own = 1.0, jax.random.fold_in(key, 6)
    for position, parts in cuts:
        steps = jnp.exp(jax.random.uniform(jax.random.fold_in(own, position), (parts,), jnp.float32, smallest / len(cuts), high / len(cuts)))
        factor_of = factor_of * jnp.repeat(steps, extent[position] // parts).reshape([-1 if axis == position else 1 for axis in range(len(extent))])
    return factor_of


def scatter_about(stream_key, dims, scale, reach, split=(), kind=jnp.bfloat16):
    drawn = scale * jax.random.normal(stream_key, dims, jnp.float32)
    if split:
        drawn = drawn * block_scale(stream_key, dims, split, -0.22, 0.18)
    return jnp.clip(drawn, -reach, reach).astype(kind)


def setup_inputs(seed: int = 0) -> dict:
    arg_keys = jax.random.split(jax.random.key(seed), 17)
    return {
        "hidden": scatter_about(arg_keys[0], (TOKENS, D), 1.0, 6.0, ((0, 16),), jnp.float32),
        "cotangent": scatter_about(arg_keys[1], (TOKENS, D), 1.0, 6.0, ((0, 16), (1, 2)), jnp.float32),
        "norm_gain": jnp.clip(1.0 + 0.1 * jax.random.normal(arg_keys[2], (D,), jnp.float32), 0.5, 1.5),
        "weight_z": scatter_about(arg_keys[3], (D, INNER), D ** -0.5, 0.1875, ((0, 2), (1, 4))),
        "weight_x": scatter_about(arg_keys[4], (D, INNER), D ** -0.5, 0.1875, ((0, 2), (1, 4))),
        "weight_dt": scatter_about(arg_keys[5], (D, HEADS), D ** -0.5, 0.1875, ((0, 2), (1, 4))),
        "weight_bc": scatter_about(arg_keys[6], (D, 2 * STATE), D ** -0.5, 0.1875, ((0, 2),)),
        "conv_weight": scatter_about(arg_keys[7], (KERNEL, INNER), KERNEL ** -0.5, 3.0, ((1, 8),), jnp.float32),
        "conv_bias": scatter_about(arg_keys[8], (INNER,), 0.5, 3.0, ((0, 8),), jnp.float32),
        "bc_conv_weight": scatter_about(arg_keys[9], (KERNEL, 2 * STATE), KERNEL ** -0.5, 3.0, (), jnp.float32),
        "bc_conv_bias": scatter_about(arg_keys[10], (2 * STATE,), 0.5, 3.0, (), jnp.float32),
        "dt_bias": jnp.clip(-5.0 + 4.0 * jax.random.uniform(arg_keys[11], (HEADS,), jnp.float32) ** block_scale(arg_keys[11], (HEADS,), ((0, 8),), -0.2, 0.2), -5.0, -1.0),
        "decay_log": jnp.clip(2.77 * jax.random.uniform(arg_keys[12], (HEADS,), jnp.float32) ** block_scale(arg_keys[12], (HEADS,), ((0, 8),), -0.2, 0.2), 0.0, 2.77),
        "skip_gain": jnp.clip(0.5 + 1.0 * jax.random.uniform(arg_keys[13], (HEADS,), jnp.float32) ** block_scale(arg_keys[13], (HEADS,), ((0, 8),), -0.2, 0.2), 0.5, 1.5),
        "gate_gain": jnp.clip(1.0 + 0.15 * jax.random.normal(arg_keys[14], (INNER,), jnp.float32), 0.25, 1.75),
        "out_weight": scatter_about(arg_keys[15], (INNER, D), INNER ** -0.5, 0.125, ((0, 4), (1, 2))),
    }


EPSILON = 1e-05
PRECISE = lax.Precision.HIGHEST

def causal_conv(values, kernel, offset_bias):
    kernel_width = kernel.shape[0]
    length = values.shape[0]
    padded = jnp.pad(values, ((kernel_width - 1, 0), (0, 0)))
    summed = jnp.broadcast_to(offset_bias[None, :], values.shape)
    for offset in range(kernel_width):
        summed = summed + kernel[offset][None, :] * padded[offset:offset + length]
    return summed

def block_scan(inputs, step_sizes, rates, b_values, c_values):
    length, head_count, head_width = inputs.shape
    block_count = length // BLOCK
    state_width = b_values.shape[1]
    blocks = inputs.reshape(block_count, BLOCK, head_count, head_width)
    block_steps = step_sizes.reshape(block_count, BLOCK, head_count)
    log_decay = jnp.cumsum(block_steps * rates[None, None, :], axis=1)
    b_blocks = b_values.reshape(block_count, BLOCK, state_width)
    c_blocks = c_values.reshape(block_count, BLOCK, state_width)
    scores = jnp.einsum('cln,csn->cls', c_blocks, b_blocks, precision=PRECISE)
    causal = jnp.arange(BLOCK)[:, None] >= jnp.arange(BLOCK)[None, :]
    log_gap = log_decay[:, :, None, :] - log_decay[:, None, :, :]
    decays = jnp.exp(jnp.where(causal[None, :, :, None], log_gap, -1e+30))
    mixing = scores[:, :, :, None] * decays * block_steps[:, None, :, :]
    inside = jnp.einsum('clsh,cshp->clhp', mixing, blocks, precision=PRECISE)
    tail_decay = jnp.exp(log_decay[:, -1:, :] - log_decay) * block_steps
    states = jnp.einsum('csn,csh,cshp->chpn', b_blocks, tail_decay, blocks, precision=PRECISE)
    carried = jnp.exp(log_decay[:, -1, :])

    def advance(running, pair_item):
        new_state, factor = pair_item
        return (running * factor[:, None, None] + new_state, running)
    initial = jnp.zeros((head_count, head_width, state_width), jnp.float32)
    _, entering = lax.scan(advance, initial, (states, carried))
    outside = jnp.einsum('cln,chpn,clh->clhp', c_blocks, entering, jnp.exp(log_decay), precision=PRECISE)
    return (inside + outside).reshape(length, head_count, head_width)

def sequence_mixer(z_raw, x_raw, step_raw, bc_raw, conv_weight, conv_bias, bc_conv_weight, bc_conv_bias, dt_bias, decay_log, skip_gain):
    x_conv = jax.nn.silu(causal_conv(x_raw, conv_weight, conv_bias))
    bc_conv = jax.nn.silu(causal_conv(bc_raw, bc_conv_weight, bc_conv_bias))
    state_width = bc_conv.shape[1] // 2
    head_count = step_raw.shape[1]
    length = x_conv.shape[0]
    heads_in = x_conv.reshape(length, head_count, -1)
    step_size = jax.nn.softplus(step_raw + dt_bias[None, :])
    rates = -jnp.exp(decay_log)
    mixed = block_scan(heads_in, step_size, rates, bc_conv[:, :state_width], bc_conv[:, state_width:])
    mixed = mixed + skip_gain[None, :, None] * heads_in
    return mixed.reshape(length, -1) * jax.nn.silu(z_raw)

def reference(hidden, cotangent, norm_gain, weight_z, weight_x, weight_dt, weight_bc, conv_weight, conv_bias, bc_conv_weight, bc_conv_bias, dt_bias, decay_log, skip_gain, gate_gain, out_weight):
    seq_count = hidden.shape[0] // SEQ_LEN
    model_width = hidden.shape[1]
    hidden_seqs = hidden.reshape(seq_count, SEQ_LEN, model_width)
    cot_seqs = cotangent.reshape(seq_count, SEQ_LEN, model_width)
    bc_wide = weight_bc.astype(jnp.float32)

    def one_sequence(totals, pair_item):
        seq_rows, seq_cot = pair_item
        inv_rms = lax.rsqrt(lax.optimization_barrier(jnp.mean(seq_rows * seq_rows, axis=1, keepdims=True)) + EPSILON)
        normed = seq_rows * inv_rms
        scaled = (normed * norm_gain[None, :]).astype(jnp.bfloat16)
        z_raw = jnp.dot(scaled, weight_z, preferred_element_type=jnp.float32)
        x_raw = jnp.dot(scaled, weight_x, preferred_element_type=jnp.float32)
        step_raw = jnp.dot(scaled, weight_dt, preferred_element_type=jnp.float32)
        bc_raw = jnp.dot(scaled, weight_bc, preferred_element_type=jnp.float32)
        gated, pullback = jax.vjp(sequence_mixer, z_raw, x_raw, step_raw, bc_raw, conv_weight, conv_bias, bc_conv_weight, bc_conv_bias, dt_bias, decay_log, skip_gain)
        inv_gate = lax.rsqrt(lax.optimization_barrier(jnp.mean(gated * gated, axis=1, keepdims=True)) + EPSILON)
        gate_hat = gated * inv_gate
        gate_out = (gate_hat * gate_gain[None, :]).astype(jnp.bfloat16)
        seq_out = seq_rows + jnp.dot(gate_out, out_weight, preferred_element_type=jnp.float32)
        cot_half = seq_cot.astype(jnp.bfloat16)
        grad_out_weight = jnp.dot(gate_out.T, cot_half, preferred_element_type=jnp.float32)
        grad_gate_out = jnp.dot(cot_half, out_weight.T, preferred_element_type=jnp.float32)
        grad_gate_gain = lax.optimization_barrier(jnp.sum(grad_gate_out * gate_hat, axis=0))
        grad_hat = grad_gate_out * gate_gain[None, :]
        grad_gated = inv_gate * (grad_hat - gate_hat * lax.optimization_barrier(jnp.mean(grad_hat * gate_hat, axis=1, keepdims=True)))
        grads = pullback(grad_gated)
        grad_bc = grads[3]
        z_half = grads[0].astype(jnp.bfloat16)
        x_half = grads[1].astype(jnp.bfloat16)
        step_half = grads[2].astype(jnp.bfloat16)
        grad_scaled = jnp.dot(z_half, weight_z.T, preferred_element_type=jnp.float32)
        grad_scaled = grad_scaled + jnp.dot(x_half, weight_x.T, preferred_element_type=jnp.float32)
        grad_scaled = grad_scaled + jnp.dot(step_half, weight_dt.T, preferred_element_type=jnp.float32)
        grad_scaled = grad_scaled + jnp.dot(grad_bc, bc_wide.T, precision=PRECISE)
        seq_grads = (lax.optimization_barrier(jnp.sum(grad_scaled * normed, axis=0)), jnp.dot(scaled.T, z_half, preferred_element_type=jnp.float32), jnp.dot(scaled.T, x_half, preferred_element_type=jnp.float32), jnp.dot(scaled.T, step_half, preferred_element_type=jnp.float32), jnp.dot(scaled.astype(jnp.float32).T, grad_bc, precision=PRECISE), grads[4], grads[5], grads[6], grads[7], grads[8], grads[9], grads[10], grad_gate_gain, grad_out_weight)
        grad_in = grad_scaled * norm_gain[None, :]
        seq_grad_hidden = seq_cot + inv_rms * (grad_in - normed * lax.optimization_barrier(jnp.mean(grad_in * normed, axis=1, keepdims=True)))
        return (jax.tree.map(jnp.add, totals, seq_grads), (seq_out, seq_grad_hidden))
    initial = tuple((jnp.zeros(item.shape, jnp.float32) for item in (norm_gain, weight_z, weight_x, weight_dt, weight_bc, conv_weight, conv_bias, bc_conv_weight, bc_conv_bias, dt_bias, decay_log, skip_gain, gate_gain, out_weight)))
    totals, (outputs, grad_rows) = lax.scan(one_sequence, initial, (hidden_seqs, cot_seqs))
    output = outputs.reshape(hidden.shape)
    grad_hidden = grad_rows.reshape(hidden.shape)
    return (output, grad_hidden, totals[0], totals[1], totals[2], totals[3], totals[4], totals[5], totals[6], totals[7], totals[8], totals[9], totals[10], totals[11], totals[12], totals[13])
```

```python
import functools

import jax
import jax.numpy as jnp
from jax import lax
from jax.experimental import pallas as pl
from jax.experimental.pallas import tpu as pltpu
from jax.sharding import PartitionSpec as P

LANES = 128
HALO = 8
TILE = 16
EPSILON = 1e-05
PRECISE = lax.Precision.HIGHEST
F32 = jnp.float32
BF16 = jnp.bfloat16
MESH = pl.DeviceIdType.MESH


def dot_f32(a, b):
    return jnp.dot(a, b, precision=PRECISE, preferred_element_type=F32)


def dot_nn(a, b):
    return lax.dot_general(a, b, (((1,), (0,)), ((), ())), preferred_element_type=F32)


def dot_nt(a, b):
    return lax.dot_general(a, b, (((1,), (1,)), ((), ())), preferred_element_type=F32)


def dot_tn(a, b):
    return lax.dot_general(a, b, (((0,), (0,)), ((), ())), preferred_element_type=F32)


def sigmoid(v):
    return 1.0 / (1.0 + jnp.exp(-v))


def iota(shape, axis):
    return lax.broadcasted_iota(jnp.int32, shape, axis)


def head_spread(chan, head_width):
    head = iota((LANES, chan), 0)
    lane = iota((LANES, chan), 1)
    return ((lane >= head * head_width) & (lane < (head + 1) * head_width)).astype(F32)


class Sizes:
    def __init__(self, mesh_sizes, hidden, weight_z, weight_dt, weight_bc):
        self.n, self.rows, self.cols = mesh_sizes
        self.pair = 2 if self.rows % 2 == 0 else 1
        self.chips = self.rows // self.pair
        self.block, self.model = hidden.shape
        self.half = weight_z.shape[0]
        self.chan = weight_z.shape[1] // self.cols
        self.row_heads = weight_dt.shape[1]
        self.heads = self.row_heads // self.cols
        self.head_width = self.chan // self.heads
        self.bc = weight_bc.shape[1]
        self.state = self.bc // 2
        self.wide = self.chan + self.bc
        self.bc_part = self.bc // self.rows
        self.head_rows = -(-self.row_heads // TILE) * TILE
        self.shard = -(-self.chan // (self.n * TILE)) * TILE
        self.shards = -(-self.chan // self.shard)
        self.inner = self.chan * self.rows * self.cols
        self.sum_rows = -(-2 * self.rows // 8) * 8
        self.gain_rows = self.model // self.chan
        self.plane_rows = -(-(5 * self.bc // self.chan + self.gain_rows) // 8) * 8


class Links:
    def __init__(self, send_sem, recv_sem):
        self.send_sem, self.recv_sem = send_sem, recv_sem
        self.count = 0
        self.makers = []

    def take(self, many=1):
        first = self.count
        self.count += many
        return first

    def copy(self, src, dst, at, device):
        return pltpu.make_async_remote_copy(
            src_ref=src,
            dst_ref=dst,
            send_sem=self.send_sem.at[at],
            recv_sem=self.recv_sem.at[at],
            device_id=device,
            device_id_type=MESH,
        )

    def send(self, src, dst, at, device, when=None):
        make = lambda: self.copy(src, dst, at, device)
        self.makers.append((make, when))
        if when is None:
            make().start()
        else:
            pl.when(when)(lambda: make().start())

    def arrived(self, dst, at, device):
        self.copy(dst, dst, at, device).wait_recv()

    def drain(self):
        for make, when in self.makers:
            if when is None:
                make().wait_send()
            else:
                pl.when(when)(lambda: make().wait_send())


def semaphore_count(sz):
    group = sz.rows * sz.cols
    units = 3 * (4 * sz.n + sz.cols)
    front = 4 * group + 8 * (sz.chips + 1) * (sz.cols + 1) + 8 * sz.cols
    scatter = 3 * (2 * sz.chips * sz.cols + sz.chips + sz.cols)
    return units + front + scatter + 2 * group + 2 * sz.n + sz.rows + sz.cols + 16


def scratch_list(sz):
    nb, n, rows, cols, chips = sz.rows, sz.n, sz.rows, sz.cols, sz.chips
    blk, half, chan, wide = sz.block, sz.half, sz.chan, sz.wide
    across = max(chips - 1, 1)
    other = max(cols - 1, 1)
    shapes = dict(
        tokens=((rows, blk, sz.model), BF16),
        weights=((cols, half, chan + wide), BF16),
        wdt_in=((cols, sz.head_rows, half), BF16),
        wdt=((cols, LANES, half), BF16),
        cots=((rows, cols, blk, half), BF16),
        outw=((cols, chan, half), BF16),
        inv_rms=((blk, LANES), F32),
        conv=((HALO, wide), F32),
        head=((HALO, LANES), F32),
        ext=((nb, HALO + blk, wide), F32),
        z_raw=((nb, blk, chan), F32),
        pre=((nb, blk, wide), F32),
        gate=((nb, blk, wide), F32),
        step_pre=((nb, blk, LANES), F32),
        log_decay=((nb, blk, LANES), F32),
        step_ch=((nb, blk, chan), F32),
        log_ch=((nb, blk, chan), F32),
        decay=((nb, sz.heads, blk, blk), F32),
        states=((nb, sz.state, chan), F32),
        state=((sz.state, chan), F32),
        mixed=((nb, blk, chan), F32),
        inside=((nb, blk, chan), F32),
        ggo=((nb, blk, chan), F32),
        sums=((rows * cols, sz.sum_rows, blk), F32),
        total=((sz.sum_rows, blk), F32),
        gate_out=((nb, blk, chan), BF16),
        grad_z=((nb, blk, chan), BF16),
        grad_x=((nb, blk, chan), BF16),
        grad_bc=((nb, blk, sz.bc), BF16),
        grad_dt=((nb, blk, LANES), BF16),
        gate_gain=((HALO, chan), F32),
        conv_grad=((HALO, wide), F32),
        head_grad=((HALO, LANES), F32),
        skip_grad=((HALO, chan), F32),
        gain_grad=((HALO, sz.model), F32),
        grad_ext=((blk + HALO, wide), F32),
        grad_state=((sz.state, chan), F32),
        own=((3, sz.shards, sz.shard, sz.model), BF16),
        landed=((3, sz.shards + 1, sz.shard, sz.model), BF16),
        other_half=((3, other, sz.shard, half), BF16),
        final=((3, sz.shards, cols, sz.shard, half), BF16),
        keep=((chips, cols, blk, half), F32),
        keep_bc=((chips, cols, sz.bc_part, half), F32),
        dt_rows=((cols, sz.head_rows, half), F32),
        small=((sz.rows * sz.cols, sz.plane_rows, chan), F32),
        dp_small=((n, HALO + sz.plane_rows, chan), F32),
        dp_bc=((n, sz.bc_part + sz.head_rows, half), BF16),
        bc_all=((rows, sz.bc_part, half), BF16),
        dots=((cols, HALO, blk), F32),
    )
    for name, part, extra in (("out", blk, 0), ("bc", sz.bc_part, sz.head_rows), ("in", blk, 0)):
        shapes[name + "_core"] = ((chips, cols, part, half), BF16)
        shapes[name + "_core_got"] = ((chips, cols, part, half), BF16)
        shapes[name + "_chip"] = ((across, cols, part, half), BF16)
        shapes[name + "_chip_got"] = ((across, cols, part, half), BF16)
        shapes[name + "_col"] = ((other, part + extra, half), BF16)
        shapes[name + "_col_got"] = ((other, part + extra, half), BF16)
    return shapes


class Scatter:
    def __init__(self, sz, links, where, bufs, name, keep):
        self.sz, self.links, self.where = sz, links, where
        self.bufs = {key: bufs[name + "_" + key] for key in ("core", "core_got", "chip", "chip_got", "col", "col_got")}
        self.keep = keep
        self.core_at = links.take(sz.chips)
        self.chip_at = links.take(sz.chips * sz.cols)
        self.col_at = links.take(sz.cols)

    def start(self, block_of):
        sz, (dp, row, col, chip, core) = self.sz, self.where
        if sz.pair == 2:
            for x in range(sz.chips):
                for h in range(sz.cols):
                    self.bufs["core"][x, h] = block_of(x * 2 + 1 - core, h).astype(BF16)
                self.links.send(
                    self.bufs["core"].at[x],
                    self.bufs["core_got"].at[x],
                    self.core_at + x,
                    (dp, chip * 2 + 1 - core, col),
                )
        for x in range(sz.chips):
            for h in range(sz.cols):
                self.keep[x, h] = block_of(x * sz.pair + core, h)

    def held(self, x, h):
        value = self.keep[x, h]
        if self.sz.pair == 2:
            value = value + self.bufs["core_got"][x, h].astype(F32)
        return value

    def across(self):
        sz, (dp, row, col, chip, core) = self.sz, self.where
        if sz.pair == 2:
            for x in range(sz.chips):
                self.links.arrived(self.bufs["core_got"].at[x], self.core_at + x, (dp, chip * 2 + 1 - core, col))
        for k in [*range(1, sz.cols), 0]:
            h = lax.rem(col + k, sz.cols)
            for dx in range(1, sz.chips):
                x = lax.rem(chip + dx, sz.chips)
                self.bufs["chip"][dx - 1, k] = self.held(x, h).astype(BF16)
                self.links.send(
                    self.bufs["chip"].at[dx - 1, k],
                    self.bufs["chip_got"].at[dx - 1, k],
                    self.chip_at + dx * sz.cols + k,
                    (dp, x * sz.pair + core, col),
                )

    def summed(self, k):
        sz, (dp, row, col, chip, core) = self.sz, self.where
        value = self.held(chip, lax.rem(col + k, sz.cols))
        for dx in range(1, sz.chips):
            x = lax.rem(chip + dx, sz.chips)
            self.links.arrived(
                self.bufs["chip_got"].at[dx - 1, k], self.chip_at + dx * sz.cols + k, (dp, x * sz.pair + core, col)
            )
            value = value + self.bufs["chip_got"][dx - 1, k].astype(F32)
        return value

    def turn(self, extra=None):
        sz, (dp, row, col, chip, core) = self.sz, self.where
        for k in range(1, sz.cols):
            h = lax.rem(col + k, sz.cols)
            value = self.summed(k)
            part = value.shape[0]
            self.bufs["col"][k - 1, 0:part, :] = value.astype(BF16)
            if extra is not None:
                more = extra(h)
                self.bufs["col"][k - 1, part : part + more.shape[0], :] = more.astype(BF16)
            self.links.send(
                self.bufs["col"].at[k - 1], self.bufs["col_got"].at[k - 1], self.col_at + k, (dp, row, h)
            )

    def finish(self, extra=None):
        sz, (dp, row, col, chip, core) = self.sz, self.where
        value = self.summed(0)
        more = None if extra is None else extra(col)
        part = value.shape[0]
        for k in range(1, sz.cols):
            h = lax.rem(col + k, sz.cols)
            self.links.arrived(self.bufs["col_got"].at[k - 1], self.col_at + k, (dp, row, h))
            value = value + self.bufs["col_got"][k - 1, 0:part, :].astype(F32)
            if more is not None:
                more = more + self.bufs["col_got"][k - 1, part:, :].astype(F32)
        return value, more


class Chain:
    def __init__(self, sz, links, where, bufs, unit):
        self.sz, self.links, self.where, self.unit = sz, links, where, unit
        self.own = bufs["own"].at[unit]
        self.landed = bufs["landed"].at[unit]
        self.other_half = bufs["other_half"].at[unit]
        self.final = bufs["final"].at[unit]
        self.sum_at = [links.take(sz.n), links.take(sz.n)]
        self.col_at = links.take(sz.cols)
        self.out_at = [links.take(sz.n), links.take(sz.n)]

    def sides(self):
        dp, row, col = self.where[:3]
        last = self.sz.n - 1
        right = (jnp.minimum(dp + 1, last), row, col)
        left = (jnp.maximum(dp - 1, 0), row, col)
        return ((0, 1, right, left, dp < last, dp > 0), (1, -1, left, right, dp > 0, dp < last))

    def fold(self, way, shard, source):
        slot = shard + 1 - way
        self.links.arrived(self.landed.at[slot], self.sum_at[way] + shard, source)
        self.own[shard] = (self.own[shard].astype(F32) + self.landed[slot].astype(F32)).astype(BF16)

    def reduce(self, distance):
        dp = self.where[0]
        for way, sign, target, source, can_send, can_take in self.sides():
            shard = dp + sign * distance
            inside = (shard >= 0) & (shard < self.sz.shards)
            safe = jnp.clip(shard, 0, self.sz.shards - 1)
            if distance < self.sz.n - 1:
                pl.when(inside & can_take)(functools.partial(self.fold, way, safe, source))
            self.links.send(
                self.own.at[safe], self.landed.at[safe + 1 - way], self.sum_at[way] + safe, target, inside
            )

    def owner(self):
        dp, sz = self.where[0], self.sz
        return dp < sz.shards, jnp.minimum(dp, sz.shards - 1)

    def settle(self):
        sz, (dp, row, col) = self.sz, self.where[:3]
        owns, safe = self.owner()
        for way, sign, target, source, can_send, can_take in self.sides():
            pl.when(can_take & owns)(functools.partial(self.fold, way, safe, source))
        for k in range(sz.cols):
            h = lax.rem(col + k, sz.cols)
            half = self.own[safe, :, pl.ds(pl.multiple_of(h * sz.half, LANES), sz.half)]
            if k > 0:
                self.other_half[k - 1] = half
                self.links.send(
                    self.other_half.at[k - 1], self.final.at[safe, col], self.col_at + k, (dp, row, h), owns
                )
            else:

                @pl.when(owns)
                def _():
                    self.final[safe, col] = half

    def share(self, distance):
        sz, (dp, row, col) = self.sz, self.where[:3]
        if distance == 0:
            owns, at = self.owner()
            for k in range(1, sz.cols):
                h = lax.rem(col + sz.cols - k, sz.cols)
                pl.when(owns)(
                    lambda: self.links.arrived(self.final.at[at, h], self.col_at + k, (dp, row, h))
                )
        for way, sign, target, source, can_send, can_take in self.sides():
            shard = dp - sign * distance
            inside = (shard >= 0) & (shard < sz.shards)
            safe = jnp.clip(shard, 0, sz.shards - 1)
            if distance > 0:
                pl.when(inside)(
                    lambda: self.links.arrived(self.final.at[safe], self.out_at[way] + safe, source)
                )
            if distance < sz.n - 1:
                self.links.send(
                    self.final.at[safe], self.final.at[safe], self.out_at[way] + safe, target, inside & can_send
                )

    def steps(self):
        n = self.sz.n
        todo = [functools.partial(self.reduce, d) for d in range(n - 1, 0, -1)]
        todo.append(self.settle)
        todo += [functools.partial(self.share, d) for d in range(n)]
        return todo


def forward_block(sz, m, b):
    blk, chan, wide, half = sz.block, sz.chan, sz.wide, sz.half
    acc = jnp.zeros((blk, chan + wide), F32)
    step_raw = jnp.zeros((blk, LANES), F32)
    for h in range(sz.cols):
        part = m.tokens[b, :, h * half : (h + 1) * half]
        acc = acc + dot_nn(part, m.weights[h])
        step_raw = step_raw + dot_nt(part, m.wdt[h])
    z_raw = acc[:, :chan]
    m.z_raw[b] = z_raw
    m.ext[b, HALO : HALO + blk, :] = acc[:, chan:]

    @pl.when(b + 1 < sz.rows)
    def _():
        m.ext[b + 1, 0:HALO, :] = m.ext[b, blk : blk + HALO, :]

    pre = m.conv[4:5, :]
    for tap in range(4):
        first = HALO - 3 + tap
        pre = pre + m.conv[tap : tap + 1, :] * m.ext[b, first : first + blk, :]
    gate = sigmoid(pre)
    m.pre[b] = pre
    m.gate[b] = gate
    conv = pre * gate
    step_pre = step_raw + m.head[0:1, :]
    m.step_pre[b] = step_pre
    step = jnp.maximum(step_pre, 0.0) + jnp.log1p(jnp.exp(-jnp.abs(step_pre)))
    rate = -jnp.exp(m.head[1:2, :])
    causal = iota((blk, blk), 0) >= iota((blk, blk), 1)
    log_decay = dot_f32(causal.astype(F32), step * rate)
    m.log_decay[b] = log_decay
    spread = head_spread(chan, sz.head_width)
    step_ch = dot_f32(step, spread)
    log_ch = dot_f32(log_decay, spread)
    m.step_ch[b] = step_ch
    m.log_ch[b] = log_ch
    skip_ch = dot_f32(jnp.broadcast_to(m.head[2:3, :], (HALO, LANES)), spread)[0:1, :]

    x_conv = conv[:, :chan]
    b_half = conv[:, chan : chan + sz.state].astype(BF16)
    c_half = conv[:, chan + sz.state :].astype(BF16)
    stepped = x_conv * step_ch
    scores = dot_nt(c_half, b_half)
    log_rows = log_decay.T
    lane = iota((blk, chan), 1)
    inside = jnp.zeros((blk, chan), F32)
    for head in range(sz.heads):
        gap = log_decay[:, head : head + 1] - log_rows[head : head + 1, :]
        decay = jnp.exp(jnp.where(causal, gap, -1e30))
        m.decay[b, head] = decay
        mixing = (scores * decay).astype(BF16)
        mine = (lane >= head * sz.head_width) & (lane < (head + 1) * sz.head_width)
        inside = inside + dot_nn(mixing, jnp.where(mine, stepped, 0.0).astype(BF16))
    entering = m.state[...]
    m.states[b] = entering
    outside = dot_nn(c_half, entering.astype(BF16)) * jnp.exp(log_ch)
    mixed = inside + outside + skip_ch * x_conv
    last = log_ch[blk - 1 : blk, :]
    tail = stepped * jnp.exp(last - log_ch)
    m.state[...] = entering * jnp.exp(last) + dot_tn(b_half, tail.astype(BF16))
    m.mixed[b] = mixed
    m.inside[b] = inside


def backward_block(sz, m, b, shift):
    blk, chan, wide = sz.block, sz.chan, sz.wide
    pre = m.pre[b]
    gate = m.gate[b]
    conv = pre * gate
    step_pre = m.step_pre[b]
    step = jnp.maximum(step_pre, 0.0) + jnp.log1p(jnp.exp(-jnp.abs(step_pre)))
    rate = -jnp.exp(m.head[1:2, :])
    step_ch = m.step_ch[b]
    log_ch = m.log_ch[b]
    spread = head_spread(chan, sz.head_width)
    skip_ch = dot_f32(jnp.broadcast_to(m.head[2:3, :], (HALO, LANES)), spread)[0:1, :]
    x_conv = conv[:, :chan]
    b_half = conv[:, chan : chan + sz.state].astype(BF16)
    c_half = conv[:, chan + sz.state :].astype(BF16)
    stepped = x_conv * step_ch
    stepped_half = stepped.astype(BF16)
    grad_mixed = m.ggo[b]
    grad_half = grad_mixed.astype(BF16)
    inside = m.inside[b]
    outside = m.mixed[b] - inside - skip_ch * x_conv

    scores = dot_nt(c_half, b_half)
    lane = iota((blk, chan), 1)
    grad_scores = jnp.zeros((blk, blk), F32)
    grad_inner = jnp.zeros((blk, chan), F32)
    for head in range(sz.heads):
        decay = m.decay[b, head]
        mixing = (scores * decay).astype(BF16)
        mine = (lane >= head * sz.head_width) & (lane < (head + 1) * sz.head_width)
        grad_mine = jnp.where(mine, grad_mixed, 0.0).astype(BF16)
        grad_scores = grad_scores + dot_nt(grad_mine, stepped_half) * decay
        grad_inner = grad_inner + dot_tn(mixing, grad_mine)
    scores_half = grad_scores.astype(BF16)

    entering = m.states[b]
    left = m.grad_state[...]
    left_half = left.astype(BF16)
    grad_outer = (grad_mixed * jnp.exp(log_ch)).astype(BF16)
    last = log_ch[blk - 1 : blk, :]
    fade = jnp.exp(last - log_ch)
    tail = stepped * fade
    grad_tail = dot_nn(b_half, left_half)
    tail_term = tail * grad_tail
    grad_c = dot_nt(grad_outer, entering.astype(BF16)) + dot_nn(scores_half, b_half)
    grad_b = dot_nt(tail.astype(BF16), left_half) + dot_tn(scores_half, c_half)
    grad_last = jnp.sum(tail_term, axis=0, keepdims=True) + jnp.exp(last) * jnp.sum(
        left * entering, axis=0, keepdims=True
    )
    m.grad_state[...] = left * jnp.exp(last) + dot_tn(c_half, grad_outer)

    grad_stepped = grad_inner + grad_tail * fade
    log_term = (
        grad_half.astype(F32) * inside
        + grad_mixed * outside
        - stepped_half.astype(F32) * grad_inner
        - tail_term
    )
    row = iota((blk, chan), 0)
    log_term = log_term + jnp.where(row == blk - 1, grad_last, 0.0)

    def per_head(values):
        return lax.dot_general(
            values, spread, (((1,), (1,)), ((), ())), precision=PRECISE, preferred_element_type=F32
        )

    later = (iota((blk, blk), 0) <= iota((blk, blk), 1)).astype(F32)
    grad_rate_step = dot_f32(later, per_head(log_term))
    grad_step = per_head(grad_stepped * x_conv) + grad_rate_step * rate
    grad_step_raw = grad_step * sigmoid(step_pre)
    m.head_grad[0:1, :] += jnp.sum(grad_step_raw, axis=0, keepdims=True)
    m.head_grad[1:2, :] += jnp.sum(grad_rate_step * step, axis=0, keepdims=True) * rate
    m.skip_grad[0:1, :] += jnp.sum(grad_mixed * x_conv, axis=0, keepdims=True)

    grad_x = grad_stepped * step_ch + grad_mixed * skip_ch
    slope = gate * (1.0 + pre * (1.0 - gate))
    m.grad_ext[blk : blk + HALO, :] = m.grad_ext[0:HALO, :]
    m.grad_ext[0:blk, 0:chan] = grad_x * slope[:, :chan]
    m.grad_ext[0:blk, chan : chan + sz.state] = grad_b * slope[:, chan : chan + sz.state]
    m.grad_ext[0:blk, chan + sz.state :] = grad_c * slope[:, chan + sz.state :]
    grad_pre = m.grad_ext[0:blk, :]
    grad_raw = jnp.zeros((blk, wide), F32)
    for tap in range(4):
        grad_raw = grad_raw + m.conv[tap : tap + 1, :] * m.grad_ext[3 - tap : 3 - tap + blk, :]
        first = HALO - 3 + tap
        m.conv_grad[tap : tap + 1, :] += jnp.sum(
            grad_pre * m.ext[b, first : first + blk, :], axis=0, keepdims=True
        )
    m.conv_grad[4:5, :] += jnp.sum(grad_pre, axis=0, keepdims=True)
    m.grad_x[b] = grad_raw[:, :chan].astype(BF16)
    m.grad_bc[b] = grad_raw[:, chan:].astype(BF16)
    m.grad_dt[b] = dot_nn(grad_step_raw.astype(BF16), shift).astype(BF16)


class Refs:
    pass


def block_kernel(sz, names, *refs):
    m = Refs()
    for name, ref in zip(names, refs):
        setattr(m, name, ref)
    bufs = m.__dict__
    nb, rows, cols, chips, pair = sz.rows, sz.rows, sz.cols, sz.chips, sz.pair
    blk, half, chan, wide, n = sz.block, sz.half, sz.chan, sz.wide, sz.n
    dp, row, col = lax.axis_index("dp"), lax.axis_index("row"), lax.axis_index("col")
    chip, core = row // pair, lax.rem(row, pair)
    where = (dp, row, col, chip, core)
    group = rows * cols
    mine = row * cols + col
    sibling = (dp, chip * pair + lax.rem(core + 1, pair), col)
    sibling_core = lax.rem(core + 1, pair)

    def plane_peer(k):
        return dp, lax.rem(row + k // cols, rows), lax.rem(col + k % cols, cols)

    def line_peer(k):
        return lax.rem(dp + k, n), row, col

    def col_peer(k):
        return dp, row, lax.rem(col + k, cols)

    def chip_peer(dx):
        return dp, lax.rem(chip + dx, chips) * pair + core, col

    def from_chip(dx):
        return lax.rem(chip + chips - dx, chips) * pair + core

    def from_sibling(dx):
        return lax.rem(chip + chips - dx, chips) * pair + sibling_core

    def from_col(k):
        return lax.rem(col + cols - k, cols)

    links = Links(m.send_sem, m.recv_sem)
    barrier = pltpu.get_barrier_semaphore()
    peers = [plane_peer(k) for k in range(1, group)] + [line_peer(k) for k in range(1, n)]
    for peer in peers:
        pl.semaphore_signal(barrier, inc=1, device_id=peer, device_id_type=MESH)

    def lanes(start, size):
        return pl.ds(pl.multiple_of(start * size, LANES), size)

    hidden = m.hidden[...]
    inv_rms = lax.rsqrt(jnp.mean(hidden * hidden, axis=1, keepdims=True) + EPSILON)
    m.inv_rms[...] = jnp.broadcast_to(inv_rms, (blk, LANES))
    m.tokens[row] = (hidden * inv_rms * m.norm_gain[...]).astype(BF16)
    m.cots[row, col] = m.cotangent[...].astype(BF16)
    m.wdt_in[col] = m.weight_dt[...]

    pl.semaphore_wait(barrier, len(peers))

    w_at, bc_at, dt_at, bc_fwd = links.take(2 * cols), links.take(cols), links.take(cols), links.take(cols)
    tok_x, tok_s = links.take(chips), links.take(chips)
    cot_y, cot_x, cot_s = links.take(cols), links.take(chips * cols), links.take(chips * cols)
    out_at = links.take(cols)
    bc_rows = half // pair
    bc_mine = pl.ds(pl.multiple_of(core * bc_rows, TILE), bc_rows)
    bc_sib = pl.ds(pl.multiple_of(sibling_core * bc_rows, TILE), bc_rows)
    bc_lanes = pl.ds(2 * chan, sz.bc)
    for k in range(1, cols):
        peer = col_peer(k)
        links.send(
            m.weight_z.at[:, lanes(peer[2], chan)], m.weights.at[col, :, pl.ds(0, chan)], w_at + 2 * k, peer
        )
        links.send(
            m.weight_x.at[:, lanes(peer[2], chan)], m.weights.at[col, :, pl.ds(chan, chan)], w_at + 2 * k + 1, peer
        )
        links.send(m.weight_bc.at[bc_mine, :], m.weights.at[col, bc_mine, bc_lanes], bc_at + k, peer)
        links.send(m.wdt_in.at[col], m.wdt_in.at[col], dt_at + k, peer)
    for dx in range(1, chips):
        links.send(m.tokens.at[row], m.tokens.at[row], tok_x + dx, chip_peer(dx))
    if pair == 2:
        links.send(m.tokens.at[row], m.tokens.at[row], tok_s, sibling)

    m.weights[col, :, 0:chan] = m.weight_z[:, lanes(col, chan)]
    m.weights[col, :, chan : 2 * chan] = m.weight_x[:, lanes(col, chan)]
    m.weights[col, :, 2 * chan :] = m.weight_bc[...]
    m.outw[col] = m.out_weight[pl.ds(pl.multiple_of(col * chan, TILE), chan), :]
    for ref in (m.conv, m.head, m.state, m.grad_state, m.grad_ext, m.gate_gain, m.conv_grad, m.head_grad):
        ref[...] = jnp.zeros_like(ref)
    for ref in (m.skip_grad, m.gain_grad):
        ref[...] = jnp.zeros_like(ref)
    m.ext[0, 0:HALO, :] = jnp.zeros((HALO, wide), F32)
    m.conv[0:4, 0:chan] = m.conv_weight[...]
    m.conv[0:4, chan:] = m.bc_conv_weight[...]
    m.conv[4:5, 0:chan] = m.conv_bias[...]
    m.conv[4:5, chan:] = m.bc_conv_bias[...]
    m.head[0:1, 0 : sz.heads] = m.dt_bias[...]
    m.head[1:2, 0 : sz.heads] = m.decay_log[...]
    m.head[2:3, 0 : sz.heads] = m.skip_gain[...]

    def send_cots(dx, k, r, c):
        if dx == 0:
            for far in range(1, chips):
                links.send(m.cots.at[r, c], m.cots.at[r, c], cot_x + far * cols + k, chip_peer(far))
        if pair == 2:
            links.send(m.cots.at[r, c], m.cots.at[r, c], cot_s + dx * cols + k, sibling)

    for dx in range(1, chips):
        links.arrived(m.tokens.at[from_chip(dx)], tok_x + dx, chip_peer(dx))
        if pair == 2:
            links.send(m.tokens.at[from_chip(dx)], m.tokens.at[from_chip(dx)], tok_s + dx, sibling)
    send_cots(0, 0, row, col)
    for k in range(1, cols):
        peer, src = col_peer(k), from_col(k)
        links.arrived(m.weights.at[src, :, pl.ds(0, chan)], w_at + 2 * k, peer)
        links.arrived(m.weights.at[src, :, pl.ds(chan, chan)], w_at + 2 * k + 1, peer)
        links.arrived(m.weights.at[src, bc_mine, bc_lanes], bc_at + k, peer)
        if pair == 2:
            links.send(
                m.weights.at[src, bc_mine, bc_lanes], m.weights.at[src, bc_mine, bc_lanes], bc_fwd + k, sibling
            )
        links.arrived(m.wdt_in.at[src], dt_at + k, peer)
        links.send(m.cots.at[row, col], m.cots.at[row, col], cot_y + k, peer)
        links.send(
            m.out_weight.at[pl.ds(pl.multiple_of(peer[2] * chan, TILE), chan), :], m.outw.at[col], out_at + k, peer
        )

    head_at, head_to = iota((LANES, LANES), 0), iota((LANES, LANES), 1)
    shift = ((head_to == head_at + col * sz.heads) & (head_at < sz.heads)).astype(BF16)
    for h in range(cols):
        padded = jnp.concatenate([m.wdt_in[h], jnp.zeros((LANES - sz.head_rows, half), BF16)], axis=0)
        m.wdt[h] = dot_nn(shift, padded).astype(BF16)

    if pair == 2:
        for dx in range(chips):
            links.arrived(m.tokens.at[from_sibling(dx)], tok_s + dx, sibling)
        for k in range(1, cols):
            links.arrived(m.weights.at[from_col(k), bc_sib, bc_lanes], bc_fwd + k, sibling)

    def pass_col_cots():
        for k in range(1, cols):
            links.arrived(m.cots.at[row, from_col(k)], cot_y + k, col_peer(k))

    def pass_chip_cots(k):
        for dx in range(1, chips):
            r, c = from_chip(dx), from_col(k)
            links.arrived(m.cots.at[r, c], cot_x + dx * cols + k, chip_peer(dx))

    def forward_step(b, carry):
        forward_block(sz, m, b)
        return carry

    early = min(2, nb)
    lax.fori_loop(0, early, forward_step, 0)
    pass_col_cots()
    for k in range(1, cols):
        send_cots(0, k, row, from_col(k))
    pass_chip_cots(0)
    for dx in range(1, chips):
        send_cots(dx, 0, from_chip(dx), col)
    lax.fori_loop(early, nb, forward_step, 0)
    for k in range(1, cols):
        pass_chip_cots(k)
        for dx in range(1, chips):
            send_cots(dx, k, from_chip(dx), from_col(k))
    for k in range(1, cols):
        links.arrived(m.outw.at[from_col(k)], out_at + k, col_peer(k))
    if pair == 2:
        for dx in range(chips):
            for k in range(cols):
                links.arrived(m.cots.at[from_sibling(dx), from_col(k)], cot_s + dx * cols + k, sibling)

    sub = iota((LANES, blk), 0)
    m.sums[mine] = jnp.zeros((sz.sum_rows, blk), F32)

    def sum_step(b, carry):
        ggo = jnp.zeros((blk, chan), F32)
        for h in range(cols):
            ggo = ggo + dot_nt(m.cots[b, h], m.outw[h])
        m.ggo[b] = ggo
        z_raw = m.z_raw[b]
        gated = m.mixed[b] * (z_raw * sigmoid(z_raw))
        squares = jnp.sum(gated * gated, axis=1, keepdims=True)
        inner = jnp.sum(ggo * m.gate_gain_in[...] * gated, axis=1, keepdims=True)
        lane = iota((blk, LANES), 1)
        both = jnp.where(lane == 0, squares, jnp.where(lane == 1, inner, 0.0)).T
        m.sums[mine, pl.ds(b, 1), :] = both[0:1, :]
        m.sums[mine, pl.ds(nb + b, 1), :] = both[1:2, :]
        return carry

    lax.fori_loop(0, nb, sum_step, 0)

    def to_plane(ref):
        at = links.take(group)
        for k in range(1, group):
            links.send(ref.at[mine], ref.at[mine], at + k, plane_peer(k))
        return at

    def from_plane(ref, at):
        for k in range(1, group):
            r, c = lax.rem(row + rows - k // cols, rows), lax.rem(col + cols - k % cols, cols)
            links.arrived(ref.at[r * cols + c], at + k, plane_peer(k))
        value = ref[0]
        for k in range(1, group):
            value = value + ref[k]
        return value

    m.total[...] = from_plane(m.sums, to_plane(m.sums))

    def gate_step(b, carry):
        first = m.total[pl.ds(b, 1), :]
        second = m.total[pl.ds(nb + b, 1), :]
        both = jnp.where(sub == 0, first, jnp.where(sub == 1, second, 0.0)).T
        inv_gate = lax.rsqrt(both[:, 0:1] / sz.inner + EPSILON)
        gate_dot = both[:, 1:2] * inv_gate
        ggo = m.ggo[b]
        gate_gain = m.gate_gain_in[...]
        z_raw = m.z_raw[b]
        z_gate = sigmoid(z_raw)
        mixed = m.mixed[b]
        gate_hat = mixed * (z_raw * z_gate) * inv_gate
        grad_gated = inv_gate * (ggo * gate_gain - gate_hat * (gate_dot / sz.inner))
        m.grad_z[b] = (grad_gated * mixed * (z_gate * (1.0 + z_raw * (1.0 - z_gate)))).astype(BF16)
        m.gate_out[b] = (gate_hat * gate_gain).astype(BF16)
        m.gate_gain[0:1, :] += jnp.sum(ggo * gate_hat, axis=0, keepdims=True)
        m.ggo[b] = grad_gated * (z_raw * z_gate)
        return carry

    lax.fori_loop(0, nb, gate_step, 0)

    def flat(ref):
        value = ref[...]
        return value.reshape(value.shape[0] * value.shape[1], value.shape[2])

    def store_shards(unit, lanes_at, value):
        for s in range(sz.shards):
            low, high = s * sz.shard, min((s + 1) * sz.shard, chan)
            m.own[unit, s, 0 : high - low, lanes_at] = value[low:high].astype(BF16)
            if high < (s + 1) * sz.shard:
                m.own[unit, s, high - low :, lanes_at] = jnp.zeros(
                    ((s + 1) * sz.shard - high, value.shape[1]), BF16
                )

    chains = [Chain(sz, links, where, bufs, unit) for unit in range(3)]
    out_steps, z_steps, x_steps = [chain.steps() for chain in chains]

    def collect(unit, ref):
        for s in range(sz.shards):
            low, high = s * sz.shard, min((s + 1) * sz.shard, chan)
            for c in range(cols):
                ref[c * chan + low : c * chan + high, :] = m.final[unit, s, c, 0 : high - low, :]

    def weight_part(unit, grads, operand_of):
        for h in range(cols):
            store_shards(unit, slice(h * half, (h + 1) * half), dot_tn(grads, operand_of(h)))

    def cots_of(h):
        return m.cots[:, h].reshape(rows * blk, half)

    def tokens_of(h):
        return m.tokens[:, :, h * half : (h + 1) * half].reshape(rows * blk, half)

    weight_part(0, flat(m.gate_out), cots_of)
    out_steps[0]()
    weight_part(1, flat(m.grad_z), tokens_of)
    z_steps[0]()
    out_sum = Scatter(sz, links, where, bufs, "out", m.keep)
    out_sum.start(lambda r, h: dot_nn(m.gate_out[r], m.outw[h]))

    def backward_step(i, carry):
        backward_block(sz, m, nb - 1 - i, shift)
        return carry

    services = [[out_sum.across, out_steps[1], z_steps[1]], [out_steps[2], z_steps[2], out_sum.turn], []]
    done = 0
    for i, service in enumerate(services):
        until = nb if i == len(services) - 1 else min(nb, done + max(nb // 4, 1))
        lax.fori_loop(done, until, backward_step, 0)
        done = until
        for step in service:
            step()

    weight_part(2, flat(m.grad_x), tokens_of)
    x_steps[0]()
    dt_grads = flat(m.grad_dt)
    for h in range(cols):
        part = dot_tn(flat(m.grad_bc), tokens_of(h))
        m.bc_full[h] = part.reshape(rows, sz.bc_part, half)
        m.dt_rows[h] = dot_tn(dt_grads, tokens_of(h))[0 : sz.head_rows, :]
    bc_sum = Scatter(sz, links, where, bufs, "bc", m.keep_bc)
    bc_sum.start(lambda r, h: m.bc_full[h, r])

    total, _ = out_sum.finish()
    m.output[...] = m.hidden[:, lanes(col, half)] + total

    def grad_block(r, h):
        w = m.weights.at[h]
        value = dot_nt(m.grad_z[r], w[:, 0:chan])
        value = value + dot_nt(m.grad_x[r], w[:, chan : 2 * chan])
        value = value + dot_nt(m.grad_bc[r], w[:, 2 * chan :])
        padded = jnp.concatenate([m.wdt_in[h], jnp.zeros((LANES - sz.head_rows, half), BF16)], axis=0)
        value = value + dot_nn(m.grad_dt[r], padded)
        at = slice(h * half, (h + 1) * half)
        m.gain_grad[0:1, at] += jnp.sum(value * m.tokens[r, :, at].astype(F32), axis=0, keepdims=True)
        return value

    in_sum = Scatter(sz, links, where, bufs, "in", m.keep)
    in_sum.start(grad_block)
    bc_sum.across()
    for step in out_steps[3:5] + z_steps[3:5] + x_steps[1:2]:
        step()
    in_sum.across()

    m.small[mine] = jnp.zeros((sz.plane_rows, chan), F32)
    per_row = sz.bc // chan
    for j in range(5):
        for p in range(per_row):
            at = chan + p * chan
            m.small[mine, j * per_row + p : j * per_row + p + 1, :] = m.conv_grad[j : j + 1, at : at + chan]
    for j in range(sz.gain_rows):
        at = 5 * per_row + j
        m.small[mine, at : at + 1, :] = m.gain_grad[0:1, j * chan : (j + 1) * chan]
    small_at = to_plane(m.small)
    for step in out_steps[5:6] + z_steps[5:6] + x_steps[2:3]:
        step()
    dt_of = lambda h: m.dt_rows[h]
    bc_sum.turn(dt_of)
    spread = head_spread(chan, sz.head_width)
    skip_heads = lax.dot_general(
        m.skip_grad[...], spread, (((1,), (1,)), ((), ())), precision=PRECISE, preferred_element_type=F32
    )
    m.dp_small[dp] = jnp.zeros((HALO + sz.plane_rows, chan), F32)
    m.dp_small[dp, 0:5, :] = m.conv_grad[0:5, 0:chan]
    m.dp_small[dp, 5:6, :] = m.gate_gain[0:1, :]
    m.dp_small[dp, 6:7, 0:LANES] = m.head_grad[0:1, :]
    m.dp_small[dp, 6:7, LANES : 2 * LANES] = m.head_grad[1:2, :]
    m.dp_small[dp, 7:8, 0:LANES] = skip_heads[0:1, :]
    m.dp_small[dp, HALO:, :] = from_plane(m.small, small_at)

    def to_line(ref):
        at = links.take(n)
        for k in range(1, n):
            links.send(ref.at[dp], ref.at[dp], at + k, line_peer(k))
        return at

    def from_line(ref, at):
        for k in range(1, n):
            links.arrived(ref.at[lax.rem(dp + n - k, n)], at + k, line_peer(k))
        value = ref[0].astype(F32)
        for k in range(1, n):
            value = value + ref[k].astype(F32)
        return value

    small_line = to_line(m.dp_small)
    bc_value, dt_value = bc_sum.finish(dt_of)
    m.dp_bc[dp, 0 : sz.bc_part, :] = bc_value.astype(BF16)
    m.dp_bc[dp, sz.bc_part :, :] = dt_value.astype(BF16)
    bc_line = to_line(m.dp_bc)
    for step in x_steps[3:5]:
        step()
    in_sum.turn()

    bc_total = from_line(m.dp_bc, bc_line)
    m.grad_weight_dt[...] = bc_total[sz.bc_part :, :]
    m.bc_all[row] = bc_total[0 : sz.bc_part, :].astype(BF16)
    row_at = links.take(rows)
    for k in range(1, rows):
        links.send(m.bc_all.at[row], m.bc_all.at[row], row_at + k, (dp, lax.rem(row + k, rows), col))

    grad_scaled, _ = in_sum.finish()
    inv_wide = m.inv_rms[:, 0:1]
    normed = m.hidden[:, lanes(col, half)] * inv_wide
    grad_in = grad_scaled * m.norm_gain[:, lanes(col, half)]
    dot = jnp.sum(grad_in * normed, axis=1, keepdims=True)
    lane = iota((blk, LANES), 1)
    m.dots[col] = jnp.where(lane == 0, dot, 0.0).T[0:HALO, :]
    dot_at = links.take(cols)
    for k in range(1, cols):
        links.send(m.dots.at[col], m.dots.at[col], dot_at + k, col_peer(k))
    for step in out_steps[6:] + z_steps[6:] + x_steps[5:6]:
        step()
    collect(0, m.grad_out_weight)
    collect(1, m.grad_weight_z)
    for k in range(1, cols):
        links.arrived(m.dots.at[from_col(k)], dot_at + k, col_peer(k))
    dots = m.dots[0]
    for k in range(1, cols):
        dots = dots + m.dots[k]
    full = jnp.concatenate([dots, jnp.zeros((LANES - HALO, blk), F32)], axis=0).T
    m.grad_hidden[...] = m.cotangent[...] + inv_wide * (grad_in - normed * (full[:, 0:1] / sz.model))

    summed = from_line(m.dp_small, small_line)
    m.small_sums[...] = summed
    per_half = half // chan
    for j in range(per_half):
        at = HALO + 5 * per_row
        line = jnp.zeros((1, chan), F32)
        for c in range(cols):
            here = summed[at + c * per_half + j : at + c * per_half + j + 1, :]
            line = jnp.where(col == c, here, line)
        gain = m.norm_gain[:, pl.ds(pl.multiple_of(col * half + j * chan, LANES), chan)]
        m.grad_norm_gain[:, j * chan : (j + 1) * chan] = line / gain

    for k in range(1, rows):
        at = lax.rem(row + rows - k, rows)
        links.arrived(m.bc_all.at[at], row_at + k, (dp, lax.rem(row + k, rows), col))
    m.grad_weight_bc[...] = flat(m.bc_all)
    for step in x_steps[6:]:
        step()
    collect(2, m.grad_weight_x)
    links.drain()


def finish_kernel(sz, sent, results, *refs):
    i, o = Refs(), Refs()
    for name, ref in zip(sent, refs):
        setattr(i, name, ref)
    for name, ref in zip(results, refs[len(sent) :]):
        setattr(o, name, ref)
    chan = sz.chan
    per_row = sz.bc // chan
    for name in ("output", "grad_hidden", "grad_norm_gain"):
        getattr(o, name)[...] = getattr(i, name)[...]
    o.grad_out_weight[...] = i.grad_out_weight[...].astype(F32)
    for name in ("grad_weight_z", "grad_weight_x", "grad_weight_bc"):
        getattr(o, name)[...] = getattr(i, name)[...].astype(F32).T
    o.grad_weight_dt[...] = i.grad_weight_dt[...].T[:, 0 : sz.row_heads]
    o.grad_conv_weight[...] = i.small_sums[0:4, :]
    o.grad_conv_bias[...] = i.small_sums[4:5, :]
    o.grad_gate_gain[...] = i.small_sums[5:6, :]
    o.grad_dt_bias[...] = i.small_sums[6:7, 0 : sz.heads]
    o.grad_decay_log[...] = i.small_sums[6:7, LANES : LANES + sz.heads]
    o.grad_skip_gain[...] = i.small_sums[7:8, 0 : sz.heads]
    for j in range(5):
        for p in range(per_row):
            at = HALO + j * per_row + p
            lanes = slice(p * chan, (p + 1) * chan)
            if j < 4:
                o.grad_bc_conv_weight[j : j + 1, lanes] = i.small_sums[at : at + 1, :]
            else:
                o.grad_bc_conv_bias[:, lanes] = i.small_sums[at : at + 1, :]


def body(
    mesh_sizes,
    hidden,
    cotangent,
    norm_gain,
    weight_z,
    weight_x,
    weight_dt,
    weight_bc,
    conv_weight,
    conv_bias,
    bc_conv_weight,
    bc_conv_bias,
    dt_bias,
    decay_log,
    skip_gain,
    gate_gain,
    out_weight,
):
    sz = Sizes(mesh_sizes, hidden, weight_z, weight_dt, weight_bc)
    wide_dt = jnp.pad(weight_dt.T, ((0, sz.head_rows - sz.row_heads), (0, 0)))
    line = lambda vector: vector[None, :]
    inputs = dict(
        hidden=hidden,
        cotangent=cotangent,
        norm_gain=line(norm_gain),
        weight_z=weight_z,
        weight_x=weight_x,
        weight_dt=wide_dt,
        weight_bc=weight_bc,
        conv_weight=conv_weight,
        conv_bias=line(conv_bias),
        bc_conv_weight=bc_conv_weight,
        bc_conv_bias=line(bc_conv_bias),
        dt_bias=line(dt_bias),
        decay_log=line(decay_log),
        skip_gain=line(skip_gain),
        gate_gain_in=line(gate_gain),
        out_weight=out_weight,
    )
    matrix = ((sz.cols * sz.chan, sz.half), BF16)
    outputs = dict(
        output=((sz.block, sz.half), F32),
        grad_hidden=((sz.block, sz.half), F32),
        grad_norm_gain=((1, sz.half), F32),
        grad_weight_z=matrix,
        grad_weight_x=matrix,
        grad_weight_dt=((sz.head_rows, sz.half), F32),
        grad_weight_bc=((sz.bc, sz.half), BF16),
        small_sums=((HALO + sz.plane_rows, sz.chan), F32),
        grad_out_weight=matrix,
    )
    scratch = scratch_list(sz)
    scratch["bc_full"] = ((sz.cols, sz.rows, sz.bc_part, sz.half), F32)
    names = [*inputs, *outputs, *scratch, "send_sem", "recv_sem"]
    count = semaphore_count(sz)
    vmem = pl.BlockSpec(memory_space=pltpu.VMEM)
    got = pl.pallas_call(
        functools.partial(block_kernel, sz, names),
        out_shape=[jax.ShapeDtypeStruct(*item) for item in outputs.values()],
        in_specs=[vmem] * len(inputs),
        out_specs=[vmem] * len(outputs),
        scratch_shapes=[pltpu.VMEM(*item) for item in scratch.values()]
        + [pltpu.SemaphoreType.DMA((count,)), pltpu.SemaphoreType.DMA((count,))],
        compiler_params=pltpu.CompilerParams(
            collective_id=0, has_side_effects=True, vmem_limit_bytes=62 << 20
        ),
        name="residual_block",
    )(*inputs.values())
    sent = dict(zip(outputs, got))
    results = dict(
        output=(sz.block, sz.half),
        grad_hidden=(sz.block, sz.half),
        grad_norm_gain=(1, sz.half),
        grad_weight_z=weight_z.shape,
        grad_weight_x=weight_x.shape,
        grad_weight_dt=weight_dt.shape,
        grad_weight_bc=weight_bc.shape,
        grad_conv_weight=conv_weight.shape,
        grad_conv_bias=(1, sz.chan),
        grad_bc_conv_weight=bc_conv_weight.shape,
        grad_bc_conv_bias=(1, sz.bc),
        grad_dt_bias=(1, sz.heads),
        grad_decay_log=(1, sz.heads),
        grad_skip_gain=(1, sz.heads),
        grad_gate_gain=(1, sz.chan),
        grad_out_weight=out_weight.shape,
    )
    got = pl.pallas_call(
        functools.partial(finish_kernel, sz, list(sent), list(results)),
        out_shape=[jax.ShapeDtypeStruct(shape, F32) for shape in results.values()],
        in_specs=[vmem] * len(sent),
        out_specs=[vmem] * len(results),
        compiler_params=pltpu.CompilerParams(vmem_limit_bytes=32 << 20),
        name="write_results",
    )(*sent.values())
    out = dict(zip(results, got))
    for name in ("norm_gain", "conv_bias", "bc_conv_bias", "dt_bias", "decay_log", "skip_gain", "gate_gain"):
        out["grad_" + name] = out["grad_" + name][0]
    return tuple(out.values())


def solution(mesh):
    in_specs = (
        P(("dp", "row"), None),
        P(("dp", "row"), "col"),
        P(),
        P("col", "row"),
        P("col", "row"),
        P("col", "row"),
        P("col", None),
        P(None, ("row", "col")),
        P(("row", "col")),
        P(),
        P(),
        P(("row", "col")),
        P(("row", "col")),
        P(("row", "col")),
        P(("row", "col")),
        P("row", "col"),
    )
    out_specs = (
        P(("dp", "row"), "col"),
        P(("dp", "row"), "col"),
        P("col"),
        P("col", "row"),
        P("col", "row"),
        P("col", "row"),
        P("col", None),
        P(None, ("row", "col")),
        P(("row", "col")),
        P(),
        P(),
        P(("row", "col")),
        P(("row", "col")),
        P(("row", "col")),
        P(("row", "col")),
        P("row", "col"),
    )
    sizes = tuple(mesh.shape[axis] for axis in ("dp", "row", "col"))
    return jax.shard_map(
        functools.partial(body, sizes), mesh=mesh, in_specs=in_specs, out_specs=out_specs, check_vma=False
    )
```

```python
import functools

import jax
import jax.numpy as jnp
from jax import lax
from jax.experimental import pallas as pl
from jax.experimental.pallas import tpu as pltpu
from jax.sharding import PartitionSpec as P

LANES = 128
HALO = 8
TILE = 16
EPSILON = 1e-05
PRECISE = lax.Precision.HIGHEST
F32 = jnp.float32
BF16 = jnp.bfloat16
MESH = pl.DeviceIdType.MESH


def dot_f32(a, b):
    return jnp.dot(a, b, precision=PRECISE, preferred_element_type=F32)


def dot_nn(a, b):
    return lax.dot_general(a, b, (((1,), (0,)), ((), ())), preferred_element_type=F32)


def dot_nt(a, b):
    return lax.dot_general(a, b, (((1,), (1,)), ((), ())), preferred_element_type=F32)


def dot_tn(a, b):
    return lax.dot_general(a, b, (((0,), (0,)), ((), ())), preferred_element_type=F32)


def sigmoid(v):
    return 1.0 / (1.0 + jnp.exp(-v))


def iota(shape, axis):
    return lax.broadcasted_iota(jnp.int32, shape, axis)


def head_spread(chan, head_width):
    head = iota((LANES, chan), 0)
    lane = iota((LANES, chan), 1)
    return ((lane >= head * head_width) & (lane < (head + 1) * head_width)).astype(F32)


class Sizes:
    def __init__(self, mesh_sizes, hidden, weight_z, weight_dt, weight_bc):
        self.n, self.rows, self.cols = mesh_sizes
        self.pair = 2 if self.rows % 2 == 0 else 1
        self.chips = self.rows // self.pair
        self.block, self.model = hidden.shape
        self.half = weight_z.shape[0]
        self.chan = weight_z.shape[1] // self.cols
        self.row_heads = weight_dt.shape[1]
        self.heads = self.row_heads // self.cols
        self.head_width = self.chan // self.heads
        self.bc = weight_bc.shape[1]
        self.state = self.bc // 2
        self.wide = self.chan + self.bc
        self.bc_part = self.bc // self.rows
        self.head_rows = -(-self.row_heads // TILE) * TILE
        assert self.n % 2 == 0
        self.pieces = next(k for k in (4, 2, 1) if self.chan % (k * TILE) == 0)
        self.piece = self.chan // self.pieces
        self.inner = self.chan * self.rows * self.cols
        self.sum_rows = -(-2 * self.rows // 8) * 8
        self.gain_rows = self.model // self.chan
        self.plane_rows = -(-(5 * self.bc // self.chan + self.gain_rows) // 8) * 8


class Links:
    def __init__(self, send_sem, recv_sem):
        self.send_sem, self.recv_sem = send_sem, recv_sem
        self.count = 0
        self.makers = []

    def take(self, many=1):
        first = self.count
        self.count += many
        return first

    def copy(self, src, dst, at, device):
        return pltpu.make_async_remote_copy(
            src_ref=src,
            dst_ref=dst,
            send_sem=self.send_sem.at[at],
            recv_sem=self.recv_sem.at[at],
            device_id=device,
            device_id_type=MESH,
        )

    def send(self, src, dst, at, device, when=None):
        make = lambda: self.copy(src, dst, at, device)
        self.makers.append((make, when))
        if when is None:
            make().start()
        else:
            pl.when(when)(lambda: make().start())

    def arrived(self, dst, at, device):
        self.copy(dst, dst, at, device).wait_recv()

    def drain(self):
        for make, when in self.makers:
            if when is None:
                make().wait_send()
            else:
                pl.when(when)(lambda: make().wait_send())


def semaphore_count(sz):
    group = sz.rows * sz.cols
    units = 3 * 2 * sz.pieces * (1 + sz.cols)
    front = 4 * group + 8 * (sz.chips + 1) * (sz.cols + 1) + 8 * sz.cols
    scatter = 3 * (2 * sz.chips * sz.cols + sz.chips + sz.cols)
    return units + front + scatter + 2 * group + 2 * sz.n + sz.rows + sz.cols + 16


def scratch_list(sz):
    nb, n, rows, cols, chips = sz.rows, sz.n, sz.rows, sz.cols, sz.chips
    blk, half, chan, wide = sz.block, sz.half, sz.chan, sz.wide
    across = max(chips - 1, 1)
    other = max(cols - 1, 1)
    shapes = dict(
        tokens=((rows, blk, sz.model), BF16),
        weights=((cols, half, chan + wide), BF16),
        wdt_in=((cols, sz.head_rows, half), BF16),
        wdt=((cols, LANES, half), BF16),
        cots=((rows, cols, blk, half), BF16),
        outw=((cols, chan, half), BF16),
        inv_rms=((blk, LANES), F32),
        conv=((HALO, wide), F32),
        head=((HALO, LANES), F32),
        ext=((nb, HALO + blk, wide), F32),
        z_raw=((nb, blk, chan), F32),
        pre=((nb, blk, wide), F32),
        gate=((nb, blk, wide), F32),
        step_pre=((nb, blk, LANES), F32),
        log_decay=((nb, blk, LANES), F32),
        step_ch=((nb, blk, chan), F32),
        log_ch=((nb, blk, chan), F32),
        decay=((nb, sz.heads, blk, blk), F32),
        states=((nb, sz.state, chan), F32),
        state=((sz.state, chan), F32),
        mixed=((nb, blk, chan), F32),
        inside=((nb, blk, chan), F32),
        ggo=((nb, blk, chan), F32),
        sums=((rows * cols, sz.sum_rows, blk), F32),
        total=((sz.sum_rows, blk), F32),
        gate_out=((nb, blk, chan), BF16),
        grad_z=((nb, blk, chan), BF16),
        grad_x=((nb, blk, chan), BF16),
        grad_bc=((nb, blk, sz.bc), BF16),
        grad_dt=((nb, blk, LANES), BF16),
        gate_gain=((HALO, chan), F32),
        conv_grad=((HALO, wide), F32),
        head_grad=((HALO, LANES), F32),
        skip_grad=((HALO, chan), F32),
        gain_grad=((HALO, sz.model), F32),
        grad_ext=((blk + HALO, wide), F32),
        grad_state=((sz.state, chan), F32),
        own=((3, sz.pieces, sz.piece, sz.model), BF16),
        landed=((3, sz.pieces, sz.piece, sz.model), BF16),
        across=((3, sz.pieces, sz.piece, sz.model), BF16),
        other_half=((3, sz.pieces, other, sz.piece, half), BF16),
        final=((3, sz.pieces, cols, sz.piece, half), BF16),
        keep=((chips, cols, blk, half), F32),
        keep_bc=((chips, cols, sz.bc_part, half), F32),
        dt_rows=((cols, sz.head_rows, half), F32),
        small=((sz.rows * sz.cols, sz.plane_rows, chan), F32),
        dp_small=((n, HALO + sz.plane_rows, chan), F32),
        dp_bc=((n, sz.bc_part + sz.head_rows, half), BF16),
        bc_all=((rows, sz.bc_part, half), BF16),
        dots=((cols, HALO, blk), F32),
    )
    for name, part, extra in (("out", blk, 0), ("bc", sz.bc_part, sz.head_rows), ("in", blk, 0)):
        shapes[name + "_core"] = ((chips, cols, part, half), BF16)
        shapes[name + "_core_got"] = ((chips, cols, part, half), BF16)
        shapes[name + "_chip"] = ((across, cols, part, half), BF16)
        shapes[name + "_chip_got"] = ((across, cols, part, half), BF16)
        shapes[name + "_col"] = ((other, part + extra, half), BF16)
        shapes[name + "_col_got"] = ((other, part + extra, half), BF16)
    return shapes


class Scatter:
    def __init__(self, sz, links, where, bufs, name, keep):
        self.sz, self.links, self.where = sz, links, where
        self.bufs = {key: bufs[name + "_" + key] for key in ("core", "core_got", "chip", "chip_got", "col", "col_got")}
        self.keep = keep
        self.core_at = links.take(sz.chips)
        self.chip_at = links.take(sz.chips * sz.cols)
        self.col_at = links.take(sz.cols)

    def start(self, block_of):
        sz, (dp, row, col, chip, core) = self.sz, self.where
        if sz.pair == 2:
            for x in range(sz.chips):
                for h in range(sz.cols):
                    self.bufs["core"][x, h] = block_of(x * 2 + 1 - core, h).astype(BF16)
                self.links.send(
                    self.bufs["core"].at[x],
                    self.bufs["core_got"].at[x],
                    self.core_at + x,
                    (dp, chip * 2 + 1 - core, col),
                )
        for x in range(sz.chips):
            for h in range(sz.cols):
                self.keep[x, h] = block_of(x * sz.pair + core, h)

    def held(self, x, h):
        value = self.keep[x, h]
        if self.sz.pair == 2:
            value = value + self.bufs["core_got"][x, h].astype(F32)
        return value

    def across(self):
        sz, (dp, row, col, chip, core) = self.sz, self.where
        if sz.pair == 2:
            for x in range(sz.chips):
                self.links.arrived(self.bufs["core_got"].at[x], self.core_at + x, (dp, chip * 2 + 1 - core, col))
        for k in [*range(1, sz.cols), 0]:
            h = lax.rem(col + k, sz.cols)
            for dx in range(1, sz.chips):
                x = lax.rem(chip + dx, sz.chips)
                self.bufs["chip"][dx - 1, k] = self.held(x, h).astype(BF16)
                self.links.send(
                    self.bufs["chip"].at[dx - 1, k],
                    self.bufs["chip_got"].at[dx - 1, k],
                    self.chip_at + dx * sz.cols + k,
                    (dp, x * sz.pair + core, col),
                )

    def summed(self, k):
        sz, (dp, row, col, chip, core) = self.sz, self.where
        value = self.held(chip, lax.rem(col + k, sz.cols))
        for dx in range(1, sz.chips):
            x = lax.rem(chip + dx, sz.chips)
            self.links.arrived(
                self.bufs["chip_got"].at[dx - 1, k], self.chip_at + dx * sz.cols + k, (dp, x * sz.pair + core, col)
            )
            value = value + self.bufs["chip_got"][dx - 1, k].astype(F32)
        return value

    def turn(self, extra=None):
        sz, (dp, row, col, chip, core) = self.sz, self.where
        for k in range(1, sz.cols):
            h = lax.rem(col + k, sz.cols)
            value = self.summed(k)
            part = value.shape[0]
            self.bufs["col"][k - 1, 0:part, :] = value.astype(BF16)
            if extra is not None:
                more = extra(h)
                self.bufs["col"][k - 1, part : part + more.shape[0], :] = more.astype(BF16)
            self.links.send(
                self.bufs["col"].at[k - 1], self.bufs["col_got"].at[k - 1], self.col_at + k, (dp, row, h)
            )

    def finish(self, extra=None):
        sz, (dp, row, col, chip, core) = self.sz, self.where
        value = self.summed(0)
        more = None if extra is None else extra(col)
        part = value.shape[0]
        for k in range(1, sz.cols):
            h = lax.rem(col + k, sz.cols)
            self.links.arrived(self.bufs["col_got"].at[k - 1], self.col_at + k, (dp, row, h))
            value = value + self.bufs["col_got"][k - 1, 0:part, :].astype(F32)
            if more is not None:
                more = more + self.bufs["col_got"][k - 1, part:, :].astype(F32)
        return value, more


class Line:
    def __init__(self, sz, links, where, bufs, part):
        self.sz, self.links, self.where = sz, links, where
        self.own, self.landed, self.across = (bufs[key].at[part] for key in ("own", "landed", "across"))
        self.other_half, self.final = bufs["other_half"].at[part], bufs["final"].at[part]
        self.in_at, self.mid_at = links.take(sz.pieces), links.take(sz.pieces)
        self.col_at, self.out_at = links.take(sz.pieces * sz.cols), links.take(sz.pieces * sz.cols)
        dp, last = where[0], sz.n - 1
        low = dp < sz.n // 2
        self.middle = sz.n // 2 - 1
        self.place = jnp.where(low, dp, last - dp)
        self.inward = jnp.where(low, dp + 1, dp - 1)
        self.outward = jnp.clip(jnp.where(low, dp - 1, dp + 1), 0, last)

    def in_copy(self, g):
        target = (self.inward, *self.where[1:3])
        return self.links.copy(self.own.at[g], self.landed.at[g], self.in_at + g, target)

    def mid_copy(self, g):
        target = (self.inward, *self.where[1:3])
        return self.links.copy(self.own.at[g], self.across.at[g], self.mid_at + g, target)

    def half_copy(self, g, k, out):
        sz, (dp, row, col) = self.sz, self.where[:3]
        source = self.final.at[g, col] if k == 0 else self.other_half.at[g, k - 1]
        at = (self.out_at if out else self.col_at) + g * sz.cols + k
        target = (self.outward if out else dp, row, lax.rem(col + k, sz.cols))
        return self.links.copy(source, self.final.at[g, col], at, target)

    def pass_copy(self, g, k, device):
        sz, (dp, row, col) = self.sz, self.where[:3]
        ref = self.final.at[g, lax.rem(col + sz.cols - k, sz.cols)]
        return self.links.copy(ref, ref, self.out_at + g * sz.cols + k, (device, row, col))

    def source(self, g):
        if self.middle > 0:
            pl.when(self.place == 0)(lambda: self.in_copy(g).start())

    def fold(self, g):
        self.in_copy(g).wait_recv()
        self.own[g] = (self.own[g].astype(F32) + self.landed[g].astype(F32)).astype(BF16)

    def enter(self, g):
        if self.middle > 0:
            pl.when(self.place > 0)(lambda: self.fold(g))
        if self.middle > 1:
            pl.when((self.place > 0) & (self.place < self.middle))(lambda: self.in_copy(g).start())
        pl.when(self.place == self.middle)(lambda: self.mid_copy(g).start())

    def meet(self, g):
        sz, col = self.sz, self.where[2]
        self.mid_copy(g).wait()
        self.own[g] = (self.own[g].astype(F32) + self.across[g].astype(F32)).astype(BF16)
        for k in range(sz.cols):
            h = lax.rem(col + k, sz.cols)
            half = self.own[g, :, pl.ds(pl.multiple_of(h * sz.half, LANES), sz.half)]
            if k == 0:
                self.final[g, col] = half
            else:
                self.other_half[g, k - 1] = half
            if self.middle > 0:
                self.half_copy(g, k, True).start()
            if k > 0:
                self.half_copy(g, k, False).start()

    def cross(self, g):
        pl.when(self.place == self.middle)(lambda: self.meet(g))

    def from_columns(self, g):
        sz, (dp, row, col) = self.sz, self.where[:3]
        for k in range(1, sz.cols):
            h = lax.rem(col + sz.cols - k, sz.cols)
            self.links.arrived(self.final.at[g, h], self.col_at + g * sz.cols + k, (dp, row, h))

    def from_inward(self, g):
        for k in range(self.sz.cols):
            self.pass_copy(g, k, self.inward).wait_recv()

    def pass_on(self, g):
        for k in range(self.sz.cols):
            self.pass_copy(g, k, self.outward).start()

    def leave(self, g):
        pl.when(self.place == self.middle)(lambda: self.from_columns(g))
        if self.middle > 0:
            pl.when(self.place < self.middle)(lambda: self.from_inward(g))
        if self.middle > 1:
            pl.when((self.place > 0) & (self.place < self.middle))(lambda: self.pass_on(g))

    def sent_halves(self, g):
        for k in range(self.sz.cols):
            if self.middle > 0:
                self.half_copy(g, k, True).wait_send()
            if k > 0:
                self.half_copy(g, k, False).wait_send()

    def sent_on(self, g):
        for k in range(self.sz.cols):
            self.pass_copy(g, k, self.outward).wait_send()

    def drain(self):
        for g in range(self.sz.pieces):
            if self.middle > 0:
                pl.when(self.place < self.middle)(lambda: self.in_copy(g).wait_send())
            pl.when(self.place == self.middle)(lambda: self.sent_halves(g))
            if self.middle > 1:
                pl.when((self.place > 0) & (self.place < self.middle))(lambda: self.sent_on(g))


def forward_block(sz, m, b):
    blk, chan, wide, half = sz.block, sz.chan, sz.wide, sz.half
    acc = jnp.zeros((blk, chan + wide), F32)
    step_raw = jnp.zeros((blk, LANES), F32)
    for h in range(sz.cols):
        part = m.tokens[b, :, h * half : (h + 1) * half]
        acc = acc + dot_nn(part, m.weights[h])
        step_raw = step_raw + dot_nt(part, m.wdt[h])
    z_raw = acc[:, :chan]
    m.z_raw[b] = z_raw
    m.ext[b, HALO : HALO + blk, :] = acc[:, chan:]

    @pl.when(b + 1 < sz.rows)
    def _():
        m.ext[b + 1, 0:HALO, :] = m.ext[b, blk : blk + HALO, :]

    pre = m.conv[4:5, :]
    for tap in range(4):
        first = HALO - 3 + tap
        pre = pre + m.conv[tap : tap + 1, :] * m.ext[b, first : first + blk, :]
    gate = sigmoid(pre)
    m.pre[b] = pre
    m.gate[b] = gate
    conv = pre * gate
    step_pre = step_raw + m.head[0:1, :]
    m.step_pre[b] = step_pre
    step = jnp.maximum(step_pre, 0.0) + jnp.log1p(jnp.exp(-jnp.abs(step_pre)))
    rate = -jnp.exp(m.head[1:2, :])
    causal = iota((blk, blk), 0) >= iota((blk, blk), 1)
    log_decay = dot_f32(causal.astype(F32), step * rate)
    m.log_decay[b] = log_decay
    spread = head_spread(chan, sz.head_width)
    step_ch = dot_f32(step, spread)
    log_ch = dot_f32(log_decay, spread)
    m.step_ch[b] = step_ch
    m.log_ch[b] = log_ch
    skip_ch = dot_f32(jnp.broadcast_to(m.head[2:3, :], (HALO, LANES)), spread)[0:1, :]

    x_conv = conv[:, :chan]
    b_half = conv[:, chan : chan + sz.state].astype(BF16)
    c_half = conv[:, chan + sz.state :].astype(BF16)
    stepped = x_conv * step_ch
    scores = dot_nt(c_half, b_half)
    log_rows = log_decay.T
    lane = iota((blk, chan), 1)
    inside = jnp.zeros((blk, chan), F32)
    for head in range(sz.heads):
        gap = log_decay[:, head : head + 1] - log_rows[head : head + 1, :]
        decay = jnp.exp(jnp.where(causal, gap, -1e30))
        m.decay[b, head] = decay
        mixing = (scores * decay).astype(BF16)
        mine = (lane >= head * sz.head_width) & (lane < (head + 1) * sz.head_width)
        inside = inside + dot_nn(mixing, jnp.where(mine, stepped, 0.0).astype(BF16))
    entering = m.state[...]
    m.states[b] = entering
    outside = dot_nn(c_half, entering.astype(BF16)) * jnp.exp(log_ch)
    mixed = inside + outside + skip_ch * x_conv
    last = log_ch[blk - 1 : blk, :]
    tail = stepped * jnp.exp(last - log_ch)
    m.state[...] = entering * jnp.exp(last) + dot_tn(b_half, tail.astype(BF16))
    m.mixed[b] = mixed
    m.inside[b] = inside


def backward_block(sz, m, b, shift):
    blk, chan, wide = sz.block, sz.chan, sz.wide
    pre = m.pre[b]
    gate = m.gate[b]
    conv = pre * gate
    step_pre = m.step_pre[b]
    step = jnp.maximum(step_pre, 0.0) + jnp.log1p(jnp.exp(-jnp.abs(step_pre)))
    rate = -jnp.exp(m.head[1:2, :])
    step_ch = m.step_ch[b]
    log_ch = m.log_ch[b]
    spread = head_spread(chan, sz.head_width)
    skip_ch = dot_f32(jnp.broadcast_to(m.head[2:3, :], (HALO, LANES)), spread)[0:1, :]
    x_conv = conv[:, :chan]
    b_half = conv[:, chan : chan + sz.state].astype(BF16)
    c_half = conv[:, chan + sz.state :].astype(BF16)
    stepped = x_conv * step_ch
    stepped_half = stepped.astype(BF16)
    grad_mixed = m.ggo[b]
    grad_half = grad_mixed.astype(BF16)
    inside = m.inside[b]
    outside = m.mixed[b] - inside - skip_ch * x_conv

    scores = dot_nt(c_half, b_half)
    lane = iota((blk, chan), 1)
    grad_scores = jnp.zeros((blk, blk), F32)
    grad_inner = jnp.zeros((blk, chan), F32)
    for head in range(sz.heads):
        decay = m.decay[b, head]
        mixing = (scores * decay).astype(BF16)
        mine = (lane >= head * sz.head_width) & (lane < (head + 1) * sz.head_width)
        grad_mine = jnp.where(mine, grad_mixed, 0.0).astype(BF16)
        grad_scores = grad_scores + dot_nt(grad_mine, stepped_half) * decay
        grad_inner = grad_inner + dot_tn(mixing, grad_mine)
    scores_half = grad_scores.astype(BF16)

    entering = m.states[b]
    left = m.grad_state[...]
    left_half = left.astype(BF16)
    grad_outer = (grad_mixed * jnp.exp(log_ch)).astype(BF16)
    last = log_ch[blk - 1 : blk, :]
    fade = jnp.exp(last - log_ch)
    tail = stepped * fade
    grad_tail = dot_nn(b_half, left_half)
    tail_term = tail * grad_tail
    grad_c = dot_nt(grad_outer, entering.astype(BF16)) + dot_nn(scores_half, b_half)
    grad_b = dot_nt(tail.astype(BF16), left_half) + dot_tn(scores_half, c_half)
    grad_last = jnp.sum(tail_term, axis=0, keepdims=True) + jnp.exp(last) * jnp.sum(
        left * entering, axis=0, keepdims=True
    )
    m.grad_state[...] = left * jnp.exp(last) + dot_tn(c_half, grad_outer)

    grad_stepped = grad_inner + grad_tail * fade
    log_term = (
        grad_half.astype(F32) * inside
        + grad_mixed * outside
        - stepped_half.astype(F32) * grad_inner
        - tail_term
    )
    row = iota((blk, chan), 0)
    log_term = log_term + jnp.where(row == blk - 1, grad_last, 0.0)

    def per_head(values):
        return lax.dot_general(
            values, spread, (((1,), (1,)), ((), ())), precision=PRECISE, preferred_element_type=F32
        )

    later = (iota((blk, blk), 0) <= iota((blk, blk), 1)).astype(F32)
    grad_rate_step = dot_f32(later, per_head(log_term))
    grad_step = per_head(grad_stepped * x_conv) + grad_rate_step * rate
    grad_step_raw = grad_step * sigmoid(step_pre)
    m.head_grad[0:1, :] += jnp.sum(grad_step_raw, axis=0, keepdims=True)
    m.head_grad[1:2, :] += jnp.sum(grad_rate_step * step, axis=0, keepdims=True) * rate
    m.skip_grad[0:1, :] += jnp.sum(grad_mixed * x_conv, axis=0, keepdims=True)

    grad_x = grad_stepped * step_ch + grad_mixed * skip_ch
    slope = gate * (1.0 + pre * (1.0 - gate))
    m.grad_ext[blk : blk + HALO, :] = m.grad_ext[0:HALO, :]
    m.grad_ext[0:blk, 0:chan] = grad_x * slope[:, :chan]
    m.grad_ext[0:blk, chan : chan + sz.state] = grad_b * slope[:, chan : chan + sz.state]
    m.grad_ext[0:blk, chan + sz.state :] = grad_c * slope[:, chan + sz.state :]
    grad_pre = m.grad_ext[0:blk, :]
    grad_raw = jnp.zeros((blk, wide), F32)
    for tap in range(4):
        grad_raw = grad_raw + m.conv[tap : tap + 1, :] * m.grad_ext[3 - tap : 3 - tap + blk, :]
        first = HALO - 3 + tap
        m.conv_grad[tap : tap + 1, :] += jnp.sum(
            grad_pre * m.ext[b, first : first + blk, :], axis=0, keepdims=True
        )
    m.conv_grad[4:5, :] += jnp.sum(grad_pre, axis=0, keepdims=True)
    m.grad_x[b] = grad_raw[:, :chan].astype(BF16)
    m.grad_bc[b] = grad_raw[:, chan:].astype(BF16)
    m.grad_dt[b] = dot_nn(grad_step_raw.astype(BF16), shift).astype(BF16)


class Refs:
    pass


def block_kernel(sz, names, *refs):
    m = Refs()
    for name, ref in zip(names, refs):
        setattr(m, name, ref)
    bufs = m.__dict__
    nb, rows, cols, chips, pair = sz.rows, sz.rows, sz.cols, sz.chips, sz.pair
    blk, half, chan, wide, n = sz.block, sz.half, sz.chan, sz.wide, sz.n
    dp, row, col = lax.axis_index("dp"), lax.axis_index("row"), lax.axis_index("col")
    chip, core = row // pair, lax.rem(row, pair)
    where = (dp, row, col, chip, core)
    group = rows * cols
    mine = row * cols + col
    sibling = (dp, chip * pair + lax.rem(core + 1, pair), col)
    sibling_core = lax.rem(core + 1, pair)

    def plane_peer(k):
        return dp, lax.rem(row + k // cols, rows), lax.rem(col + k % cols, cols)

    def line_peer(k):
        return lax.rem(dp + k, n), row, col

    def col_peer(k):
        return dp, row, lax.rem(col + k, cols)

    def chip_peer(dx):
        return dp, lax.rem(chip + dx, chips) * pair + core, col

    def from_chip(dx):
        return lax.rem(chip + chips - dx, chips) * pair + core

    def from_sibling(dx):
        return lax.rem(chip + chips - dx, chips) * pair + sibling_core

    def from_col(k):
        return lax.rem(col + cols - k, cols)

    links = Links(m.send_sem, m.recv_sem)
    barrier = pltpu.get_barrier_semaphore()
    peers = [plane_peer(k) for k in range(1, group)] + [line_peer(k) for k in range(1, n)]
    for peer in peers:
        pl.semaphore_signal(barrier, inc=1, device_id=peer, device_id_type=MESH)

    def lanes(start, size):
        return pl.ds(pl.multiple_of(start * size, LANES), size)

    hidden = m.hidden[...]
    inv_rms = lax.rsqrt(jnp.mean(hidden * hidden, axis=1, keepdims=True) + EPSILON)
    m.inv_rms[...] = jnp.broadcast_to(inv_rms, (blk, LANES))
    m.tokens[row] = (hidden * inv_rms * m.norm_gain[...]).astype(BF16)
    m.cots[row, col] = m.cotangent[...].astype(BF16)
    steps_in = m.weight_dt[...].astype(F32)
    if sz.head_rows > sz.row_heads:
        steps_in = jnp.concatenate([steps_in, jnp.zeros((sz.head_rows - sz.row_heads, half), F32)], axis=0)
    m.wdt_in[col] = steps_in.astype(BF16)

    pl.semaphore_wait(barrier, len(peers))

    w_at, bc_at, dt_at, bc_fwd = links.take(2 * cols), links.take(cols), links.take(cols), links.take(cols)
    tok_x, tok_s = links.take(chips), links.take(chips)
    cot_y, cot_x, cot_s = links.take(cols), links.take(chips * cols), links.take(chips * cols)
    out_at = links.take(cols)
    bc_rows = half // pair
    bc_mine = pl.ds(pl.multiple_of(core * bc_rows, TILE), bc_rows)
    bc_sib = pl.ds(pl.multiple_of(sibling_core * bc_rows, TILE), bc_rows)
    bc_lanes = pl.ds(2 * chan, sz.bc)
    for k in range(1, cols):
        peer = col_peer(k)
        links.send(
            m.weight_z.at[:, lanes(peer[2], chan)], m.weights.at[col, :, pl.ds(0, chan)], w_at + 2 * k, peer
        )
        links.send(
            m.weight_x.at[:, lanes(peer[2], chan)], m.weights.at[col, :, pl.ds(chan, chan)], w_at + 2 * k + 1, peer
        )
        links.send(m.weight_bc.at[bc_mine, :], m.weights.at[col, bc_mine, bc_lanes], bc_at + k, peer)
        links.send(m.wdt_in.at[col], m.wdt_in.at[col], dt_at + k, peer)
    for dx in range(1, chips):
        links.send(m.tokens.at[row], m.tokens.at[row], tok_x + dx, chip_peer(dx))
    if pair == 2:
        links.send(m.tokens.at[row], m.tokens.at[row], tok_s, sibling)

    m.weights[col, :, 0:chan] = m.weight_z[:, lanes(col, chan)]
    m.weights[col, :, chan : 2 * chan] = m.weight_x[:, lanes(col, chan)]
    m.weights[col, :, 2 * chan :] = m.weight_bc[...]
    m.outw[col] = m.out_weight[pl.ds(pl.multiple_of(col * chan, TILE), chan), :]
    for ref in (m.conv, m.head, m.state, m.grad_state, m.grad_ext, m.gate_gain, m.conv_grad, m.head_grad):
        ref[...] = jnp.zeros_like(ref)
    for ref in (m.skip_grad, m.gain_grad):
        ref[...] = jnp.zeros_like(ref)
    m.ext[0, 0:HALO, :] = jnp.zeros((HALO, wide), F32)
    m.conv[0:4, 0:chan] = m.conv_weight[...]
    m.conv[0:4, chan:] = m.bc_conv_weight[...]
    m.conv[4:5, 0:chan] = m.conv_bias[...]
    m.conv[4:5, chan:] = m.bc_conv_bias[...]
    m.head[0:1, 0 : sz.heads] = m.dt_bias[...]
    m.head[1:2, 0 : sz.heads] = m.decay_log[...]
    m.head[2:3, 0 : sz.heads] = m.skip_gain[...]

    def send_cots(dx, k, r, c):
        if dx == 0:
            for far in range(1, chips):
                links.send(m.cots.at[r, c], m.cots.at[r, c], cot_x + far * cols + k, chip_peer(far))
        if pair == 2:
            links.send(m.cots.at[r, c], m.cots.at[r, c], cot_s + dx * cols + k, sibling)

    for dx in range(1, chips):
        links.arrived(m.tokens.at[from_chip(dx)], tok_x + dx, chip_peer(dx))
        if pair == 2:
            links.send(m.tokens.at[from_chip(dx)], m.tokens.at[from_chip(dx)], tok_s + dx, sibling)
    send_cots(0, 0, row, col)
    for k in range(1, cols):
        peer, src = col_peer(k), from_col(k)
        links.arrived(m.weights.at[src, :, pl.ds(0, chan)], w_at + 2 * k, peer)
        links.arrived(m.weights.at[src, :, pl.ds(chan, chan)], w_at + 2 * k + 1, peer)
        links.arrived(m.weights.at[src, bc_mine, bc_lanes], bc_at + k, peer)
        if pair == 2:
            links.send(
                m.weights.at[src, bc_mine, bc_lanes], m.weights.at[src, bc_mine, bc_lanes], bc_fwd + k, sibling
            )
        links.arrived(m.wdt_in.at[src], dt_at + k, peer)
        links.send(m.cots.at[row, col], m.cots.at[row, col], cot_y + k, peer)
        links.send(
            m.out_weight.at[pl.ds(pl.multiple_of(peer[2] * chan, TILE), chan), :], m.outw.at[col], out_at + k, peer
        )

    head_at, head_to = iota((LANES, LANES), 0), iota((LANES, LANES), 1)
    shift = ((head_to == head_at + col * sz.heads) & (head_at < sz.heads)).astype(BF16)
    for h in range(cols):
        padded = jnp.concatenate([m.wdt_in[h], jnp.zeros((LANES - sz.head_rows, half), BF16)], axis=0)
        m.wdt[h] = dot_nn(shift, padded).astype(BF16)

    if pair == 2:
        for dx in range(chips):
            links.arrived(m.tokens.at[from_sibling(dx)], tok_s + dx, sibling)
        for k in range(1, cols):
            links.arrived(m.weights.at[from_col(k), bc_sib, bc_lanes], bc_fwd + k, sibling)

    def pass_col_cots():
        for k in range(1, cols):
            links.arrived(m.cots.at[row, from_col(k)], cot_y + k, col_peer(k))

    def pass_chip_cots(k):
        for dx in range(1, chips):
            r, c = from_chip(dx), from_col(k)
            links.arrived(m.cots.at[r, c], cot_x + dx * cols + k, chip_peer(dx))

    def forward_step(b, carry):
        forward_block(sz, m, b)
        return carry

    early = min(2, nb)
    lax.fori_loop(0, early, forward_step, 0)
    pass_col_cots()
    for k in range(1, cols):
        send_cots(0, k, row, from_col(k))
    pass_chip_cots(0)
    for dx in range(1, chips):
        send_cots(dx, 0, from_chip(dx), col)
    lax.fori_loop(early, nb, forward_step, 0)
    for k in range(1, cols):
        pass_chip_cots(k)
        for dx in range(1, chips):
            send_cots(dx, k, from_chip(dx), from_col(k))
    for k in range(1, cols):
        links.arrived(m.outw.at[from_col(k)], out_at + k, col_peer(k))
    if pair == 2:
        for dx in range(chips):
            for k in range(cols):
                links.arrived(m.cots.at[from_sibling(dx), from_col(k)], cot_s + dx * cols + k, sibling)

    sub = iota((LANES, blk), 0)
    m.sums[mine] = jnp.zeros((sz.sum_rows, blk), F32)

    def sum_step(b, carry):
        ggo = jnp.zeros((blk, chan), F32)
        for h in range(cols):
            ggo = ggo + dot_nt(m.cots[b, h], m.outw[h])
        m.ggo[b] = ggo
        z_raw = m.z_raw[b]
        gated = m.mixed[b] * (z_raw * sigmoid(z_raw))
        squares = jnp.sum(gated * gated, axis=1, keepdims=True)
        inner = jnp.sum(ggo * m.gate_gain_in[...] * gated, axis=1, keepdims=True)
        lane = iota((blk, LANES), 1)
        both = jnp.where(lane == 0, squares, jnp.where(lane == 1, inner, 0.0)).T
        m.sums[mine, pl.ds(b, 1), :] = both[0:1, :]
        m.sums[mine, pl.ds(nb + b, 1), :] = both[1:2, :]
        return carry

    lax.fori_loop(0, nb, sum_step, 0)

    def to_plane(ref):
        at = links.take(group)
        for k in range(1, group):
            links.send(ref.at[mine], ref.at[mine], at + k, plane_peer(k))
        return at

    def from_plane(ref, at):
        for k in range(1, group):
            r, c = lax.rem(row + rows - k // cols, rows), lax.rem(col + cols - k % cols, cols)
            links.arrived(ref.at[r * cols + c], at + k, plane_peer(k))
        value = ref[0]
        for k in range(1, group):
            value = value + ref[k]
        return value

    m.total[...] = from_plane(m.sums, to_plane(m.sums))

    def gate_step(b, carry):
        first = m.total[pl.ds(b, 1), :]
        second = m.total[pl.ds(nb + b, 1), :]
        both = jnp.where(sub == 0, first, jnp.where(sub == 1, second, 0.0)).T
        inv_gate = lax.rsqrt(both[:, 0:1] / sz.inner + EPSILON)
        gate_dot = both[:, 1:2] * inv_gate
        ggo = m.ggo[b]
        gate_gain = m.gate_gain_in[...]
        z_raw = m.z_raw[b]
        z_gate = sigmoid(z_raw)
        mixed = m.mixed[b]
        gate_hat = mixed * (z_raw * z_gate) * inv_gate
        grad_gated = inv_gate * (ggo * gate_gain - gate_hat * (gate_dot / sz.inner))
        m.grad_z[b] = (grad_gated * mixed * (z_gate * (1.0 + z_raw * (1.0 - z_gate)))).astype(BF16)
        m.gate_out[b] = (gate_hat * gate_gain).astype(BF16)
        m.gate_gain[0:1, :] += jnp.sum(ggo * gate_hat, axis=0, keepdims=True)
        m.ggo[b] = grad_gated * (z_raw * z_gate)
        return carry

    lax.fori_loop(0, nb, gate_step, 0)

    def flat(ref):
        value = ref[...]
        return value.reshape(value.shape[0] * value.shape[1], value.shape[2])

    lines = [Line(sz, links, where, bufs, part) for part in range(3)]
    order = [(line, g) for line in lines for g in range(sz.pieces)]

    def stage(i):
        for back, name in ((0, "enter"), (2, "cross"), (4, "leave")):
            if 0 <= i - back < len(order):
                line, g = order[i - back]
                getattr(line, name)(g)

    stages = [functools.partial(stage, i) for i in range(len(order) + 4)]

    def advance(many=1, keep=0):
        for _ in range(many):
            if len(stages) > keep:
                stages.pop(0)()

    def sources(part, first, last):
        for g in range(sz.pieces):
            if first <= g * 4 // sz.pieces < last:
                lines[part].source(g)

    def collect(part, ref):
        for c in range(cols):
            for i in range(sz.pieces):
                at = c * chan + i * sz.piece
                ref[at : at + sz.piece, :] = m.final[part, i, c]

    def weight_part(part, grads, operand_of):
        for h in range(cols):
            value = dot_tn(grads, operand_of(h)).astype(BF16)
            m.own[part, :, :, h * half : (h + 1) * half] = value.reshape(sz.pieces, sz.piece, half)

    def cots_of(h):
        return m.cots[:, h].reshape(rows * blk, half)

    def tokens_of(h):
        return m.tokens[:, :, h * half : (h + 1) * half].reshape(rows * blk, half)

    weight_part(0, flat(m.gate_out), cots_of)
    sources(0, 0, 2)
    weight_part(1, flat(m.grad_z), tokens_of)
    sources(0, 2, 4)
    out_sum = Scatter(sz, links, where, bufs, "out", m.keep)
    out_sum.start(lambda r, h: dot_nn(m.gate_out[r], m.outw[h]))
    sources(1, 0, 2)

    def backward_step(i, carry):
        backward_block(sz, m, nb - 1 - i, shift)
        return carry

    before_x = sz.pieces + 4
    services = [
        [lambda: advance(1, before_x), lambda: sources(1, 2, 4), out_sum.across],
        [lambda: advance(1, before_x)],
        [lambda: advance(1, before_x)],
        [],
    ]
    done = 0
    for i, service in enumerate(services):
        until = nb if i == len(services) - 1 else min(nb, done + max(nb // 4, 1))
        lax.fori_loop(done, until, backward_step, 0)
        done = until
        for step in service:
            step()

    weight_part(2, flat(m.grad_x), tokens_of)
    sources(2, 0, 4)
    advance()
    out_sum.turn()
    dt_grads = flat(m.grad_dt)
    for h in range(cols):
        part = dot_tn(flat(m.grad_bc), tokens_of(h))
        m.bc_full[h] = part.reshape(rows, sz.bc_part, half)
        m.dt_rows[h] = dot_tn(dt_grads, tokens_of(h))[0 : sz.head_rows, :]
    bc_sum = Scatter(sz, links, where, bufs, "bc", m.keep_bc)
    bc_sum.start(lambda r, h: m.bc_full[h, r])
    advance()
    total, _ = out_sum.finish()
    m.output[...] = m.hidden[:, lanes(col, half)] + total

    def grad_block(r, h):
        w = m.weights.at[h]
        value = dot_nt(m.grad_z[r], w[:, 0:chan])
        value = value + dot_nt(m.grad_x[r], w[:, chan : 2 * chan])
        value = value + dot_nt(m.grad_bc[r], w[:, 2 * chan :])
        padded = jnp.concatenate([m.wdt_in[h], jnp.zeros((LANES - sz.head_rows, half), BF16)], axis=0)
        value = value + dot_nn(m.grad_dt[r], padded)
        at = slice(h * half, (h + 1) * half)
        m.gain_grad[0:1, at] += jnp.sum(value * m.tokens[r, :, at].astype(F32), axis=0, keepdims=True)
        return value

    in_sum = Scatter(sz, links, where, bufs, "in", m.keep)
    bc_sum.across()
    advance()
    in_sum.start(grad_block)
    advance()

    m.small[mine] = jnp.zeros((sz.plane_rows, chan), F32)
    per_row = sz.bc // chan
    for j in range(5):
        for p in range(per_row):
            at = chan + p * chan
            m.small[mine, j * per_row + p : j * per_row + p + 1, :] = m.conv_grad[j : j + 1, at : at + chan]
    for j in range(sz.gain_rows):
        at = 5 * per_row + j
        m.small[mine, at : at + 1, :] = m.gain_grad[0:1, j * chan : (j + 1) * chan]
    small_at = to_plane(m.small)
    in_sum.across()
    advance()
    dt_of = lambda h: m.dt_rows[h]
    bc_sum.turn(dt_of)
    advance()
    spread = head_spread(chan, sz.head_width)
    skip_heads = lax.dot_general(
        m.skip_grad[...], spread, (((1,), (1,)), ((), ())), precision=PRECISE, preferred_element_type=F32
    )
    m.dp_small[dp] = jnp.zeros((HALO + sz.plane_rows, chan), F32)
    m.dp_small[dp, 0:5, :] = m.conv_grad[0:5, 0:chan]
    m.dp_small[dp, 5:6, :] = m.gate_gain[0:1, :]
    m.dp_small[dp, 6:7, 0:LANES] = m.head_grad[0:1, :]
    m.dp_small[dp, 6:7, LANES : 2 * LANES] = m.head_grad[1:2, :]
    m.dp_small[dp, 7:8, 0:LANES] = skip_heads[0:1, :]
    m.dp_small[dp, HALO:, :] = from_plane(m.small, small_at)

    def to_line(ref):
        at = links.take(n)
        for k in range(1, n):
            links.send(ref.at[dp], ref.at[dp], at + k, line_peer(k))
        return at

    def from_line(ref, at):
        for k in range(1, n):
            links.arrived(ref.at[lax.rem(dp + n - k, n)], at + k, line_peer(k))
        value = ref[0].astype(F32)
        for k in range(1, n):
            value = value + ref[k].astype(F32)
        return value

    small_line = to_line(m.dp_small)
    bc_value, dt_value = bc_sum.finish(dt_of)
    m.dp_bc[dp, 0 : sz.bc_part, :] = bc_value.astype(BF16)
    m.dp_bc[dp, sz.bc_part :, :] = dt_value.astype(BF16)
    bc_line = to_line(m.dp_bc)
    advance()
    in_sum.turn()
    advance()

    bc_total = from_line(m.dp_bc, bc_line)
    m.grad_weight_dt[...] = bc_total[sz.bc_part :, :]
    m.bc_all[row] = bc_total[0 : sz.bc_part, :].astype(BF16)
    row_at = links.take(rows)
    for k in range(1, rows):
        links.send(m.bc_all.at[row], m.bc_all.at[row], row_at + k, (dp, lax.rem(row + k, rows), col))

    grad_scaled, _ = in_sum.finish()
    inv_wide = m.inv_rms[:, 0:1]
    normed = m.hidden[:, lanes(col, half)] * inv_wide
    grad_in = grad_scaled * m.norm_gain[:, lanes(col, half)]
    dot = jnp.sum(grad_in * normed, axis=1, keepdims=True)
    lane = iota((blk, LANES), 1)
    m.dots[col] = jnp.where(lane == 0, dot, 0.0).T[0:HALO, :]
    dot_at = links.take(cols)
    for k in range(1, cols):
        links.send(m.dots.at[col], m.dots.at[col], dot_at + k, col_peer(k))
    advance()
    advance(1, 3)
    collect(0, m.grad_out_weight)
    collect(1, m.grad_weight_z)
    for k in range(1, cols):
        links.arrived(m.dots.at[from_col(k)], dot_at + k, col_peer(k))
    dots = m.dots[0]
    for k in range(1, cols):
        dots = dots + m.dots[k]
    full = jnp.concatenate([dots, jnp.zeros((LANES - HALO, blk), F32)], axis=0).T
    m.grad_hidden[...] = m.cotangent[...] + inv_wide * (grad_in - normed * (full[:, 0:1] / sz.model))

    summed = from_line(m.dp_small, small_line)
    m.small_sums[...] = summed
    per_half = half // chan
    for j in range(per_half):
        at = HALO + 5 * per_row
        line = jnp.zeros((1, chan), F32)
        for c in range(cols):
            here = summed[at + c * per_half + j : at + c * per_half + j + 1, :]
            line = jnp.where(col == c, here, line)
        gain = m.norm_gain[:, pl.ds(pl.multiple_of(col * half + j * chan, LANES), chan)]
        m.grad_norm_gain[:, j * chan : (j + 1) * chan] = line / gain

    for k in range(1, rows):
        at = lax.rem(row + rows - k, rows)
        links.arrived(m.bc_all.at[at], row_at + k, (dp, lax.rem(row + k, rows), col))
    m.grad_weight_bc[...] = flat(m.bc_all)
    advance(len(stages))
    collect(2, m.grad_weight_x)
    links.drain()
    for line in lines:
        line.drain()


def finish_kernel(sz, sent, results, *refs):
    i, o = Refs(), Refs()
    for name, ref in zip(sent, refs):
        setattr(i, name, ref)
    for name, ref in zip(results, refs[len(sent) :]):
        setattr(o, name, ref)
    chan = sz.chan
    per_row = sz.bc // chan
    for name in ("output", "grad_hidden", "grad_norm_gain"):
        getattr(o, name)[...] = getattr(i, name)[...]
    o.grad_out_weight[...] = i.grad_out_weight[...].astype(F32)
    for name in ("grad_weight_z", "grad_weight_x", "grad_weight_bc"):
        getattr(o, name)[...] = getattr(i, name)[...].astype(F32).T
    o.grad_weight_dt[...] = i.grad_weight_dt[0 : sz.row_heads, :]
    o.grad_conv_weight[...] = i.small_sums[0:4, :]
    o.grad_conv_bias[...] = i.small_sums[4:5, :]
    o.grad_gate_gain[...] = i.small_sums[5:6, :]
    o.grad_dt_bias[...] = i.small_sums[6:7, 0 : sz.heads]
    o.grad_decay_log[...] = i.small_sums[6:7, LANES : LANES + sz.heads]
    o.grad_skip_gain[...] = i.small_sums[7:8, 0 : sz.heads]
    for j in range(5):
        for p in range(per_row):
            at = HALO + j * per_row + p
            lanes = slice(p * chan, (p + 1) * chan)
            if j < 4:
                o.grad_bc_conv_weight[j : j + 1, lanes] = i.small_sums[at : at + 1, :]
            else:
                o.grad_bc_conv_bias[:, lanes] = i.small_sums[at : at + 1, :]


def body(
    mesh_sizes,
    hidden,
    cotangent,
    norm_gain,
    weight_z,
    weight_x,
    weight_dt,
    weight_bc,
    conv_weight,
    conv_bias,
    bc_conv_weight,
    bc_conv_bias,
    dt_bias,
    decay_log,
    skip_gain,
    gate_gain,
    out_weight,
):
    sz = Sizes(mesh_sizes, hidden, weight_z, weight_dt, weight_bc)
    line = lambda vector: vector[None, :]
    inputs = dict(
        hidden=hidden,
        cotangent=cotangent,
        norm_gain=line(norm_gain),
        weight_z=weight_z,
        weight_x=weight_x,
        weight_dt=weight_dt.T,
        weight_bc=weight_bc,
        conv_weight=conv_weight,
        conv_bias=line(conv_bias),
        bc_conv_weight=bc_conv_weight,
        bc_conv_bias=line(bc_conv_bias),
        dt_bias=line(dt_bias),
        decay_log=line(decay_log),
        skip_gain=line(skip_gain),
        gate_gain_in=line(gate_gain),
        out_weight=out_weight,
    )
    matrix = ((sz.cols * sz.chan, sz.half), BF16)
    outputs = dict(
        output=((sz.block, sz.half), F32),
        grad_hidden=((sz.block, sz.half), F32),
        grad_norm_gain=((1, sz.half), F32),
        grad_weight_z=matrix,
        grad_weight_x=matrix,
        grad_weight_dt=((sz.head_rows, sz.half), F32),
        grad_weight_bc=((sz.bc, sz.half), BF16),
        small_sums=((HALO + sz.plane_rows, sz.chan), F32),
        grad_out_weight=matrix,
    )
    scratch = scratch_list(sz)
    scratch["bc_full"] = ((sz.cols, sz.rows, sz.bc_part, sz.half), F32)
    names = [*inputs, *outputs, *scratch, "send_sem", "recv_sem"]
    count = semaphore_count(sz)
    vmem = pl.BlockSpec(memory_space=pltpu.VMEM)
    got = pl.pallas_call(
        functools.partial(block_kernel, sz, names),
        out_shape=[jax.ShapeDtypeStruct(*item) for item in outputs.values()],
        in_specs=[vmem] * len(inputs),
        out_specs=[vmem] * len(outputs),
        scratch_shapes=[pltpu.VMEM(*item) for item in scratch.values()]
        + [pltpu.SemaphoreType.DMA((count,)), pltpu.SemaphoreType.DMA((count,))],
        compiler_params=pltpu.CompilerParams(
            collective_id=0, has_side_effects=True, vmem_limit_bytes=62 << 20
        ),
        name="residual_block",
    )(*inputs.values())
    sent = dict(zip(outputs, got))
    results = dict(
        output=(sz.block, sz.half),
        grad_hidden=(sz.block, sz.half),
        grad_norm_gain=(1, sz.half),
        grad_weight_z=weight_z.shape,
        grad_weight_x=weight_x.shape,
        grad_weight_dt=weight_dt.shape[::-1],
        grad_weight_bc=weight_bc.shape,
        grad_conv_weight=conv_weight.shape,
        grad_conv_bias=(1, sz.chan),
        grad_bc_conv_weight=bc_conv_weight.shape,
        grad_bc_conv_bias=(1, sz.bc),
        grad_dt_bias=(1, sz.heads),
        grad_decay_log=(1, sz.heads),
        grad_skip_gain=(1, sz.heads),
        grad_gate_gain=(1, sz.chan),
        grad_out_weight=out_weight.shape,
    )
    got = pl.pallas_call(
        functools.partial(finish_kernel, sz, list(sent), list(results)),
        out_shape=[jax.ShapeDtypeStruct(shape, F32) for shape in results.values()],
        in_specs=[vmem] * len(sent),
        out_specs=[vmem] * len(results),
        compiler_params=pltpu.CompilerParams(vmem_limit_bytes=62 << 20),
        name="write_results",
    )(*sent.values())
    out = dict(zip(results, got))
    out["grad_weight_dt"] = out["grad_weight_dt"].T
    for name in ("norm_gain", "conv_bias", "bc_conv_bias", "dt_bias", "decay_log", "skip_gain", "gate_gain"):
        out["grad_" + name] = out["grad_" + name][0]
    return tuple(out.values())


def solution(mesh):
    in_specs = (
        P(("dp", "row"), None),
        P(("dp", "row"), "col"),
        P(),
        P("col", "row"),
        P("col", "row"),
        P("col", "row"),
        P("col", None),
        P(None, ("row", "col")),
        P(("row", "col")),
        P(),
        P(),
        P(("row", "col")),
        P(("row", "col")),
        P(("row", "col")),
        P(("row", "col")),
        P("row", "col"),
    )
    out_specs = (
        P(("dp", "row"), "col"),
        P(("dp", "row"), "col"),
        P("col"),
        P("col", "row"),
        P("col", "row"),
        P("col", "row"),
        P("col", None),
        P(None, ("row", "col")),
        P(("row", "col")),
        P(),
        P(),
        P(("row", "col")),
        P(("row", "col")),
        P(("row", "col")),
        P(("row", "col")),
        P("row", "col"),
    )
    sizes = tuple(mesh.shape[axis] for axis in ("dp", "row", "col"))
    return jax.shard_map(
        functools.partial(body, sizes), mesh=mesh, in_specs=in_specs, out_specs=out_specs, check_vma=False
    )
```

```python
import functools

import jax
import jax.numpy as jnp
from jax import lax
from jax.experimental import pallas as pl
from jax.experimental.pallas import tpu as pltpu
from jax.sharding import PartitionSpec as P

LANES = 128
HALO = 8
TILE = 16
EPSILON = 1e-05
PRECISE = lax.Precision.HIGHEST
F32 = jnp.float32
BF16 = jnp.bfloat16
MESH = pl.DeviceIdType.MESH


def dot_f32(a, b):
    return jnp.dot(a, b, precision=PRECISE, preferred_element_type=F32)


def dot_nn(a, b):
    return lax.dot_general(a, b, (((1,), (0,)), ((), ())), preferred_element_type=F32)


def dot_nt(a, b):
    return lax.dot_general(a, b, (((1,), (1,)), ((), ())), preferred_element_type=F32)


def dot_tn(a, b):
    return lax.dot_general(a, b, (((0,), (0,)), ((), ())), preferred_element_type=F32)


def sigmoid(v):
    return 1.0 / (1.0 + jnp.exp(-v))


def iota(shape, axis):
    return lax.broadcasted_iota(jnp.int32, shape, axis)


def head_spread(chan, head_width):
    head = iota((LANES, chan), 0)
    lane = iota((LANES, chan), 1)
    return ((lane >= head * head_width) & (lane < (head + 1) * head_width)).astype(F32)


class Sizes:
    def __init__(self, mesh_sizes, hidden, weight_z, weight_dt, weight_bc):
        self.n, self.rows, self.cols = mesh_sizes
        self.pair = 2 if self.rows % 2 == 0 else 1
        self.chips = self.rows // self.pair
        self.block, self.model = hidden.shape
        self.half = weight_z.shape[0]
        self.chan = weight_z.shape[1] // self.cols
        self.row_heads = weight_dt.shape[1]
        self.heads = self.row_heads // self.cols
        self.head_width = self.chan // self.heads
        self.bc = weight_bc.shape[1]
        self.state = self.bc // 2
        self.wide = self.chan + self.bc
        self.bc_part = self.bc // self.rows
        self.head_rows = -(-self.row_heads // TILE) * TILE
        assert self.n % 2 == 0
        self.pieces = next(k for k in (4, 2, 1) if self.chan % (k * TILE) == 0)
        self.piece = self.chan // self.pieces
        self.inner = self.chan * self.rows * self.cols
        self.sum_rows = -(-2 * self.rows // 8) * 8
        self.gain_rows = self.model // self.chan
        self.plane_rows = -(-(5 * self.bc // self.chan + self.gain_rows) // 8) * 8


class Links:
    def __init__(self, send_sem, recv_sem):
        self.send_sem, self.recv_sem = send_sem, recv_sem
        self.count = 0
        self.makers = []

    def take(self, many=1):
        first = self.count
        self.count += many
        return first

    def copy(self, src, dst, at, device):
        return pltpu.make_async_remote_copy(
            src_ref=src,
            dst_ref=dst,
            send_sem=self.send_sem.at[at],
            recv_sem=self.recv_sem.at[at],
            device_id=device,
            device_id_type=MESH,
        )

    def send(self, src, dst, at, device, when=None):
        make = lambda: self.copy(src, dst, at, device)
        self.makers.append((make, when))
        if when is None:
            make().start()
        else:
            pl.when(when)(lambda: make().start())

    def arrived(self, dst, at, device):
        self.copy(dst, dst, at, device).wait_recv()

    def drain(self):
        for make, when in self.makers:
            if when is None:
                make().wait_send()
            else:
                pl.when(when)(lambda: make().wait_send())


def semaphore_count(sz):
    group = sz.rows * sz.cols
    units = 3 * 2 * sz.pieces * (1 + sz.cols)
    front = sz.cols * (sz.n + 1) + 4 * group + 8 * (sz.chips + 1) * (sz.cols + 1) + 8 * sz.cols
    scatter = 3 * (2 * sz.chips * sz.cols + sz.chips + sz.cols)
    return units + front + scatter + 2 * group + 2 * sz.n + sz.rows + sz.cols + 16


def scratch_list(sz):
    nb, n, rows, cols, chips = sz.rows, sz.n, sz.rows, sz.cols, sz.chips
    blk, half, chan, wide = sz.block, sz.half, sz.chan, sz.wide
    across = max(chips - 1, 1)
    other = max(cols - 1, 1)
    shapes = dict(
        tokens=((rows, blk, sz.model), BF16),
        weights=((cols, half, chan + wide), BF16),
        wdt_in=((cols, sz.head_rows, half), BF16),
        wdt=((cols, LANES, half), BF16),
        cots=((rows, cols, blk, half), BF16),
        outw=((cols, chan, half), BF16),
        inv_rms=((blk, LANES), F32),
        conv=((HALO, wide), F32),
        head=((HALO, LANES), F32),
        ext=((nb, HALO + blk, wide), F32),
        z_raw=((nb, blk, chan), F32),
        pre=((nb, blk, wide), F32),
        gate=((nb, blk, wide), F32),
        step_pre=((nb, blk, LANES), F32),
        log_decay=((nb, blk, LANES), F32),
        step_ch=((nb, blk, chan), F32),
        log_ch=((nb, blk, chan), F32),
        decay=((nb, sz.heads, blk, blk), F32),
        states=((nb, sz.state, chan), F32),
        state=((sz.state, chan), F32),
        mixed=((nb, blk, chan), F32),
        inside=((nb, blk, chan), F32),
        ggo=((nb, blk, chan), F32),
        sums=((rows * cols, sz.sum_rows, blk), F32),
        total=((sz.sum_rows, blk), F32),
        gate_out=((nb, blk, chan), BF16),
        grad_z=((nb, blk, chan), BF16),
        grad_x=((nb, blk, chan), BF16),
        grad_bc=((nb, blk, sz.bc), BF16),
        grad_dt=((nb, blk, LANES), BF16),
        gate_gain=((HALO, chan), F32),
        conv_grad=((HALO, wide), F32),
        head_grad=((HALO, LANES), F32),
        skip_grad=((HALO, chan), F32),
        gain_grad=((HALO, sz.model), F32),
        grad_ext=((blk + HALO, wide), F32),
        grad_state=((sz.state, chan), F32),
        own=((3, sz.pieces, sz.piece, sz.model), BF16),
        landed=((3, sz.pieces, sz.piece, sz.model), BF16),
        across=((3, sz.pieces, sz.piece, sz.model), BF16),
        other_half=((3, sz.pieces, other, sz.piece, half), BF16),
        final=((3, sz.pieces, cols, sz.piece, half), BF16),
        keep=((chips, cols, blk, half), F32),
        keep_bc=((chips, cols, sz.bc_part, half), F32),
        dt_rows=((cols, sz.head_rows, half), F32),
        small=((sz.rows * sz.cols, sz.plane_rows, chan), F32),
        dp_small=((n, HALO + sz.plane_rows, chan), F32),
        dp_bc=((n, sz.bc_part + sz.head_rows, half), BF16),
        bc_all=((rows, sz.bc_part, half), BF16),
        dots=((cols, HALO, blk), F32),
    )
    for name, part, extra in (("out", blk, 0), ("bc", sz.bc_part, sz.head_rows), ("in", blk, 0)):
        shapes[name + "_core"] = ((chips, cols, part, half), BF16)
        shapes[name + "_core_got"] = ((chips, cols, part, half), BF16)
        shapes[name + "_chip"] = ((across, cols, part, half), BF16)
        shapes[name + "_chip_got"] = ((across, cols, part, half), BF16)
        shapes[name + "_col"] = ((other, part + extra, half), BF16)
        shapes[name + "_col_got"] = ((other, part + extra, half), BF16)
    return shapes


class Scatter:
    def __init__(self, sz, links, where, bufs, name, keep):
        self.sz, self.links, self.where = sz, links, where
        self.bufs = {key: bufs[name + "_" + key] for key in ("core", "core_got", "chip", "chip_got", "col", "col_got")}
        self.keep = keep
        self.core_at = links.take(sz.chips)
        self.chip_at = links.take(sz.chips * sz.cols)
        self.col_at = links.take(sz.cols)

    def start(self, block_of):
        sz, (dp, row, col, chip, core) = self.sz, self.where
        if sz.pair == 2:
            for x in range(sz.chips):
                for h in range(sz.cols):
                    self.bufs["core"][x, h] = block_of(x * 2 + 1 - core, h).astype(BF16)
                self.links.send(
                    self.bufs["core"].at[x],
                    self.bufs["core_got"].at[x],
                    self.core_at + x,
                    (dp, chip * 2 + 1 - core, col),
                )
        for x in range(sz.chips):
            for h in range(sz.cols):
                self.keep[x, h] = block_of(x * sz.pair + core, h)

    def held(self, x, h):
        value = self.keep[x, h]
        if self.sz.pair == 2:
            value = value + self.bufs["core_got"][x, h].astype(F32)
        return value

    def across(self):
        sz, (dp, row, col, chip, core) = self.sz, self.where
        if sz.pair == 2:
            for x in range(sz.chips):
                self.links.arrived(self.bufs["core_got"].at[x], self.core_at + x, (dp, chip * 2 + 1 - core, col))
        for k in [*range(1, sz.cols), 0]:
            h = lax.rem(col + k, sz.cols)
            for dx in range(1, sz.chips):
                x = lax.rem(chip + dx, sz.chips)
                self.bufs["chip"][dx - 1, k] = self.held(x, h).astype(BF16)
                self.links.send(
                    self.bufs["chip"].at[dx - 1, k],
                    self.bufs["chip_got"].at[dx - 1, k],
                    self.chip_at + dx * sz.cols + k,
                    (dp, x * sz.pair + core, col),
                )

    def summed(self, k):
        sz, (dp, row, col, chip, core) = self.sz, self.where
        value = self.held(chip, lax.rem(col + k, sz.cols))
        for dx in range(1, sz.chips):
            x = lax.rem(chip + dx, sz.chips)
            self.links.arrived(
                self.bufs["chip_got"].at[dx - 1, k], self.chip_at + dx * sz.cols + k, (dp, x * sz.pair + core, col)
            )
            value = value + self.bufs["chip_got"][dx - 1, k].astype(F32)
        return value

    def turn(self, extra=None):
        sz, (dp, row, col, chip, core) = self.sz, self.where
        for k in range(1, sz.cols):
            h = lax.rem(col + k, sz.cols)
            value = self.summed(k)
            part = value.shape[0]
            self.bufs["col"][k - 1, 0:part, :] = value.astype(BF16)
            if extra is not None:
                more = extra(h)
                self.bufs["col"][k - 1, part : part + more.shape[0], :] = more.astype(BF16)
            self.links.send(
                self.bufs["col"].at[k - 1], self.bufs["col_got"].at[k - 1], self.col_at + k, (dp, row, h)
            )

    def finish(self, extra=None):
        sz, (dp, row, col, chip, core) = self.sz, self.where
        value = self.summed(0)
        more = None if extra is None else extra(col)
        part = value.shape[0]
        for k in range(1, sz.cols):
            h = lax.rem(col + k, sz.cols)
            self.links.arrived(self.bufs["col_got"].at[k - 1], self.col_at + k, (dp, row, h))
            value = value + self.bufs["col_got"][k - 1, 0:part, :].astype(F32)
            if more is not None:
                more = more + self.bufs["col_got"][k - 1, part:, :].astype(F32)
        return value, more


class Line:
    def __init__(self, sz, links, where, bufs, part):
        self.sz, self.links, self.where = sz, links, where
        self.own, self.landed, self.across = (bufs[key].at[part] for key in ("own", "landed", "across"))
        self.other_half, self.final = bufs["other_half"].at[part], bufs["final"].at[part]
        self.in_at, self.mid_at = links.take(sz.pieces), links.take(sz.pieces)
        self.col_at, self.out_at = links.take(sz.pieces * sz.cols), links.take(sz.pieces * sz.cols)
        dp, last = where[0], sz.n - 1
        low = dp < sz.n // 2
        self.middle = sz.n // 2 - 1
        self.place = jnp.where(low, dp, last - dp)
        self.inward = jnp.where(low, dp + 1, dp - 1)
        self.outward = jnp.clip(jnp.where(low, dp - 1, dp + 1), 0, last)

    def in_copy(self, g):
        target = (self.inward, *self.where[1:3])
        return self.links.copy(self.own.at[g], self.landed.at[g], self.in_at + g, target)

    def mid_copy(self, g):
        target = (self.inward, *self.where[1:3])
        return self.links.copy(self.own.at[g], self.across.at[g], self.mid_at + g, target)

    def half_copy(self, g, k, out):
        sz, (dp, row, col) = self.sz, self.where[:3]
        source = self.final.at[g, col] if k == 0 else self.other_half.at[g, k - 1]
        at = (self.out_at if out else self.col_at) + g * sz.cols + k
        target = (self.outward if out else dp, row, lax.rem(col + k, sz.cols))
        return self.links.copy(source, self.final.at[g, col], at, target)

    def pass_copy(self, g, k, device):
        sz, (dp, row, col) = self.sz, self.where[:3]
        ref = self.final.at[g, lax.rem(col + sz.cols - k, sz.cols)]
        return self.links.copy(ref, ref, self.out_at + g * sz.cols + k, (device, row, col))

    def source(self, g):
        if self.middle > 0:
            pl.when(self.place == 0)(lambda: self.in_copy(g).start())

    def fold(self, g):
        self.in_copy(g).wait_recv()
        self.own[g] = (self.own[g].astype(F32) + self.landed[g].astype(F32)).astype(BF16)

    def enter(self, g):
        if self.middle > 0:
            pl.when(self.place > 0)(lambda: self.fold(g))
        if self.middle > 1:
            pl.when((self.place > 0) & (self.place < self.middle))(lambda: self.in_copy(g).start())
        pl.when(self.place == self.middle)(lambda: self.mid_copy(g).start())

    def meet(self, g):
        sz, col = self.sz, self.where[2]
        self.mid_copy(g).wait()
        self.own[g] = (self.own[g].astype(F32) + self.across[g].astype(F32)).astype(BF16)
        for k in range(sz.cols):
            h = lax.rem(col + k, sz.cols)
            half = self.own[g, :, pl.ds(pl.multiple_of(h * sz.half, LANES), sz.half)]
            if k == 0:
                self.final[g, col] = half
            else:
                self.other_half[g, k - 1] = half
            if self.middle > 0:
                self.half_copy(g, k, True).start()
            if k > 0:
                self.half_copy(g, k, False).start()

    def cross(self, g):
        pl.when(self.place == self.middle)(lambda: self.meet(g))

    def from_columns(self, g):
        sz, (dp, row, col) = self.sz, self.where[:3]
        for k in range(1, sz.cols):
            h = lax.rem(col + sz.cols - k, sz.cols)
            self.links.arrived(self.final.at[g, h], self.col_at + g * sz.cols + k, (dp, row, h))

    def from_inward(self, g):
        for k in range(self.sz.cols):
            self.pass_copy(g, k, self.inward).wait_recv()

    def pass_on(self, g):
        for k in range(self.sz.cols):
            self.pass_copy(g, k, self.outward).start()

    def leave(self, g):
        pl.when(self.place == self.middle)(lambda: self.from_columns(g))
        if self.middle > 0:
            pl.when(self.place < self.middle)(lambda: self.from_inward(g))
        if self.middle > 1:
            pl.when((self.place > 0) & (self.place < self.middle))(lambda: self.pass_on(g))

    def sent_halves(self, g):
        for k in range(self.sz.cols):
            if self.middle > 0:
                self.half_copy(g, k, True).wait_send()
            if k > 0:
                self.half_copy(g, k, False).wait_send()

    def sent_on(self, g):
        for k in range(self.sz.cols):
            self.pass_copy(g, k, self.outward).wait_send()

    def drain(self):
        for g in range(self.sz.pieces):
            if self.middle > 0:
                pl.when(self.place < self.middle)(lambda: self.in_copy(g).wait_send())
            pl.when(self.place == self.middle)(lambda: self.sent_halves(g))
            if self.middle > 1:
                pl.when((self.place > 0) & (self.place < self.middle))(lambda: self.sent_on(g))


def forward_block(sz, m, b):
    blk, chan, wide, half = sz.block, sz.chan, sz.wide, sz.half
    acc = jnp.zeros((blk, chan + wide), F32)
    step_raw = jnp.zeros((blk, LANES), F32)
    for h in range(sz.cols):
        part = m.tokens[b, :, h * half : (h + 1) * half]
        acc = acc + dot_nn(part, m.weights[h])
        step_raw = step_raw + dot_nt(part, m.wdt[h])
    z_raw = acc[:, :chan]
    m.z_raw[b] = z_raw
    m.ext[b, HALO : HALO + blk, :] = acc[:, chan:]

    @pl.when(b + 1 < sz.rows)
    def _():
        m.ext[b + 1, 0:HALO, :] = m.ext[b, blk : blk + HALO, :]

    pre = m.conv[4:5, :]
    for tap in range(4):
        first = HALO - 3 + tap
        pre = pre + m.conv[tap : tap + 1, :] * m.ext[b, first : first + blk, :]
    gate = sigmoid(pre)
    m.pre[b] = pre
    m.gate[b] = gate
    conv = pre * gate
    step_pre = step_raw + m.head[0:1, :]
    m.step_pre[b] = step_pre
    step = jnp.maximum(step_pre, 0.0) + jnp.log1p(jnp.exp(-jnp.abs(step_pre)))
    rate = -jnp.exp(m.head[1:2, :])
    causal = iota((blk, blk), 0) >= iota((blk, blk), 1)
    log_decay = dot_f32(causal.astype(F32), step * rate)
    m.log_decay[b] = log_decay
    spread = head_spread(chan, sz.head_width)
    step_ch = dot_f32(step, spread)
    log_ch = dot_f32(log_decay, spread)
    m.step_ch[b] = step_ch
    m.log_ch[b] = log_ch
    skip_ch = dot_f32(jnp.broadcast_to(m.head[2:3, :], (HALO, LANES)), spread)[0:1, :]

    x_conv = conv[:, :chan]
    b_half = conv[:, chan : chan + sz.state].astype(BF16)
    c_half = conv[:, chan + sz.state :].astype(BF16)
    stepped = x_conv * step_ch
    scores = dot_nt(c_half, b_half)
    log_rows = log_decay.T
    lane = iota((blk, chan), 1)
    inside = jnp.zeros((blk, chan), F32)
    for head in range(sz.heads):
        gap = log_decay[:, head : head + 1] - log_rows[head : head + 1, :]
        decay = jnp.exp(jnp.where(causal, gap, -1e30))
        m.decay[b, head] = decay
        mixing = (scores * decay).astype(BF16)
        mine = (lane >= head * sz.head_width) & (lane < (head + 1) * sz.head_width)
        inside = inside + dot_nn(mixing, jnp.where(mine, stepped, 0.0).astype(BF16))
    entering = m.state[...]
    m.states[b] = entering
    outside = dot_nn(c_half, entering.astype(BF16)) * jnp.exp(log_ch)
    mixed = inside + outside + skip_ch * x_conv
    last = log_ch[blk - 1 : blk, :]
    tail = stepped * jnp.exp(last - log_ch)
    m.state[...] = entering * jnp.exp(last) + dot_tn(b_half, tail.astype(BF16))
    m.mixed[b] = mixed
    m.inside[b] = inside


def backward_block(sz, m, b, shift):
    blk, chan, wide = sz.block, sz.chan, sz.wide
    pre = m.pre[b]
    gate = m.gate[b]
    conv = pre * gate
    step_pre = m.step_pre[b]
    step = jnp.maximum(step_pre, 0.0) + jnp.log1p(jnp.exp(-jnp.abs(step_pre)))
    rate = -jnp.exp(m.head[1:2, :])
    step_ch = m.step_ch[b]
    log_ch = m.log_ch[b]
    spread = head_spread(chan, sz.head_width)
    skip_ch = dot_f32(jnp.broadcast_to(m.head[2:3, :], (HALO, LANES)), spread)[0:1, :]
    x_conv = conv[:, :chan]
    b_half = conv[:, chan : chan + sz.state].astype(BF16)
    c_half = conv[:, chan + sz.state :].astype(BF16)
    stepped = x_conv * step_ch
    stepped_half = stepped.astype(BF16)
    grad_mixed = m.ggo[b]
    grad_half = grad_mixed.astype(BF16)
    inside = m.inside[b]
    outside = m.mixed[b] - inside - skip_ch * x_conv

    scores = dot_nt(c_half, b_half)
    lane = iota((blk, chan), 1)
    grad_scores = jnp.zeros((blk, blk), F32)
    grad_inner = jnp.zeros((blk, chan), F32)
    for head in range(sz.heads):
        decay = m.decay[b, head]
        mixing = (scores * decay).astype(BF16)
        mine = (lane >= head * sz.head_width) & (lane < (head + 1) * sz.head_width)
        grad_mine = jnp.where(mine, grad_mixed, 0.0).astype(BF16)
        grad_scores = grad_scores + dot_nt(grad_mine, stepped_half) * decay
        grad_inner = grad_inner + dot_tn(mixing, grad_mine)
    scores_half = grad_scores.astype(BF16)

    entering = m.states[b]
    left = m.grad_state[...]
    left_half = left.astype(BF16)
    grad_outer = (grad_mixed * jnp.exp(log_ch)).astype(BF16)
    last = log_ch[blk - 1 : blk, :]
    fade = jnp.exp(last - log_ch)
    tail = stepped * fade
    grad_tail = dot_nn(b_half, left_half)
    tail_term = tail * grad_tail
    grad_c = dot_nt(grad_outer, entering.astype(BF16)) + dot_nn(scores_half, b_half)
    grad_b = dot_nt(tail.astype(BF16), left_half) + dot_tn(scores_half, c_half)
    grad_last = jnp.sum(tail_term, axis=0, keepdims=True) + jnp.exp(last) * jnp.sum(
        left * entering, axis=0, keepdims=True
    )
    m.grad_state[...] = left * jnp.exp(last) + dot_tn(c_half, grad_outer)

    grad_stepped = grad_inner + grad_tail * fade
    log_term = (
        grad_half.astype(F32) * inside
        + grad_mixed * outside
        - stepped_half.astype(F32) * grad_inner
        - tail_term
    )
    row = iota((blk, chan), 0)
    log_term = log_term + jnp.where(row == blk - 1, grad_last, 0.0)

    def per_head(values):
        return lax.dot_general(
            values, spread, (((1,), (1,)), ((), ())), precision=PRECISE, preferred_element_type=F32
        )

    later = (iota((blk, blk), 0) <= iota((blk, blk), 1)).astype(F32)
    grad_rate_step = dot_f32(later, per_head(log_term))
    grad_step = per_head(grad_stepped * x_conv) + grad_rate_step * rate
    grad_step_raw = grad_step * sigmoid(step_pre)
    m.head_grad[0:1, :] += jnp.sum(grad_step_raw, axis=0, keepdims=True)
    m.head_grad[1:2, :] += jnp.sum(grad_rate_step * step, axis=0, keepdims=True) * rate
    m.skip_grad[0:1, :] += jnp.sum(grad_mixed * x_conv, axis=0, keepdims=True)

    grad_x = grad_stepped * step_ch + grad_mixed * skip_ch
    slope = gate * (1.0 + pre * (1.0 - gate))
    m.grad_ext[blk : blk + HALO, :] = m.grad_ext[0:HALO, :]
    m.grad_ext[0:blk, 0:chan] = grad_x * slope[:, :chan]
    m.grad_ext[0:blk, chan : chan + sz.state] = grad_b * slope[:, chan : chan + sz.state]
    m.grad_ext[0:blk, chan + sz.state :] = grad_c * slope[:, chan + sz.state :]
    grad_pre = m.grad_ext[0:blk, :]
    grad_raw = jnp.zeros((blk, wide), F32)
    for tap in range(4):
        grad_raw = grad_raw + m.conv[tap : tap + 1, :] * m.grad_ext[3 - tap : 3 - tap + blk, :]
        first = HALO - 3 + tap
        m.conv_grad[tap : tap + 1, :] += jnp.sum(
            grad_pre * m.ext[b, first : first + blk, :], axis=0, keepdims=True
        )
    m.conv_grad[4:5, :] += jnp.sum(grad_pre, axis=0, keepdims=True)
    m.grad_x[b] = grad_raw[:, :chan].astype(BF16)
    m.grad_bc[b] = grad_raw[:, chan:].astype(BF16)
    m.grad_dt[b] = dot_nn(grad_step_raw.astype(BF16), shift).astype(BF16)


class Refs:
    pass


def block_kernel(sz, names, *refs):
    m = Refs()
    for name, ref in zip(names, refs):
        setattr(m, name, ref)
    bufs = m.__dict__
    nb, rows, cols, chips, pair = sz.rows, sz.rows, sz.cols, sz.chips, sz.pair
    blk, half, chan, wide, n = sz.block, sz.half, sz.chan, sz.wide, sz.n
    dp, row, col = lax.axis_index("dp"), lax.axis_index("row"), lax.axis_index("col")
    chip, core = row // pair, lax.rem(row, pair)
    where = (dp, row, col, chip, core)
    group = rows * cols
    mine = row * cols + col
    sibling = (dp, chip * pair + lax.rem(core + 1, pair), col)
    sibling_core = lax.rem(core + 1, pair)

    def plane_peer(k):
        return dp, lax.rem(row + k // cols, rows), lax.rem(col + k % cols, cols)

    def line_peer(k):
        return lax.rem(dp + k, n), row, col

    def col_peer(k):
        return dp, row, lax.rem(col + k, cols)

    def chip_peer(dx):
        return dp, lax.rem(chip + dx, chips) * pair + core, col

    def from_chip(dx):
        return lax.rem(chip + chips - dx, chips) * pair + core

    def from_sibling(dx):
        return lax.rem(chip + chips - dx, chips) * pair + sibling_core

    def from_col(k):
        return lax.rem(col + cols - k, cols)

    links = Links(m.send_sem, m.recv_sem)
    barrier = pltpu.get_barrier_semaphore()
    peers = [plane_peer(k) for k in range(1, group)] + [line_peer(k) for k in range(1, n)]
    for peer in peers:
        pl.semaphore_signal(barrier, inc=1, device_id=peer, device_id_type=MESH)

    def lanes(start, size):
        return pl.ds(pl.multiple_of(start * size, LANES), size)

    hidden = m.hidden[...]
    inv_rms = lax.rsqrt(jnp.mean(hidden * hidden, axis=1, keepdims=True) + EPSILON)
    m.inv_rms[...] = jnp.broadcast_to(inv_rms, (blk, LANES))
    m.tokens[row] = (hidden * inv_rms * m.norm_gain[...]).astype(BF16)
    m.cots[row, col] = m.cotangent[...].astype(BF16)
    steps_in = m.weight_dt[...].astype(F32)
    if sz.head_rows > sz.row_heads:
        steps_in = jnp.concatenate([steps_in, jnp.zeros((sz.head_rows - sz.row_heads, half), F32)], axis=0)
    m.wdt_in[col] = steps_in.astype(BF16)

    pl.semaphore_wait(barrier, len(peers))

    w_at, bc_at, dt_at, bc_fwd = links.take(2 * cols), links.take(cols), links.take(cols), links.take(cols)
    tok_x, tok_s = links.take(chips), links.take(chips)
    cot_y, cot_x, cot_s = links.take(cols), links.take(chips * cols), links.take(chips * cols)
    out_at = links.take(cols)
    bc_rows = half // pair
    bc_mine = pl.ds(pl.multiple_of(core * bc_rows, TILE), bc_rows)
    bc_sib = pl.ds(pl.multiple_of(sibling_core * bc_rows, TILE), bc_rows)
    bc_lanes = pl.ds(2 * chan, sz.bc)
    x_lanes = pl.ds(chan, chan)
    spread_x = n if half % (n * TILE) == 0 else 1
    x_slice = half // spread_x
    x_at = links.take(cols * n)

    def x_rows(k):
        owner = lax.rem(dp + n - k, n) if spread_x > 1 else 0
        return pl.ds(pl.multiple_of(owner * x_slice, TILE), x_slice)

    for k in range(1, cols):
        peer = col_peer(k)
        links.send(
            m.weight_x.at[x_rows(0), lanes(peer[2], chan)], m.weights.at[col, x_rows(0), x_lanes], w_at + 2 * k + 1, peer
        )
        links.send(
            m.weight_z.at[:, lanes(peer[2], chan)], m.weights.at[col, :, pl.ds(0, chan)], w_at + 2 * k, peer
        )
        links.send(m.weight_bc.at[bc_mine, :], m.weights.at[col, bc_mine, bc_lanes], bc_at + k, peer)
        links.send(m.wdt_in.at[col], m.wdt_in.at[col], dt_at + k, peer)
    for dx in range(1, chips):
        links.send(m.tokens.at[row], m.tokens.at[row], tok_x + dx, chip_peer(dx))
    if pair == 2:
        links.send(m.tokens.at[row], m.tokens.at[row], tok_s, sibling)

    m.weights[col, :, 0:chan] = m.weight_z[:, lanes(col, chan)]
    m.weights[col, :, chan : 2 * chan] = m.weight_x[:, lanes(col, chan)]
    m.weights[col, :, 2 * chan :] = m.weight_bc[...]
    m.outw[col] = m.out_weight[pl.ds(pl.multiple_of(col * chan, TILE), chan), :]
    for ref in (m.conv, m.head, m.state, m.grad_state, m.grad_ext, m.gate_gain, m.conv_grad, m.head_grad):
        ref[...] = jnp.zeros_like(ref)
    for ref in (m.skip_grad, m.gain_grad):
        ref[...] = jnp.zeros_like(ref)
    m.ext[0, 0:HALO, :] = jnp.zeros((HALO, wide), F32)
    m.conv[0:4, 0:chan] = m.conv_weight[...]
    m.conv[0:4, chan:] = m.bc_conv_weight[...]
    m.conv[4:5, 0:chan] = m.conv_bias[...]
    m.conv[4:5, chan:] = m.bc_conv_bias[...]
    m.head[0:1, 0 : sz.heads] = m.dt_bias[...]
    m.head[1:2, 0 : sz.heads] = m.decay_log[...]
    m.head[2:3, 0 : sz.heads] = m.skip_gain[...]

    def send_cots(dx, k, r, c):
        if dx == 0:
            for far in range(1, chips):
                links.send(m.cots.at[r, c], m.cots.at[r, c], cot_x + far * cols + k, chip_peer(far))
        if pair == 2:
            links.send(m.cots.at[r, c], m.cots.at[r, c], cot_s + dx * cols + k, sibling)

    for k in range(1, cols):
        part = m.weights.at[from_col(k), x_rows(0), x_lanes]
        links.arrived(part, w_at + 2 * k + 1, col_peer(k))
        for j in range(1, spread_x):
            links.send(part, part, x_at + k * n + j, line_peer(j))
    for dx in range(1, chips):
        links.arrived(m.tokens.at[from_chip(dx)], tok_x + dx, chip_peer(dx))
        if pair == 2:
            links.send(m.tokens.at[from_chip(dx)], m.tokens.at[from_chip(dx)], tok_s + dx, sibling)
    send_cots(0, 0, row, col)
    for k in range(1, cols):
        peer, src = col_peer(k), from_col(k)
        links.arrived(m.weights.at[src, :, pl.ds(0, chan)], w_at + 2 * k, peer)
        links.arrived(m.weights.at[src, bc_mine, bc_lanes], bc_at + k, peer)
        if pair == 2:
            links.send(
                m.weights.at[src, bc_mine, bc_lanes], m.weights.at[src, bc_mine, bc_lanes], bc_fwd + k, sibling
            )
        links.arrived(m.wdt_in.at[src], dt_at + k, peer)
        links.send(m.cots.at[row, col], m.cots.at[row, col], cot_y + k, peer)

    head_at, head_to = iota((LANES, LANES), 0), iota((LANES, LANES), 1)
    shift = ((head_to == head_at + col * sz.heads) & (head_at < sz.heads)).astype(BF16)
    for h in range(cols):
        padded = jnp.concatenate([m.wdt_in[h], jnp.zeros((LANES - sz.head_rows, half), BF16)], axis=0)
        m.wdt[h] = dot_nn(shift, padded).astype(BF16)

    for k in range(1, cols):
        for j in range(1, spread_x):
            links.arrived(m.weights.at[from_col(k), x_rows(j), x_lanes], x_at + k * n + j, line_peer(j))
    if pair == 2:
        for dx in range(chips):
            links.arrived(m.tokens.at[from_sibling(dx)], tok_s + dx, sibling)
        for k in range(1, cols):
            links.arrived(m.weights.at[from_col(k), bc_sib, bc_lanes], bc_fwd + k, sibling)

    def pass_col_cots():
        for k in range(1, cols):
            links.arrived(m.cots.at[row, from_col(k)], cot_y + k, col_peer(k))

    def pass_chip_cots(k):
        for dx in range(1, chips):
            r, c = from_chip(dx), from_col(k)
            links.arrived(m.cots.at[r, c], cot_x + dx * cols + k, chip_peer(dx))

    def forward_step(b, carry):
        forward_block(sz, m, b)
        return carry

    early = min(2, nb)
    lax.fori_loop(0, early, forward_step, 0)
    pass_col_cots()
    for k in range(1, cols):
        send_cots(0, k, row, from_col(k))
        peer = col_peer(k)
        links.send(
            m.out_weight.at[pl.ds(pl.multiple_of(peer[2] * chan, TILE), chan), :], m.outw.at[col], out_at + k, peer
        )
    pass_chip_cots(0)
    for dx in range(1, chips):
        send_cots(dx, 0, from_chip(dx), col)
    lax.fori_loop(early, nb, forward_step, 0)
    for k in range(1, cols):
        pass_chip_cots(k)
        for dx in range(1, chips):
            send_cots(dx, k, from_chip(dx), from_col(k))
    for k in range(1, cols):
        links.arrived(m.outw.at[from_col(k)], out_at + k, col_peer(k))
    if pair == 2:
        for dx in range(chips):
            for k in range(cols):
                links.arrived(m.cots.at[from_sibling(dx), from_col(k)], cot_s + dx * cols + k, sibling)

    sub = iota((LANES, blk), 0)
    m.sums[mine] = jnp.zeros((sz.sum_rows, blk), F32)

    def sum_step(b, carry):
        ggo = jnp.zeros((blk, chan), F32)
        for h in range(cols):
            ggo = ggo + dot_nt(m.cots[b, h], m.outw[h])
        m.ggo[b] = ggo
        z_raw = m.z_raw[b]
        gated = m.mixed[b] * (z_raw * sigmoid(z_raw))
        squares = jnp.sum(gated * gated, axis=1, keepdims=True)
        inner = jnp.sum(ggo * m.gate_gain_in[...] * gated, axis=1, keepdims=True)
        lane = iota((blk, LANES), 1)
        both = jnp.where(lane == 0, squares, jnp.where(lane == 1, inner, 0.0)).T
        m.sums[mine, pl.ds(b, 1), :] = both[0:1, :]
        m.sums[mine, pl.ds(nb + b, 1), :] = both[1:2, :]
        return carry

    lax.fori_loop(0, nb, sum_step, 0)

    def to_plane(ref):
        at = links.take(group)
        for k in range(1, group):
            links.send(ref.at[mine], ref.at[mine], at + k, plane_peer(k))
        return at

    def from_plane(ref, at):
        for k in range(1, group):
            r, c = lax.rem(row + rows - k // cols, rows), lax.rem(col + cols - k % cols, cols)
            links.arrived(ref.at[r * cols + c], at + k, plane_peer(k))
        value = ref[0]
        for k in range(1, group):
            value = value + ref[k]
        return value

    m.total[...] = from_plane(m.sums, to_plane(m.sums))

    def gate_step(b, carry):
        first = m.total[pl.ds(b, 1), :]
        second = m.total[pl.ds(nb + b, 1), :]
        both = jnp.where(sub == 0, first, jnp.where(sub == 1, second, 0.0)).T
        inv_gate = lax.rsqrt(both[:, 0:1] / sz.inner + EPSILON)
        gate_dot = both[:, 1:2] * inv_gate
        ggo = m.ggo[b]
        gate_gain = m.gate_gain_in[...]
        z_raw = m.z_raw[b]
        z_gate = sigmoid(z_raw)
        mixed = m.mixed[b]
        gate_hat = mixed * (z_raw * z_gate) * inv_gate
        grad_gated = inv_gate * (ggo * gate_gain - gate_hat * (gate_dot / sz.inner))
        m.grad_z[b] = (grad_gated * mixed * (z_gate * (1.0 + z_raw * (1.0 - z_gate)))).astype(BF16)
        m.gate_out[b] = (gate_hat * gate_gain).astype(BF16)
        m.gate_gain[0:1, :] += jnp.sum(ggo * gate_hat, axis=0, keepdims=True)
        m.ggo[b] = grad_gated * (z_raw * z_gate)
        return carry

    lax.fori_loop(0, nb, gate_step, 0)

    def flat(ref):
        value = ref[...]
        return value.reshape(value.shape[0] * value.shape[1], value.shape[2])

    lines = [Line(sz, links, where, bufs, part) for part in range(3)]
    order = [(line, g) for line in lines for g in range(sz.pieces)]

    def stage(i):
        for back, name in ((0, "enter"), (2, "cross"), (4, "leave")):
            if 0 <= i - back < len(order):
                line, g = order[i - back]
                getattr(line, name)(g)

    stages = [functools.partial(stage, i) for i in range(len(order) + 4)]

    def advance(many=1, keep=0):
        for _ in range(many):
            if len(stages) > keep:
                stages.pop(0)()

    def sources(part, first, last):
        for g in range(sz.pieces):
            if first <= g * 4 // sz.pieces < last:
                lines[part].source(g)

    def collect(part, ref):
        for c in range(cols):
            for i in range(sz.pieces):
                at = c * chan + i * sz.piece
                ref[at : at + sz.piece, :] = m.final[part, i, c]

    def weight_part(part, grads, operand_of):
        for h in range(cols):
            value = dot_tn(grads, operand_of(h)).astype(BF16)
            m.own[part, :, :, h * half : (h + 1) * half] = value.reshape(sz.pieces, sz.piece, half)

    def cots_of(h):
        return m.cots[:, h].reshape(rows * blk, half)

    def tokens_of(h):
        return m.tokens[:, :, h * half : (h + 1) * half].reshape(rows * blk, half)

    weight_part(0, flat(m.gate_out), cots_of)
    sources(0, 0, 2)
    weight_part(1, flat(m.grad_z), tokens_of)
    sources(0, 2, 4)
    out_sum = Scatter(sz, links, where, bufs, "out", m.keep)
    out_sum.start(lambda r, h: dot_nn(m.gate_out[r], m.outw[h]))
    sources(1, 0, 2)

    def backward_step(i, carry):
        backward_block(sz, m, nb - 1 - i, shift)
        return carry

    before_x = sz.pieces + 4
    services = [
        [lambda: advance(1, before_x), lambda: sources(1, 2, 4), out_sum.across],
        [lambda: advance(1, before_x)],
        [lambda: advance(1, before_x)],
        [],
    ]
    done = 0
    for i, service in enumerate(services):
        until = nb if i == len(services) - 1 else min(nb, done + max(nb // 4, 1))
        lax.fori_loop(done, until, backward_step, 0)
        done = until
        for step in service:
            step()

    weight_part(2, flat(m.grad_x), tokens_of)
    sources(2, 0, 4)
    advance()
    out_sum.turn()
    dt_grads = flat(m.grad_dt)
    for h in range(cols):
        part = dot_tn(flat(m.grad_bc), tokens_of(h))
        m.bc_full[h] = part.reshape(rows, sz.bc_part, half)
        m.dt_rows[h] = dot_tn(dt_grads, tokens_of(h))[0 : sz.head_rows, :]
    bc_sum = Scatter(sz, links, where, bufs, "bc", m.keep_bc)
    bc_sum.start(lambda r, h: m.bc_full[h, r])
    advance()
    total, _ = out_sum.finish()
    m.output[...] = m.hidden[:, lanes(col, half)] + total

    def grad_block(r, h):
        w = m.weights.at[h]
        value = dot_nt(m.grad_z[r], w[:, 0:chan])
        value = value + dot_nt(m.grad_x[r], w[:, chan : 2 * chan])
        value = value + dot_nt(m.grad_bc[r], w[:, 2 * chan :])
        padded = jnp.concatenate([m.wdt_in[h], jnp.zeros((LANES - sz.head_rows, half), BF16)], axis=0)
        value = value + dot_nn(m.grad_dt[r], padded)
        at = slice(h * half, (h + 1) * half)
        m.gain_grad[0:1, at] += jnp.sum(value * m.tokens[r, :, at].astype(F32), axis=0, keepdims=True)
        return value

    in_sum = Scatter(sz, links, where, bufs, "in", m.keep)
    bc_sum.across()
    advance()
    in_sum.start(grad_block)
    advance()

    m.small[mine] = jnp.zeros((sz.plane_rows, chan), F32)
    per_row = sz.bc // chan
    for j in range(5):
        for p in range(per_row):
            at = chan + p * chan
            m.small[mine, j * per_row + p : j * per_row + p + 1, :] = m.conv_grad[j : j + 1, at : at + chan]
    for j in range(sz.gain_rows):
        at = 5 * per_row + j
        m.small[mine, at : at + 1, :] = m.gain_grad[0:1, j * chan : (j + 1) * chan]
    small_at = to_plane(m.small)
    in_sum.across()
    advance()
    dt_of = lambda h: m.dt_rows[h]
    bc_sum.turn(dt_of)
    advance()
    spread = head_spread(chan, sz.head_width)
    skip_heads = lax.dot_general(
        m.skip_grad[...], spread, (((1,), (1,)), ((), ())), precision=PRECISE, preferred_element_type=F32
    )
    m.dp_small[dp] = jnp.zeros((HALO + sz.plane_rows, chan), F32)
    m.dp_small[dp, 0:5, :] = m.conv_grad[0:5, 0:chan]
    m.dp_small[dp, 5:6, :] = m.gate_gain[0:1, :]
    m.dp_small[dp, 6:7, 0:LANES] = m.head_grad[0:1, :]
    m.dp_small[dp, 6:7, LANES : 2 * LANES] = m.head_grad[1:2, :]
    m.dp_small[dp, 7:8, 0:LANES] = skip_heads[0:1, :]
    m.dp_small[dp, HALO:, :] = from_plane(m.small, small_at)

    def to_line(ref):
        at = links.take(n)
        for k in range(1, n):
            links.send(ref.at[dp], ref.at[dp], at + k, line_peer(k))
        return at

    def from_line(ref, at):
        for k in range(1, n):
            links.arrived(ref.at[lax.rem(dp + n - k, n)], at + k, line_peer(k))
        value = ref[0].astype(F32)
        for k in range(1, n):
            value = value + ref[k].astype(F32)
        return value

    small_line = to_line(m.dp_small)
    bc_value, dt_value = bc_sum.finish(dt_of)
    m.dp_bc[dp, 0 : sz.bc_part, :] = bc_value.astype(BF16)
    m.dp_bc[dp, sz.bc_part :, :] = dt_value.astype(BF16)
    bc_line = to_line(m.dp_bc)
    advance()
    in_sum.turn()
    advance()

    bc_total = from_line(m.dp_bc, bc_line)
    m.grad_weight_dt[...] = bc_total[sz.bc_part :, :]
    m.bc_all[row] = bc_total[0 : sz.bc_part, :].astype(BF16)
    row_at = links.take(rows)
    for k in range(1, rows):
        links.send(m.bc_all.at[row], m.bc_all.at[row], row_at + k, (dp, lax.rem(row + k, rows), col))

    grad_scaled, _ = in_sum.finish()
    inv_wide = m.inv_rms[:, 0:1]
    normed = m.hidden[:, lanes(col, half)] * inv_wide
    grad_in = grad_scaled * m.norm_gain[:, lanes(col, half)]
    dot = jnp.sum(grad_in * normed, axis=1, keepdims=True)
    lane = iota((blk, LANES), 1)
    m.dots[col] = jnp.where(lane == 0, dot, 0.0).T[0:HALO, :]
    dot_at = links.take(cols)
    for k in range(1, cols):
        links.send(m.dots.at[col], m.dots.at[col], dot_at + k, col_peer(k))
    advance()
    advance(1, 3)
    collect(0, m.grad_out_weight)
    collect(1, m.grad_weight_z)
    for k in range(1, cols):
        links.arrived(m.dots.at[from_col(k)], dot_at + k, col_peer(k))
    dots = m.dots[0]
    for k in range(1, cols):
        dots = dots + m.dots[k]
    full = jnp.concatenate([dots, jnp.zeros((LANES - HALO, blk), F32)], axis=0).T
    m.grad_hidden[...] = m.cotangent[...] + inv_wide * (grad_in - normed * (full[:, 0:1] / sz.model))

    summed = from_line(m.dp_small, small_line)
    m.small_sums[...] = summed
    per_half = half // chan
    for j in range(per_half):
        at = HALO + 5 * per_row
        line = jnp.zeros((1, chan), F32)
        for c in range(cols):
            here = summed[at + c * per_half + j : at + c * per_half + j + 1, :]
            line = jnp.where(col == c, here, line)
        gain = m.norm_gain[:, pl.ds(pl.multiple_of(col * half + j * chan, LANES), chan)]
        m.grad_norm_gain[:, j * chan : (j + 1) * chan] = line / gain

    for k in range(1, rows):
        at = lax.rem(row + rows - k, rows)
        links.arrived(m.bc_all.at[at], row_at + k, (dp, lax.rem(row + k, rows), col))
    m.grad_weight_bc[...] = flat(m.bc_all)
    advance(len(stages))
    collect(2, m.grad_weight_x)
    links.drain()
    for line in lines:
        line.drain()


def finish_kernel(sz, sent, results, *refs):
    i, o = Refs(), Refs()
    for name, ref in zip(sent, refs):
        setattr(i, name, ref)
    for name, ref in zip(results, refs[len(sent) :]):
        setattr(o, name, ref)
    chan = sz.chan
    per_row = sz.bc // chan
    for name in ("output", "grad_hidden"):
        getattr(o, name)[...] = getattr(i, name)[...]
    o.grad_out_weight[...] = i.grad_out_weight[...].astype(F32)
    for name in ("grad_weight_z", "grad_weight_x", "grad_weight_bc"):
        getattr(o, name)[...] = getattr(i, name)[...].astype(F32).T

    o.grad_norm_gain[...] = i.grad_norm_gain[...]
    o.grad_weight_dt[...] = i.grad_weight_dt[0 : sz.row_heads, :]
    o.grad_conv_weight[...] = i.small_sums[0:4, :]
    o.grad_conv_bias[...] = i.small_sums[4:5, :]
    o.grad_gate_gain[...] = i.small_sums[5:6, :]
    o.grad_dt_bias[...] = i.small_sums[6:7, 0 : sz.heads]
    o.grad_decay_log[...] = i.small_sums[6:7, LANES : LANES + sz.heads]
    o.grad_skip_gain[...] = i.small_sums[7:8, 0 : sz.heads]
    for j in range(5):
        for p in range(per_row):
            at = HALO + j * per_row + p
            lanes = slice(p * chan, (p + 1) * chan)
            if j < 4:
                o.grad_bc_conv_weight[j : j + 1, lanes] = i.small_sums[at : at + 1, :]
            else:
                o.grad_bc_conv_bias[:, lanes] = i.small_sums[at : at + 1, :]


def body(
    mesh_sizes,
    hidden,
    cotangent,
    norm_gain,
    weight_z,
    weight_x,
    weight_dt,
    weight_bc,
    conv_weight,
    conv_bias,
    bc_conv_weight,
    bc_conv_bias,
    dt_bias,
    decay_log,
    skip_gain,
    gate_gain,
    out_weight,
):
    sz = Sizes(mesh_sizes, hidden, weight_z, weight_dt, weight_bc)
    line = lambda vector: vector[None, :]
    inputs = dict(
        hidden=hidden,
        cotangent=cotangent,
        norm_gain=line(norm_gain),
        weight_z=weight_z,
        weight_x=weight_x,
        weight_dt=weight_dt.T,
        weight_bc=weight_bc,
        conv_weight=conv_weight,
        conv_bias=line(conv_bias),
        bc_conv_weight=bc_conv_weight,
        bc_conv_bias=line(bc_conv_bias),
        dt_bias=line(dt_bias),
        decay_log=line(decay_log),
        skip_gain=line(skip_gain),
        gate_gain_in=line(gate_gain),
        out_weight=out_weight,
    )
    matrix = ((sz.cols * sz.chan, sz.half), BF16)
    outputs = dict(
        output=((sz.block, sz.half), F32),
        grad_hidden=((sz.block, sz.half), F32),
        grad_norm_gain=((1, sz.half), F32),
        grad_weight_z=matrix,
        grad_weight_x=matrix,
        grad_weight_dt=((sz.head_rows, sz.half), F32),
        grad_weight_bc=((sz.bc, sz.half), BF16),
        small_sums=((HALO + sz.plane_rows, sz.chan), F32),
        grad_out_weight=matrix,
    )
    scratch = scratch_list(sz)
    scratch["bc_full"] = ((sz.cols, sz.rows, sz.bc_part, sz.half), F32)
    names = [*inputs, *outputs, *scratch, "send_sem", "recv_sem"]
    count = semaphore_count(sz)
    vmem = pl.BlockSpec(memory_space=pltpu.VMEM)
    got = pl.pallas_call(
        functools.partial(block_kernel, sz, names),
        out_shape=[jax.ShapeDtypeStruct(*item) for item in outputs.values()],
        in_specs=[vmem] * len(inputs),
        out_specs=[vmem] * len(outputs),
        scratch_shapes=[pltpu.VMEM(*item) for item in scratch.values()]
        + [pltpu.SemaphoreType.DMA((count,)), pltpu.SemaphoreType.DMA((count,))],
        compiler_params=pltpu.CompilerParams(
            collective_id=0, has_side_effects=True, vmem_limit_bytes=62 << 20
        ),
        name="residual_block",
    )(*inputs.values())
    sent = dict(zip(outputs, got))
    results = dict(
        output=(sz.block, sz.half),
        grad_hidden=(sz.block, sz.half),
        grad_norm_gain=(1, sz.half),
        grad_weight_z=weight_z.shape,
        grad_weight_x=weight_x.shape,
        grad_weight_dt=weight_dt.shape[::-1],
        grad_weight_bc=weight_bc.shape,
        grad_conv_weight=conv_weight.shape,
        grad_conv_bias=(1, sz.chan),
        grad_bc_conv_weight=bc_conv_weight.shape,
        grad_bc_conv_bias=(1, sz.bc),
        grad_dt_bias=(1, sz.heads),
        grad_decay_log=(1, sz.heads),
        grad_skip_gain=(1, sz.heads),
        grad_gate_gain=(1, sz.chan),
        grad_out_weight=out_weight.shape,
    )
    got = pl.pallas_call(
        functools.partial(finish_kernel, sz, list(sent), list(results)),
        out_shape=[jax.ShapeDtypeStruct(shape, F32) for shape in results.values()],
        in_specs=[vmem] * len(sent),
        out_specs=[vmem] * len(results),
        compiler_params=pltpu.CompilerParams(vmem_limit_bytes=62 << 20),
        name="write_results",
    )(*sent.values())
    out = dict(zip(results, got))
    out["grad_weight_dt"] = out["grad_weight_dt"].T
    for name in ("norm_gain", "conv_bias", "bc_conv_bias", "dt_bias", "decay_log", "skip_gain", "gate_gain"):
        out["grad_" + name] = out["grad_" + name][0]
    return tuple(out.values())


def solution(mesh):
    in_specs = (
        P(("dp", "row"), None),
        P(("dp", "row"), "col"),
        P(),
        P("col", "row"),
        P("col", "row"),
        P("col", "row"),
        P("col", None),
        P(None, ("row", "col")),
        P(("row", "col")),
        P(),
        P(),
        P(("row", "col")),
        P(("row", "col")),
        P(("row", "col")),
        P(("row", "col")),
        P("row", "col"),
    )
    out_specs = (
        P(("dp", "row"), "col"),
        P(("dp", "row"), "col"),
        P("col"),
        P("col", "row"),
        P("col", "row"),
        P("col", "row"),
        P("col", None),
        P(None, ("row", "col")),
        P(("row", "col")),
        P(),
        P(),
        P(("row", "col")),
        P(("row", "col")),
        P(("row", "col")),
        P(("row", "col")),
        P("row", "col"),
    )
    sizes = tuple(mesh.shape[axis] for axis in ("dp", "row", "col"))
    return jax.shard_map(
        functools.partial(body, sizes), mesh=mesh, in_specs=in_specs, out_specs=out_specs, check_vma=False
    )
```

```python
import functools

import jax
import jax.numpy as jnp
from jax import lax
from jax.experimental import pallas as pl
from jax.experimental.pallas import tpu as pltpu
from jax.sharding import PartitionSpec as P

LANES = 128
HALO = 8
TILE = 16
EPSILON = 1e-05
PRECISE = lax.Precision.HIGHEST
F32 = jnp.float32
BF16 = jnp.bfloat16
MESH = pl.DeviceIdType.MESH


def dot_f32(a, b):
    return jnp.dot(a, b, precision=PRECISE, preferred_element_type=F32)


def dot_nn(a, b):
    return lax.dot_general(a, b, (((1,), (0,)), ((), ())), preferred_element_type=F32)


def dot_nt(a, b):
    return lax.dot_general(a, b, (((1,), (1,)), ((), ())), preferred_element_type=F32)


def dot_tn(a, b):
    return lax.dot_general(a, b, (((0,), (0,)), ((), ())), preferred_element_type=F32)


def sigmoid(v):
    return 1.0 / (1.0 + jnp.exp(-v))


def iota(shape, axis):
    return lax.broadcasted_iota(jnp.int32, shape, axis)


def head_spread(chan, head_width):
    head = iota((LANES, chan), 0)
    lane = iota((LANES, chan), 1)
    return ((lane >= head * head_width) & (lane < (head + 1) * head_width)).astype(F32)


class Sizes:
    def __init__(self, mesh_sizes, hidden, weight_z, weight_dt, weight_bc):
        self.n, self.rows, self.cols = mesh_sizes
        self.pair = 2 if self.rows % 2 == 0 else 1
        self.chips = self.rows // self.pair
        self.block, self.model = hidden.shape
        self.half = weight_z.shape[0]
        self.chan = weight_z.shape[1] // self.cols
        self.row_heads = weight_dt.shape[1]
        self.heads = self.row_heads // self.cols
        self.head_width = self.chan // self.heads
        self.bc = weight_bc.shape[1]
        self.state = self.bc // 2
        self.wide = self.chan + self.bc
        self.bc_part = self.bc // self.rows
        self.head_rows = -(-self.row_heads // TILE) * TILE
        assert self.n % 2 == 0
        self.pieces = next(k for k in (4, 2, 1) if self.chan % (k * TILE) == 0)
        self.piece = self.chan // self.pieces
        self.inner = self.chan * self.rows * self.cols
        self.sum_rows = -(-2 * self.rows // 8) * 8
        self.gain_rows = self.model // self.chan
        assert self.block <= self.chan and self.rows <= HALO
        self.dot_row = 5 * self.bc // self.chan + self.gain_rows
        self.plane_rows = -(-(self.dot_row + self.rows) // 8) * 8


class Links:
    def __init__(self, send_sem, recv_sem):
        self.send_sem, self.recv_sem = send_sem, recv_sem
        self.count = 0
        self.makers = []

    def take(self, many=1):
        first = self.count
        self.count += many
        return first

    def copy(self, src, dst, at, device):
        return pltpu.make_async_remote_copy(
            src_ref=src,
            dst_ref=dst,
            send_sem=self.send_sem.at[at],
            recv_sem=self.recv_sem.at[at],
            device_id=device,
            device_id_type=MESH,
        )

    def send(self, src, dst, at, device, when=None):
        make = lambda: self.copy(src, dst, at, device)
        self.makers.append((make, when))
        if when is None:
            make().start()
        else:
            pl.when(when)(lambda: make().start())

    def arrived(self, dst, at, device):
        self.copy(dst, dst, at, device).wait_recv()

    def drain(self):
        for make, when in self.makers:
            if when is None:
                make().wait_send()
            else:
                pl.when(when)(lambda: make().wait_send())


def semaphore_count(sz):
    group = sz.rows * sz.cols
    units = 3 * 2 * sz.pieces * (1 + sz.cols)
    front = sz.cols * (sz.n + 1) + 4 * group + 8 * (sz.chips + 1) * (sz.cols + 1) + 8 * sz.cols
    scatter = 3 * (2 * sz.chips * sz.cols + sz.chips + sz.cols)
    return units + front + scatter + 2 * group + 2 * sz.n + sz.rows + sz.cols + 16


def scratch_list(sz):
    nb, n, rows, cols, chips = sz.rows, sz.n, sz.rows, sz.cols, sz.chips
    blk, half, chan, wide = sz.block, sz.half, sz.chan, sz.wide
    across = max(chips - 1, 1)
    other = max(cols - 1, 1)
    shapes = dict(
        tokens=((rows, blk, sz.model), BF16),
        weights=((cols, half, chan + wide), BF16),
        wdt_in=((cols, sz.head_rows, half), BF16),
        wdt=((cols, LANES, half), BF16),
        cots=((rows, cols, blk, half), BF16),
        outw=((cols, chan, half), BF16),
        inv_rms=((blk, LANES), F32),
        conv=((HALO, wide), F32),
        head=((HALO, LANES), F32),
        ext=((nb, HALO + blk, wide), F32),
        z_raw=((nb, blk, chan), F32),
        pre=((nb, blk, wide), F32),
        gate=((nb, blk, wide), F32),
        step_pre=((nb, blk, LANES), F32),
        log_decay=((nb, blk, LANES), F32),
        step_ch=((nb, blk, chan), F32),
        log_ch=((nb, blk, chan), F32),
        decay=((nb, sz.heads, blk, blk), F32),
        states=((nb, sz.state, chan), F32),
        state=((sz.state, chan), F32),
        mixed=((nb, blk, chan), F32),
        inside=((nb, blk, chan), F32),
        ggo=((nb, blk, chan), F32),
        sums=((rows * cols, sz.sum_rows, blk), F32),
        total=((sz.sum_rows, blk), F32),
        gate_out=((nb, blk, chan), BF16),
        grad_z=((nb, blk, chan), BF16),
        grad_x=((nb, blk, chan), BF16),
        grad_bc=((nb, blk, sz.bc), BF16),
        grad_dt=((nb, blk, LANES), BF16),
        gate_gain=((HALO, chan), F32),
        conv_grad=((HALO, wide), F32),
        head_grad=((HALO, LANES), F32),
        skip_grad=((HALO, chan), F32),
        gain_grad=((HALO, sz.model), F32),
        grad_ext=((blk + HALO, wide), F32),
        grad_state=((sz.state, chan), F32),
        own=((3, sz.pieces, sz.piece, sz.model), BF16),
        landed=((3, sz.pieces, sz.piece, sz.model), BF16),
        across=((3, sz.pieces, sz.piece, sz.model), BF16),
        other_half=((3, sz.pieces, other, sz.piece, half), BF16),
        final=((3, sz.pieces, cols, sz.piece, half), BF16),
        keep=((chips, cols, blk, half), F32),
        keep_bc=((chips, cols, sz.bc_part, half), F32),
        dt_rows=((cols, sz.head_rows, half), F32),
        small=((sz.rows * sz.cols, sz.plane_rows, chan), F32),
        dp_small=((n, HALO + sz.plane_rows, chan), F32),
        dp_bc=((n, sz.bc_part + sz.head_rows, half), BF16),
        bc_all=((rows, sz.bc_part, half), BF16),
        dots=((cols, HALO, blk), F32),
        plane_dots=((HALO, blk), F32),
    )
    for name, part, extra in (("out", blk, 0), ("bc", sz.bc_part, sz.head_rows), ("in", blk, 0)):
        shapes[name + "_core"] = ((chips, cols, part, half), BF16)
        shapes[name + "_core_got"] = ((chips, cols, part, half), BF16)
        shapes[name + "_chip"] = ((across, cols, part, half), BF16)
        shapes[name + "_chip_got"] = ((across, cols, part, half), BF16)
        shapes[name + "_col"] = ((other, part + extra, half), BF16)
        shapes[name + "_col_got"] = ((other, part + extra, half), BF16)
    return shapes


class Scatter:
    def __init__(self, sz, links, where, bufs, name, keep):
        self.sz, self.links, self.where = sz, links, where
        self.bufs = {key: bufs[name + "_" + key] for key in ("core", "core_got", "chip", "chip_got", "col", "col_got")}
        self.keep = keep
        self.core_at = links.take(sz.chips)
        self.chip_at = links.take(sz.chips * sz.cols)
        self.col_at = links.take(sz.cols)

    def start(self, block_of):
        sz, (dp, row, col, chip, core) = self.sz, self.where
        if sz.pair == 2:
            for x in range(sz.chips):
                for h in range(sz.cols):
                    self.bufs["core"][x, h] = block_of(x * 2 + 1 - core, h).astype(BF16)
                self.links.send(
                    self.bufs["core"].at[x],
                    self.bufs["core_got"].at[x],
                    self.core_at + x,
                    (dp, chip * 2 + 1 - core, col),
                )
        for x in range(sz.chips):
            for h in range(sz.cols):
                self.keep[x, h] = block_of(x * sz.pair + core, h)

    def held(self, x, h):
        value = self.keep[x, h]
        if self.sz.pair == 2:
            value = value + self.bufs["core_got"][x, h].astype(F32)
        return value

    def across(self):
        sz, (dp, row, col, chip, core) = self.sz, self.where
        if sz.pair == 2:
            for x in range(sz.chips):
                self.links.arrived(self.bufs["core_got"].at[x], self.core_at + x, (dp, chip * 2 + 1 - core, col))
        for k in [*range(1, sz.cols), 0]:
            h = lax.rem(col + k, sz.cols)
            for dx in range(1, sz.chips):
                x = lax.rem(chip + dx, sz.chips)
                self.bufs["chip"][dx - 1, k] = self.held(x, h).astype(BF16)
                self.links.send(
                    self.bufs["chip"].at[dx - 1, k],
                    self.bufs["chip_got"].at[dx - 1, k],
                    self.chip_at + dx * sz.cols + k,
                    (dp, x * sz.pair + core, col),
                )

    def summed(self, k):
        sz, (dp, row, col, chip, core) = self.sz, self.where
        value = self.held(chip, lax.rem(col + k, sz.cols))
        for dx in range(1, sz.chips):
            x = lax.rem(chip + dx, sz.chips)
            self.links.arrived(
                self.bufs["chip_got"].at[dx - 1, k], self.chip_at + dx * sz.cols + k, (dp, x * sz.pair + core, col)
            )
            value = value + self.bufs["chip_got"][dx - 1, k].astype(F32)
        return value

    def turn(self, extra=None):
        sz, (dp, row, col, chip, core) = self.sz, self.where
        for k in range(1, sz.cols):
            h = lax.rem(col + k, sz.cols)
            value = self.summed(k)
            part = value.shape[0]
            self.bufs["col"][k - 1, 0:part, :] = value.astype(BF16)
            if extra is not None:
                more = extra(h)
                self.bufs["col"][k - 1, part : part + more.shape[0], :] = more.astype(BF16)
            self.links.send(
                self.bufs["col"].at[k - 1], self.bufs["col_got"].at[k - 1], self.col_at + k, (dp, row, h)
            )

    def finish(self, extra=None):
        sz, (dp, row, col, chip, core) = self.sz, self.where
        value = self.summed(0)
        more = None if extra is None else extra(col)
        part = value.shape[0]
        for k in range(1, sz.cols):
            h = lax.rem(col + k, sz.cols)
            self.links.arrived(self.bufs["col_got"].at[k - 1], self.col_at + k, (dp, row, h))
            value = value + self.bufs["col_got"][k - 1, 0:part, :].astype(F32)
            if more is not None:
                more = more + self.bufs["col_got"][k - 1, part:, :].astype(F32)
        return value, more


class Line:
    def __init__(self, sz, links, where, bufs, part):
        self.sz, self.links, self.where = sz, links, where
        self.own, self.landed, self.across = (bufs[key].at[part] for key in ("own", "landed", "across"))
        self.other_half, self.final = bufs["other_half"].at[part], bufs["final"].at[part]
        self.in_at, self.mid_at = links.take(sz.pieces), links.take(sz.pieces)
        self.col_at, self.out_at = links.take(sz.pieces * sz.cols), links.take(sz.pieces * sz.cols)
        dp, last = where[0], sz.n - 1
        low = dp < sz.n // 2
        self.middle = sz.n // 2 - 1
        self.place = jnp.where(low, dp, last - dp)
        self.inward = jnp.where(low, dp + 1, dp - 1)
        self.outward = jnp.clip(jnp.where(low, dp - 1, dp + 1), 0, last)

    def in_copy(self, g):
        target = (self.inward, *self.where[1:3])
        return self.links.copy(self.own.at[g], self.landed.at[g], self.in_at + g, target)

    def mid_copy(self, g):
        target = (self.inward, *self.where[1:3])
        return self.links.copy(self.own.at[g], self.across.at[g], self.mid_at + g, target)

    def half_copy(self, g, k, out):
        sz, (dp, row, col) = self.sz, self.where[:3]
        source = self.final.at[g, col] if k == 0 else self.other_half.at[g, k - 1]
        at = (self.out_at if out else self.col_at) + g * sz.cols + k
        target = (self.outward if out else dp, row, lax.rem(col + k, sz.cols))
        return self.links.copy(source, self.final.at[g, col], at, target)

    def pass_copy(self, g, k, device):
        sz, (dp, row, col) = self.sz, self.where[:3]
        ref = self.final.at[g, lax.rem(col + sz.cols - k, sz.cols)]
        return self.links.copy(ref, ref, self.out_at + g * sz.cols + k, (device, row, col))

    def source(self, g):
        if self.middle > 0:
            pl.when(self.place == 0)(lambda: self.in_copy(g).start())

    def fold(self, g):
        self.in_copy(g).wait_recv()
        self.own[g] = (self.own[g].astype(F32) + self.landed[g].astype(F32)).astype(BF16)

    def enter(self, g):
        if self.middle > 0:
            pl.when(self.place > 0)(lambda: self.fold(g))
        if self.middle > 1:
            pl.when((self.place > 0) & (self.place < self.middle))(lambda: self.in_copy(g).start())
        pl.when(self.place == self.middle)(lambda: self.mid_copy(g).start())

    def meet(self, g):
        sz, col = self.sz, self.where[2]
        self.mid_copy(g).wait()
        self.own[g] = (self.own[g].astype(F32) + self.across[g].astype(F32)).astype(BF16)
        for k in range(sz.cols):
            h = lax.rem(col + k, sz.cols)
            half = self.own[g, :, pl.ds(pl.multiple_of(h * sz.half, LANES), sz.half)]
            if k == 0:
                self.final[g, col] = half
            else:
                self.other_half[g, k - 1] = half
            if self.middle > 0:
                self.half_copy(g, k, True).start()
            if k > 0:
                self.half_copy(g, k, False).start()

    def cross(self, g):
        pl.when(self.place == self.middle)(lambda: self.meet(g))

    def from_columns(self, g):
        sz, (dp, row, col) = self.sz, self.where[:3]
        for k in range(1, sz.cols):
            h = lax.rem(col + sz.cols - k, sz.cols)
            self.links.arrived(self.final.at[g, h], self.col_at + g * sz.cols + k, (dp, row, h))

    def from_inward(self, g):
        for k in range(self.sz.cols):
            self.pass_copy(g, k, self.inward).wait_recv()

    def pass_on(self, g):
        for k in range(self.sz.cols):
            self.pass_copy(g, k, self.outward).start()

    def leave(self, g):
        pl.when(self.place == self.middle)(lambda: self.from_columns(g))
        if self.middle > 0:
            pl.when(self.place < self.middle)(lambda: self.from_inward(g))
        if self.middle > 1:
            pl.when((self.place > 0) & (self.place < self.middle))(lambda: self.pass_on(g))

    def sent_halves(self, g):
        for k in range(self.sz.cols):
            if self.middle > 0:
                self.half_copy(g, k, True).wait_send()
            if k > 0:
                self.half_copy(g, k, False).wait_send()

    def sent_on(self, g):
        for k in range(self.sz.cols):
            self.pass_copy(g, k, self.outward).wait_send()

    def drain(self):
        for g in range(self.sz.pieces):
            if self.middle > 0:
                pl.when(self.place < self.middle)(lambda: self.in_copy(g).wait_send())
            pl.when(self.place == self.middle)(lambda: self.sent_halves(g))
            if self.middle > 1:
                pl.when((self.place > 0) & (self.place < self.middle))(lambda: self.sent_on(g))


def forward_block(sz, m, b):
    blk, chan, wide, half = sz.block, sz.chan, sz.wide, sz.half
    acc = jnp.zeros((blk, chan + wide), F32)
    step_raw = jnp.zeros((blk, LANES), F32)
    for h in range(sz.cols):
        part = m.tokens[b, :, h * half : (h + 1) * half]
        acc = acc + dot_nn(part, m.weights[h])
        step_raw = step_raw + dot_nt(part, m.wdt[h])
    z_raw = acc[:, :chan]
    m.z_raw[b] = z_raw
    m.ext[b, HALO : HALO + blk, :] = acc[:, chan:]

    @pl.when(b + 1 < sz.rows)
    def _():
        m.ext[b + 1, 0:HALO, :] = m.ext[b, blk : blk + HALO, :]

    pre = m.conv[4:5, :]
    for tap in range(4):
        first = HALO - 3 + tap
        pre = pre + m.conv[tap : tap + 1, :] * m.ext[b, first : first + blk, :]
    gate = sigmoid(pre)
    m.pre[b] = pre
    m.gate[b] = gate
    conv = pre * gate
    step_pre = step_raw + m.head[0:1, :]
    m.step_pre[b] = step_pre
    step = jnp.maximum(step_pre, 0.0) + jnp.log1p(jnp.exp(-jnp.abs(step_pre)))
    rate = -jnp.exp(m.head[1:2, :])
    causal = iota((blk, blk), 0) >= iota((blk, blk), 1)
    log_decay = dot_f32(causal.astype(F32), step * rate)
    m.log_decay[b] = log_decay
    spread = head_spread(chan, sz.head_width)
    step_ch = dot_f32(step, spread)
    log_ch = dot_f32(log_decay, spread)
    m.step_ch[b] = step_ch
    m.log_ch[b] = log_ch
    skip_ch = dot_f32(jnp.broadcast_to(m.head[2:3, :], (HALO, LANES)), spread)[0:1, :]

    x_conv = conv[:, :chan]
    b_half = conv[:, chan : chan + sz.state].astype(BF16)
    c_half = conv[:, chan + sz.state :].astype(BF16)
    stepped = x_conv * step_ch
    scores = dot_nt(c_half, b_half)
    log_rows = log_decay.T
    lane = iota((blk, chan), 1)
    inside = jnp.zeros((blk, chan), F32)
    for head in range(sz.heads):
        gap = log_decay[:, head : head + 1] - log_rows[head : head + 1, :]
        decay = jnp.exp(jnp.where(causal, gap, -1e30))
        m.decay[b, head] = decay
        mixing = (scores * decay).astype(BF16)
        mine = (lane >= head * sz.head_width) & (lane < (head + 1) * sz.head_width)
        inside = inside + dot_nn(mixing, jnp.where(mine, stepped, 0.0).astype(BF16))
    entering = m.state[...]
    m.states[b] = entering
    outside = dot_nn(c_half, entering.astype(BF16)) * jnp.exp(log_ch)
    mixed = inside + outside + skip_ch * x_conv
    last = log_ch[blk - 1 : blk, :]
    tail = stepped * jnp.exp(last - log_ch)
    m.state[...] = entering * jnp.exp(last) + dot_tn(b_half, tail.astype(BF16))
    m.mixed[b] = mixed
    m.inside[b] = inside


def backward_block(sz, m, b, shift):
    blk, chan, wide = sz.block, sz.chan, sz.wide
    pre = m.pre[b]
    gate = m.gate[b]
    conv = pre * gate
    step_pre = m.step_pre[b]
    step = jnp.maximum(step_pre, 0.0) + jnp.log1p(jnp.exp(-jnp.abs(step_pre)))
    rate = -jnp.exp(m.head[1:2, :])
    step_ch = m.step_ch[b]
    log_ch = m.log_ch[b]
    spread = head_spread(chan, sz.head_width)
    skip_ch = dot_f32(jnp.broadcast_to(m.head[2:3, :], (HALO, LANES)), spread)[0:1, :]
    x_conv = conv[:, :chan]
    b_half = conv[:, chan : chan + sz.state].astype(BF16)
    c_half = conv[:, chan + sz.state :].astype(BF16)
    stepped = x_conv * step_ch
    stepped_half = stepped.astype(BF16)
    grad_mixed = m.ggo[b]
    grad_half = grad_mixed.astype(BF16)
    inside = m.inside[b]
    outside = m.mixed[b] - inside - skip_ch * x_conv

    scores = dot_nt(c_half, b_half)
    lane = iota((blk, chan), 1)
    grad_scores = jnp.zeros((blk, blk), F32)
    grad_inner = jnp.zeros((blk, chan), F32)
    for head in range(sz.heads):
        decay = m.decay[b, head]
        mixing = (scores * decay).astype(BF16)
        mine = (lane >= head * sz.head_width) & (lane < (head + 1) * sz.head_width)
        grad_mine = jnp.where(mine, grad_mixed, 0.0).astype(BF16)
        grad_scores = grad_scores + dot_nt(grad_mine, stepped_half) * decay
        grad_inner = grad_inner + dot_tn(mixing, grad_mine)
    scores_half = grad_scores.astype(BF16)

    entering = m.states[b]
    left = m.grad_state[...]
    left_half = left.astype(BF16)
    grad_outer = (grad_mixed * jnp.exp(log_ch)).astype(BF16)
    last = log_ch[blk - 1 : blk, :]
    fade = jnp.exp(last - log_ch)
    tail = stepped * fade
    grad_tail = dot_nn(b_half, left_half)
    tail_term = tail * grad_tail
    grad_c = dot_nt(grad_outer, entering.astype(BF16)) + dot_nn(scores_half, b_half)
    grad_b = dot_nt(tail.astype(BF16), left_half) + dot_tn(scores_half, c_half)
    grad_last = jnp.sum(tail_term, axis=0, keepdims=True) + jnp.exp(last) * jnp.sum(
        left * entering, axis=0, keepdims=True
    )
    m.grad_state[...] = left * jnp.exp(last) + dot_tn(c_half, grad_outer)

    grad_stepped = grad_inner + grad_tail * fade
    log_term = (
        grad_half.astype(F32) * inside
        + grad_mixed * outside
        - stepped_half.astype(F32) * grad_inner
        - tail_term
    )
    row = iota((blk, chan), 0)
    log_term = log_term + jnp.where(row == blk - 1, grad_last, 0.0)

    def per_head(values):
        return lax.dot_general(
            values, spread, (((1,), (1,)), ((), ())), precision=PRECISE, preferred_element_type=F32
        )

    later = (iota((blk, blk), 0) <= iota((blk, blk), 1)).astype(F32)
    grad_rate_step = dot_f32(later, per_head(log_term))
    grad_step = per_head(grad_stepped * x_conv) + grad_rate_step * rate
    grad_step_raw = grad_step * sigmoid(step_pre)
    m.head_grad[0:1, :] += jnp.sum(grad_step_raw, axis=0, keepdims=True)
    m.head_grad[1:2, :] += jnp.sum(grad_rate_step * step, axis=0, keepdims=True) * rate
    m.skip_grad[0:1, :] += jnp.sum(grad_mixed * x_conv, axis=0, keepdims=True)

    grad_x = grad_stepped * step_ch + grad_mixed * skip_ch
    slope = gate * (1.0 + pre * (1.0 - gate))
    m.grad_ext[blk : blk + HALO, :] = m.grad_ext[0:HALO, :]
    m.grad_ext[0:blk, 0:chan] = grad_x * slope[:, :chan]
    m.grad_ext[0:blk, chan : chan + sz.state] = grad_b * slope[:, chan : chan + sz.state]
    m.grad_ext[0:blk, chan + sz.state :] = grad_c * slope[:, chan + sz.state :]
    grad_pre = m.grad_ext[0:blk, :]
    grad_raw = jnp.zeros((blk, wide), F32)
    for tap in range(4):
        grad_raw = grad_raw + m.conv[tap : tap + 1, :] * m.grad_ext[3 - tap : 3 - tap + blk, :]
        first = HALO - 3 + tap
        m.conv_grad[tap : tap + 1, :] += jnp.sum(
            grad_pre * m.ext[b, first : first + blk, :], axis=0, keepdims=True
        )
    m.conv_grad[4:5, :] += jnp.sum(grad_pre, axis=0, keepdims=True)
    m.grad_x[b] = grad_raw[:, :chan].astype(BF16)
    m.grad_bc[b] = grad_raw[:, chan:].astype(BF16)
    m.grad_dt[b] = dot_nn(grad_step_raw.astype(BF16), shift).astype(BF16)


class Refs:
    pass


def block_kernel(sz, names, *refs):
    m = Refs()
    for name, ref in zip(names, refs):
        setattr(m, name, ref)
    bufs = m.__dict__
    nb, rows, cols, chips, pair = sz.rows, sz.rows, sz.cols, sz.chips, sz.pair
    blk, half, chan, wide, n = sz.block, sz.half, sz.chan, sz.wide, sz.n
    dp, row, col = lax.axis_index("dp"), lax.axis_index("row"), lax.axis_index("col")
    chip, core = row // pair, lax.rem(row, pair)
    where = (dp, row, col, chip, core)
    group = rows * cols
    mine = row * cols + col
    sibling = (dp, chip * pair + lax.rem(core + 1, pair), col)
    sibling_core = lax.rem(core + 1, pair)

    def plane_peer(k):
        return dp, lax.rem(row + k // cols, rows), lax.rem(col + k % cols, cols)

    def line_peer(k):
        return lax.rem(dp + k, n), row, col

    def col_peer(k):
        return dp, row, lax.rem(col + k, cols)

    def chip_peer(dx):
        return dp, lax.rem(chip + dx, chips) * pair + core, col

    def from_chip(dx):
        return lax.rem(chip + chips - dx, chips) * pair + core

    def from_sibling(dx):
        return lax.rem(chip + chips - dx, chips) * pair + sibling_core

    def from_col(k):
        return lax.rem(col + cols - k, cols)

    links = Links(m.send_sem, m.recv_sem)
    barrier = pltpu.get_barrier_semaphore()
    peers = [plane_peer(k) for k in range(1, group)] + [line_peer(k) for k in range(1, n)]
    for peer in peers:
        pl.semaphore_signal(barrier, inc=1, device_id=peer, device_id_type=MESH)

    def lanes(start, size):
        return pl.ds(pl.multiple_of(start * size, LANES), size)

    hidden = m.hidden[...]
    inv_rms = lax.rsqrt(jnp.mean(hidden * hidden, axis=1, keepdims=True) + EPSILON)
    m.inv_rms[...] = jnp.broadcast_to(inv_rms, (blk, LANES))
    m.tokens[row] = (hidden * inv_rms * m.norm_gain[...]).astype(BF16)
    m.cots[row, col] = m.cotangent[...].astype(BF16)
    steps_in = m.weight_dt[...].astype(F32)
    if sz.head_rows > sz.row_heads:
        steps_in = jnp.concatenate([steps_in, jnp.zeros((sz.head_rows - sz.row_heads, half), F32)], axis=0)
    m.wdt_in[col] = steps_in.astype(BF16)

    pl.semaphore_wait(barrier, len(peers))

    w_at, bc_at, dt_at, bc_fwd = links.take(2 * cols), links.take(cols), links.take(cols), links.take(cols)
    tok_x, tok_s = links.take(chips), links.take(chips)
    cot_y, cot_x, cot_s = links.take(cols), links.take(chips * cols), links.take(chips * cols)
    out_at = links.take(cols)
    bc_rows = half // pair
    bc_mine = pl.ds(pl.multiple_of(core * bc_rows, TILE), bc_rows)
    bc_sib = pl.ds(pl.multiple_of(sibling_core * bc_rows, TILE), bc_rows)
    bc_lanes = pl.ds(2 * chan, sz.bc)
    x_lanes = pl.ds(chan, chan)
    spread_x = n if half % (n * TILE) == 0 else 1
    x_slice = half // spread_x
    x_at = links.take(cols * n)

    def x_rows(k):
        owner = lax.rem(dp + n - k, n) if spread_x > 1 else 0
        return pl.ds(pl.multiple_of(owner * x_slice, TILE), x_slice)

    for k in range(1, cols):
        peer = col_peer(k)
        links.send(
            m.weight_x.at[x_rows(0), lanes(peer[2], chan)], m.weights.at[col, x_rows(0), x_lanes], w_at + 2 * k + 1, peer
        )
        links.send(
            m.weight_z.at[:, lanes(peer[2], chan)], m.weights.at[col, :, pl.ds(0, chan)], w_at + 2 * k, peer
        )
        links.send(m.weight_bc.at[bc_mine, :], m.weights.at[col, bc_mine, bc_lanes], bc_at + k, peer)
        links.send(m.wdt_in.at[col], m.wdt_in.at[col], dt_at + k, peer)
    for dx in range(1, chips):
        links.send(m.tokens.at[row], m.tokens.at[row], tok_x + dx, chip_peer(dx))
    if pair == 2:
        links.send(m.tokens.at[row], m.tokens.at[row], tok_s, sibling)

    m.weights[col, :, 0:chan] = m.weight_z[:, lanes(col, chan)]
    m.weights[col, :, chan : 2 * chan] = m.weight_x[:, lanes(col, chan)]
    m.weights[col, :, 2 * chan :] = m.weight_bc[...]
    m.outw[col] = m.out_weight[pl.ds(pl.multiple_of(col * chan, TILE), chan), :]
    for ref in (m.conv, m.head, m.state, m.grad_state, m.grad_ext, m.gate_gain, m.conv_grad, m.head_grad):
        ref[...] = jnp.zeros_like(ref)
    for ref in (m.skip_grad, m.gain_grad):
        ref[...] = jnp.zeros_like(ref)
    m.ext[0, 0:HALO, :] = jnp.zeros((HALO, wide), F32)
    m.conv[0:4, 0:chan] = m.conv_weight[...]
    m.conv[0:4, chan:] = m.bc_conv_weight[...]
    m.conv[4:5, 0:chan] = m.conv_bias[...]
    m.conv[4:5, chan:] = m.bc_conv_bias[...]
    m.head[0:1, 0 : sz.heads] = m.dt_bias[...]
    m.head[1:2, 0 : sz.heads] = m.decay_log[...]
    m.head[2:3, 0 : sz.heads] = m.skip_gain[...]

    def send_cots(dx, k, r, c):
        if dx == 0:
            for far in range(1, chips):
                links.send(m.cots.at[r, c], m.cots.at[r, c], cot_x + far * cols + k, chip_peer(far))
        if pair == 2:
            links.send(m.cots.at[r, c], m.cots.at[r, c], cot_s + dx * cols + k, sibling)

    for k in range(1, cols):
        part = m.weights.at[from_col(k), x_rows(0), x_lanes]
        links.arrived(part, w_at + 2 * k + 1, col_peer(k))
        for j in range(1, spread_x):
            links.send(part, part, x_at + k * n + j, line_peer(j))
    for dx in range(1, chips):
        links.arrived(m.tokens.at[from_chip(dx)], tok_x + dx, chip_peer(dx))
        if pair == 2:
            links.send(m.tokens.at[from_chip(dx)], m.tokens.at[from_chip(dx)], tok_s + dx, sibling)
    send_cots(0, 0, row, col)
    for k in range(1, cols):
        peer, src = col_peer(k), from_col(k)
        links.arrived(m.weights.at[src, :, pl.ds(0, chan)], w_at + 2 * k, peer)
        links.arrived(m.weights.at[src, bc_mine, bc_lanes], bc_at + k, peer)
        if pair == 2:
            links.send(
                m.weights.at[src, bc_mine, bc_lanes], m.weights.at[src, bc_mine, bc_lanes], bc_fwd + k, sibling
            )
        links.arrived(m.wdt_in.at[src], dt_at + k, peer)
        links.send(m.cots.at[row, col], m.cots.at[row, col], cot_y + k, peer)

    head_at, head_to = iota((LANES, LANES), 0), iota((LANES, LANES), 1)
    shift = ((head_to == head_at + col * sz.heads) & (head_at < sz.heads)).astype(BF16)
    for h in range(cols):
        padded = jnp.concatenate([m.wdt_in[h], jnp.zeros((LANES - sz.head_rows, half), BF16)], axis=0)
        m.wdt[h] = dot_nn(shift, padded).astype(BF16)

    for k in range(1, cols):
        for j in range(1, spread_x):
            links.arrived(m.weights.at[from_col(k), x_rows(j), x_lanes], x_at + k * n + j, line_peer(j))
    if pair == 2:
        for dx in range(chips):
            links.arrived(m.tokens.at[from_sibling(dx)], tok_s + dx, sibling)
        for k in range(1, cols):
            links.arrived(m.weights.at[from_col(k), bc_sib, bc_lanes], bc_fwd + k, sibling)

    def pass_col_cots():
        for k in range(1, cols):
            links.arrived(m.cots.at[row, from_col(k)], cot_y + k, col_peer(k))

    def pass_chip_cots(k):
        for dx in range(1, chips):
            r, c = from_chip(dx), from_col(k)
            links.arrived(m.cots.at[r, c], cot_x + dx * cols + k, chip_peer(dx))

    def forward_step(b, carry):
        forward_block(sz, m, b)
        return carry

    early = min(2, nb)
    lax.fori_loop(0, early, forward_step, 0)
    pass_col_cots()
    for k in range(1, cols):
        send_cots(0, k, row, from_col(k))
        peer = col_peer(k)
        links.send(
            m.out_weight.at[pl.ds(pl.multiple_of(peer[2] * chan, TILE), chan), :], m.outw.at[col], out_at + k, peer
        )
    pass_chip_cots(0)
    for dx in range(1, chips):
        send_cots(dx, 0, from_chip(dx), col)
    lax.fori_loop(early, nb, forward_step, 0)
    for k in range(1, cols):
        pass_chip_cots(k)
        for dx in range(1, chips):
            send_cots(dx, k, from_chip(dx), from_col(k))
    for k in range(1, cols):
        links.arrived(m.outw.at[from_col(k)], out_at + k, col_peer(k))
    if pair == 2:
        for dx in range(chips):
            for k in range(cols):
                links.arrived(m.cots.at[from_sibling(dx), from_col(k)], cot_s + dx * cols + k, sibling)

    sub = iota((LANES, blk), 0)
    m.sums[mine] = jnp.zeros((sz.sum_rows, blk), F32)

    def sum_step(b, carry):
        ggo = jnp.zeros((blk, chan), F32)
        for h in range(cols):
            ggo = ggo + dot_nt(m.cots[b, h], m.outw[h])
        m.ggo[b] = ggo
        z_raw = m.z_raw[b]
        gated = m.mixed[b] * (z_raw * sigmoid(z_raw))
        squares = jnp.sum(gated * gated, axis=1, keepdims=True)
        inner = jnp.sum(ggo * m.gate_gain_in[...] * gated, axis=1, keepdims=True)
        lane = iota((blk, LANES), 1)
        both = jnp.where(lane == 0, squares, jnp.where(lane == 1, inner, 0.0)).T
        m.sums[mine, pl.ds(b, 1), :] = both[0:1, :]
        m.sums[mine, pl.ds(nb + b, 1), :] = both[1:2, :]
        return carry

    lax.fori_loop(0, nb, sum_step, 0)

    def to_plane(ref):
        at = links.take(group)
        for k in range(1, group):
            links.send(ref.at[mine], ref.at[mine], at + k, plane_peer(k))
        return at

    def from_plane(ref, at):
        for k in range(1, group):
            r, c = lax.rem(row + rows - k // cols, rows), lax.rem(col + cols - k % cols, cols)
            links.arrived(ref.at[r * cols + c], at + k, plane_peer(k))
        value = ref[0]
        for k in range(1, group):
            value = value + ref[k]
        return value

    m.total[...] = from_plane(m.sums, to_plane(m.sums))

    def gate_step(b, carry):
        first = m.total[pl.ds(b, 1), :]
        second = m.total[pl.ds(nb + b, 1), :]
        both = jnp.where(sub == 0, first, jnp.where(sub == 1, second, 0.0)).T
        inv_gate = lax.rsqrt(both[:, 0:1] / sz.inner + EPSILON)
        gate_dot = both[:, 1:2] * inv_gate
        ggo = m.ggo[b]
        gate_gain = m.gate_gain_in[...]
        z_raw = m.z_raw[b]
        z_gate = sigmoid(z_raw)
        mixed = m.mixed[b]
        gate_hat = mixed * (z_raw * z_gate) * inv_gate
        grad_gated = inv_gate * (ggo * gate_gain - gate_hat * (gate_dot / sz.inner))
        m.grad_z[b] = (grad_gated * mixed * (z_gate * (1.0 + z_raw * (1.0 - z_gate)))).astype(BF16)
        m.gate_out[b] = (gate_hat * gate_gain).astype(BF16)
        m.gate_gain[0:1, :] += jnp.sum(ggo * gate_hat, axis=0, keepdims=True)
        m.ggo[b] = grad_gated * (z_raw * z_gate)
        return carry

    lax.fori_loop(0, nb, gate_step, 0)

    def flat(ref):
        value = ref[...]
        return value.reshape(value.shape[0] * value.shape[1], value.shape[2])

    lines = [Line(sz, links, where, bufs, part) for part in range(3)]
    order = [(line, g) for line in lines for g in range(sz.pieces)]

    def stage(i):
        for back, name in ((0, "enter"), (2, "cross"), (4, "leave")):
            if 0 <= i - back < len(order):
                line, g = order[i - back]
                getattr(line, name)(g)

    stages = [functools.partial(stage, i) for i in range(len(order) + 4)]

    def advance(many=1, keep=0):
        for _ in range(many):
            if len(stages) > keep:
                stages.pop(0)()

    def sources(part, first, last):
        for g in range(sz.pieces):
            if first <= g * 4 // sz.pieces < last:
                lines[part].source(g)

    def collect(part, ref):
        for c in range(cols):
            for i in range(sz.pieces):
                at = c * chan + i * sz.piece
                ref[at : at + sz.piece, :] = m.final[part, i, c]

    def weight_part(part, grads, operand_of):
        for h in range(cols):
            value = dot_tn(grads, operand_of(h)).astype(BF16)
            m.own[part, :, :, h * half : (h + 1) * half] = value.reshape(sz.pieces, sz.piece, half)

    def cots_of(h):
        return m.cots[:, h].reshape(rows * blk, half)

    def tokens_of(h):
        return m.tokens[:, :, h * half : (h + 1) * half].reshape(rows * blk, half)

    weight_part(0, flat(m.gate_out), cots_of)
    sources(0, 0, 2)
    weight_part(1, flat(m.grad_z), tokens_of)
    sources(0, 2, 4)
    out_sum = Scatter(sz, links, where, bufs, "out", m.keep)
    out_sum.start(lambda r, h: dot_nn(m.gate_out[r], m.outw[h]))
    sources(1, 0, 2)

    def backward_step(i, carry):
        backward_block(sz, m, nb - 1 - i, shift)
        return carry

    before_x = sz.pieces + 4
    services = [
        [lambda: advance(1, before_x), lambda: sources(1, 2, 4), out_sum.across],
        [lambda: advance(1, before_x)],
        [lambda: advance(1, before_x)],
        [],
    ]
    done = 0
    for i, service in enumerate(services):
        until = nb if i == len(services) - 1 else min(nb, done + max(nb // 4, 1))
        lax.fori_loop(done, until, backward_step, 0)
        done = until
        for step in service:
            step()

    weight_part(2, flat(m.grad_x), tokens_of)
    sources(2, 0, 4)
    advance()
    out_sum.turn()
    dt_grads = flat(m.grad_dt)
    for h in range(cols):
        part = dot_tn(flat(m.grad_bc), tokens_of(h))
        m.bc_full[h] = part.reshape(rows, sz.bc_part, half)
        m.dt_rows[h] = dot_tn(dt_grads, tokens_of(h))[0 : sz.head_rows, :]
    bc_sum = Scatter(sz, links, where, bufs, "bc", m.keep_bc)
    bc_sum.start(lambda r, h: m.bc_full[h, r])
    advance()
    total, _ = out_sum.finish()
    m.output[...] = m.hidden[:, lanes(col, half)] + total

    def grad_block(r, h):
        w = m.weights.at[h]
        value = dot_nt(m.grad_z[r], w[:, 0:chan])
        value = value + dot_nt(m.grad_x[r], w[:, chan : 2 * chan])
        value = value + dot_nt(m.grad_bc[r], w[:, 2 * chan :])
        padded = jnp.concatenate([m.wdt_in[h], jnp.zeros((LANES - sz.head_rows, half), BF16)], axis=0)
        value = value + dot_nn(m.grad_dt[r], padded)
        at = slice(h * half, (h + 1) * half)
        product = value * m.tokens[r, :, at].astype(F32)
        m.gain_grad[0:1, at] += jnp.sum(product, axis=0, keepdims=True)
        dot = jnp.sum(product, axis=1, keepdims=True)
        m.dots[h, pl.ds(r, 1), :] = jnp.where(iota((blk, LANES), 1) == 0, dot, 0.0).T[0:1, :]
        return value

    in_sum = Scatter(sz, links, where, bufs, "in", m.keep)
    bc_sum.across()
    advance()
    in_sum.start(grad_block)
    advance()

    m.small[mine] = jnp.zeros((sz.plane_rows, chan), F32)
    per_row = sz.bc // chan
    for j in range(5):
        for p in range(per_row):
            at = chan + p * chan
            m.small[mine, j * per_row + p : j * per_row + p + 1, :] = m.conv_grad[j : j + 1, at : at + chan]
    for j in range(sz.gain_rows):
        at = 5 * per_row + j
        m.small[mine, at : at + 1, :] = m.gain_grad[0:1, j * chan : (j + 1) * chan]
    dot_rows = m.dots[0, 0:rows, :]
    for h in range(1, cols):
        dot_rows = dot_rows + m.dots[h, 0:rows, :]
    m.small[mine, sz.dot_row : sz.dot_row + rows, 0:blk] = dot_rows
    small_at = to_plane(m.small)
    in_sum.across()
    advance()
    dt_of = lambda h: m.dt_rows[h]
    bc_sum.turn(dt_of)
    advance()
    spread = head_spread(chan, sz.head_width)
    skip_heads = lax.dot_general(
        m.skip_grad[...], spread, (((1,), (1,)), ((), ())), precision=PRECISE, preferred_element_type=F32
    )
    m.dp_small[dp] = jnp.zeros((HALO + sz.plane_rows, chan), F32)
    m.dp_small[dp, 0:5, :] = m.conv_grad[0:5, 0:chan]
    m.dp_small[dp, 5:6, :] = m.gate_gain[0:1, :]
    m.dp_small[dp, 6:7, 0:LANES] = m.head_grad[0:1, :]
    m.dp_small[dp, 6:7, LANES : 2 * LANES] = m.head_grad[1:2, :]
    m.dp_small[dp, 7:8, 0:LANES] = skip_heads[0:1, :]
    plane_sums = from_plane(m.small, small_at)
    m.dp_small[dp, HALO:, :] = plane_sums
    m.plane_dots[0:rows, :] = plane_sums[sz.dot_row : sz.dot_row + rows, 0:blk]

    def to_line(ref):
        at = links.take(n)
        for k in range(1, n):
            links.send(ref.at[dp], ref.at[dp], at + k, line_peer(k))
        return at

    def from_line(ref, at):
        for k in range(1, n):
            links.arrived(ref.at[lax.rem(dp + n - k, n)], at + k, line_peer(k))
        value = ref[0].astype(F32)
        for k in range(1, n):
            value = value + ref[k].astype(F32)
        return value

    small_line = to_line(m.dp_small)
    bc_value, dt_value = bc_sum.finish(dt_of)
    m.dp_bc[dp, 0 : sz.bc_part, :] = bc_value.astype(BF16)
    m.dp_bc[dp, sz.bc_part :, :] = dt_value.astype(BF16)
    bc_line = to_line(m.dp_bc)
    advance()
    in_sum.turn()
    advance()

    bc_total = from_line(m.dp_bc, bc_line)
    m.grad_weight_dt[...] = bc_total[sz.bc_part :, :]
    m.bc_all[row] = bc_total[0 : sz.bc_part, :].astype(BF16)
    row_at = links.take(rows)
    for k in range(1, rows):
        links.send(m.bc_all.at[row], m.bc_all.at[row], row_at + k, (dp, lax.rem(row + k, rows), col))

    grad_scaled, _ = in_sum.finish()
    inv_wide = m.inv_rms[:, 0:1]
    normed = m.hidden[:, lanes(col, half)] * inv_wide
    grad_in = grad_scaled * m.norm_gain[:, lanes(col, half)]
    full = jnp.where(sub == 0, m.plane_dots[pl.ds(row, 1), :], 0.0).T
    m.grad_hidden[...] = m.cotangent[...] + inv_wide * (grad_in - normed * (full[:, 0:1] / sz.model))
    advance()
    advance(1, 3)
    collect(0, m.grad_out_weight)
    collect(1, m.grad_weight_z)
    summed = from_line(m.dp_small, small_line)
    m.small_sums[...] = summed
    per_half = half // chan
    for j in range(per_half):
        at = HALO + 5 * per_row
        line = jnp.zeros((1, chan), F32)
        for c in range(cols):
            here = summed[at + c * per_half + j : at + c * per_half + j + 1, :]
            line = jnp.where(col == c, here, line)
        gain = m.norm_gain[:, pl.ds(pl.multiple_of(col * half + j * chan, LANES), chan)]
        m.grad_norm_gain[:, j * chan : (j + 1) * chan] = line / gain

    for k in range(1, rows):
        at = lax.rem(row + rows - k, rows)
        links.arrived(m.bc_all.at[at], row_at + k, (dp, lax.rem(row + k, rows), col))
    m.grad_weight_bc[...] = flat(m.bc_all)
    advance(len(stages))
    collect(2, m.grad_weight_x)
    links.drain()
    for line in lines:
        line.drain()


def finish_kernel(sz, sent, results, *refs):
    i, o = Refs(), Refs()
    for name, ref in zip(sent, refs):
        setattr(i, name, ref)
    for name, ref in zip(results, refs[len(sent) :]):
        setattr(o, name, ref)
    chan = sz.chan
    per_row = sz.bc // chan
    for name in ("output", "grad_hidden"):
        getattr(o, name)[...] = getattr(i, name)[...]
    o.grad_out_weight[...] = i.grad_out_weight[...].astype(F32)
    for name in ("grad_weight_z", "grad_weight_x", "grad_weight_bc"):
        getattr(o, name)[...] = getattr(i, name)[...].astype(F32).T

    o.grad_norm_gain[...] = i.grad_norm_gain[...]
    o.grad_weight_dt[...] = i.grad_weight_dt[0 : sz.row_heads, :]
    o.grad_conv_weight[...] = i.small_sums[0:4, :]
    o.grad_conv_bias[...] = i.small_sums[4:5, :]
    o.grad_gate_gain[...] = i.small_sums[5:6, :]
    o.grad_dt_bias[...] = i.small_sums[6:7, 0 : sz.heads]
    o.grad_decay_log[...] = i.small_sums[6:7, LANES : LANES + sz.heads]
    o.grad_skip_gain[...] = i.small_sums[7:8, 0 : sz.heads]
    for j in range(5):
        for p in range(per_row):
            at = HALO + j * per_row + p
            lanes = slice(p * chan, (p + 1) * chan)
            if j < 4:
                o.grad_bc_conv_weight[j : j + 1, lanes] = i.small_sums[at : at + 1, :]
            else:
                o.grad_bc_conv_bias[:, lanes] = i.small_sums[at : at + 1, :]


def body(
    mesh_sizes,
    hidden,
    cotangent,
    norm_gain,
    weight_z,
    weight_x,
    weight_dt,
    weight_bc,
    conv_weight,
    conv_bias,
    bc_conv_weight,
    bc_conv_bias,
    dt_bias,
    decay_log,
    skip_gain,
    gate_gain,
    out_weight,
):
    sz = Sizes(mesh_sizes, hidden, weight_z, weight_dt, weight_bc)
    line = lambda vector: vector[None, :]
    inputs = dict(
        hidden=hidden,
        cotangent=cotangent,
        norm_gain=line(norm_gain),
        weight_z=weight_z,
        weight_x=weight_x,
        weight_dt=weight_dt.T,
        weight_bc=weight_bc,
        conv_weight=conv_weight,
        conv_bias=line(conv_bias),
        bc_conv_weight=bc_conv_weight,
        bc_conv_bias=line(bc_conv_bias),
        dt_bias=line(dt_bias),
        decay_log=line(decay_log),
        skip_gain=line(skip_gain),
        gate_gain_in=line(gate_gain),
        out_weight=out_weight,
    )
    matrix = ((sz.cols * sz.chan, sz.half), BF16)
    outputs = dict(
        output=((sz.block, sz.half), F32),
        grad_hidden=((sz.block, sz.half), F32),
        grad_norm_gain=((1, sz.half), F32),
        grad_weight_z=matrix,
        grad_weight_x=matrix,
        grad_weight_dt=((sz.head_rows, sz.half), F32),
        grad_weight_bc=((sz.bc, sz.half), BF16),
        small_sums=((HALO + sz.plane_rows, sz.chan), F32),
        grad_out_weight=matrix,
    )
    scratch = scratch_list(sz)
    scratch["bc_full"] = ((sz.cols, sz.rows, sz.bc_part, sz.half), F32)
    names = [*inputs, *outputs, *scratch, "send_sem", "recv_sem"]
    count = semaphore_count(sz)
    vmem = pl.BlockSpec(memory_space=pltpu.VMEM)
    got = pl.pallas_call(
        functools.partial(block_kernel, sz, names),
        out_shape=[jax.ShapeDtypeStruct(*item) for item in outputs.values()],
        in_specs=[vmem] * len(inputs),
        out_specs=[vmem] * len(outputs),
        scratch_shapes=[pltpu.VMEM(*item) for item in scratch.values()]
        + [pltpu.SemaphoreType.DMA((count,)), pltpu.SemaphoreType.DMA((count,))],
        compiler_params=pltpu.CompilerParams(
            collective_id=0, has_side_effects=True, vmem_limit_bytes=62 << 20
        ),
        name="residual_block",
    )(*inputs.values())
    sent = dict(zip(outputs, got))
    results = dict(
        output=(sz.block, sz.half),
        grad_hidden=(sz.block, sz.half),
        grad_norm_gain=(1, sz.half),
        grad_weight_z=weight_z.shape,
        grad_weight_x=weight_x.shape,
        grad_weight_dt=weight_dt.shape[::-1],
        grad_weight_bc=weight_bc.shape,
        grad_conv_weight=conv_weight.shape,
        grad_conv_bias=(1, sz.chan),
        grad_bc_conv_weight=bc_conv_weight.shape,
        grad_bc_conv_bias=(1, sz.bc),
        grad_dt_bias=(1, sz.heads),
        grad_decay_log=(1, sz.heads),
        grad_skip_gain=(1, sz.heads),
        grad_gate_gain=(1, sz.chan),
        grad_out_weight=out_weight.shape,
    )
    got = pl.pallas_call(
        functools.partial(finish_kernel, sz, list(sent), list(results)),
        out_shape=[jax.ShapeDtypeStruct(shape, F32) for shape in results.values()],
        in_specs=[vmem] * len(sent),
        out_specs=[vmem] * len(results),
        compiler_params=pltpu.CompilerParams(vmem_limit_bytes=62 << 20),
        name="write_results",
    )(*sent.values())
    out = dict(zip(results, got))
    out["grad_weight_dt"] = out["grad_weight_dt"].T
    for name in ("norm_gain", "conv_bias", "bc_conv_bias", "dt_bias", "decay_log", "skip_gain", "gate_gain"):
        out["grad_" + name] = out["grad_" + name][0]
    return tuple(out.values())


def solution(mesh):
    in_specs = (
        P(("dp", "row"), None),
        P(("dp", "row"), "col"),
        P(),
        P("col", "row"),
        P("col", "row"),
        P("col", "row"),
        P("col", None),
        P(None, ("row", "col")),
        P(("row", "col")),
        P(),
        P(),
        P(("row", "col")),
        P(("row", "col")),
        P(("row", "col")),
        P(("row", "col")),
        P("row", "col"),
    )
    out_specs = (
        P(("dp", "row"), "col"),
        P(("dp", "row"), "col"),
        P("col"),
        P("col", "row"),
        P("col", "row"),
        P("col", "row"),
        P("col", None),
        P(None, ("row", "col")),
        P(("row", "col")),
        P(),
        P(),
        P(("row", "col")),
        P(("row", "col")),
        P(("row", "col")),
        P(("row", "col")),
        P("row", "col"),
    )
    sizes = tuple(mesh.shape[axis] for axis in ("dp", "row", "col"))
    return jax.shard_map(
        functools.partial(body, sizes), mesh=mesh, in_specs=in_specs, out_specs=out_specs, check_vma=False
    )
```
